32 devices in a mesh: ctx: 4 (over y, x), fsdp: 8 (over z, core).
Axes of the slice: x: 2, y: 2, z: 4, core: 2. Of those that a mesh axis runs over, the one named last changes fastest.
Arguments:
- tokens: bfloat16 [8, 2048, 576], P('fsdp', 'ctx'), may hold values from -6 to 6
- positions: int32 [8, 2048], P('fsdp', 'ctx'), may hold values from 0 to 2047, as said below
- query_weight: bfloat16 [2, 576, 576], P(None, 'fsdp'), may hold values from -0.25 to 0.25
- key_matrix: bfloat16 [2, 576, 192], P(None, 'fsdp'), may hold values from -0.25 to 0.25
- value_weight: bfloat16 [2, 576, 192], P(None, 'fsdp'), may hold values from -0.25 to 0.25
- out_weight: bfloat16 [2, 576, 576], P(None, 'fsdp'), may hold values from -1 to 1
- gate_weight: bfloat16 [2, 576, 1536], P(None, 'fsdp'), may hold values from -0.25 to 0.25
- up_weight: bfloat16 [2, 576, 1536], P(None, 'fsdp'), may hold values from -0.25 to 0.25
- down_weight: bfloat16 [2, 1536, 576], P(None, 'fsdp'), may hold values from -0.15625 to 0.15625
- attn_gain: bfloat16 [2, 576], P(None, 'fsdp'), may hold values from 0.5 to 1.5
- mlp_gain: bfloat16 [2, 576], P(None, 'fsdp'), may hold values from 0.5 to 1.5
- cotangent: bfloat16 [8, 2048, 576], P('fsdp', 'ctx'), may hold values from -6 to 6
Outputs:
- layer_out: bfloat16 [8, 2048, 576], P('fsdp', 'ctx')
- input_grad: float32 [8, 2048, 576], P('fsdp', 'ctx')
- grad_query: float32 [2, 576, 576], P(None, 'fsdp')
- grad_key: float32 [2, 576, 192], P(None, 'fsdp')
- grad_value: float32 [2, 576, 192], P(None, 'fsdp')
- grad_out: float32 [2, 576, 576], P(None, 'fsdp')
- grad_gate: float32 [2, 576, 1536], P(None, 'fsdp')
- grad_up: float32 [2, 576, 1536], P(None, 'fsdp')
- grad_down: float32 [2, 1536, 576], P(None, 'fsdp')
- grad_attn_gain: float32 [2, 576], P(None, 'fsdp')
- grad_mlp_gain: float32 [2, 576], P(None, 'fsdp')
The draws below stay inside these ranges and needn't reach their ends.
Inputs may be any that keep to these rules, and one draw needn't show every extreme that they name: `positions`: A token's position is 0 where a document begins and one more than the previous token's otherwise; every sequence begins a document at its first token; sequence 0 is one document of 2048 tokens.
All inputs are finite; a program needn't handle non-finite values.
Results may differ from the reference program's by a relative error of at most 0.028.
Values may be sent and summed in bfloat16 or wider, within the bound.
No kernel may reach another device: no remote copies, remote signals or barrier semaphores. Data moves between devices by JAX's collectives and lax.ppermute only.
A program may use at most 192 MiB of HBM per device.

```python
import jax
import jax.numpy as jnp
from jax import lax

D = 576
FF = 1536
HEADS = 9
KV_HEADS = 3
HD = 64
LAYERS = 2
HQ = 576
KVW = 192
SEQS = 8
LEN = 2048


def draw_positions(key, part):
    marks = jax.random.randint(key, (SEQS, LEN), 0, LEN) < 3
    index = jnp.broadcast_to(jnp.arange(LEN, dtype=jnp.int32), (SEQS, LEN))
    first_seq = jnp.arange(SEQS, dtype=jnp.int32)[:, None] == 0
    marks = marks & jnp.logical_not(first_seq) | (index == 0)
    begins = lax.cummax(jnp.where(marks, index, 0), axis=1)
    return (index - begins).astype(jnp.int32)


def strengthened(drawn, stream_key, source, target, blocks, factor):
    owner, partner = [(jnp.arange(drawn.shape[axis_at]) // (drawn.shape[axis_at] // blocks)).reshape([-1 if axis == axis_at else 1 for axis in range(drawn.ndim)]) for axis_at in (source, target)]
    chosen = jax.random.permutation(stream_key, blocks)[partner]
    strong = (owner == chosen) | (owner == (partner + blocks // 2) % blocks)
    return jnp.where(strong, factor * drawn, drawn)


def shard_levels(own_key, extent, cuts, low, largest):
    level = 1.0
    for dim, blocks in cuts:
        draws = jax.random.uniform(jax.random.fold_in(jax.random.fold_in(own_key, 6), dim), (blocks,), jnp.float32, low / len(cuts), largest / len(cuts))
        level = level * jnp.repeat(jnp.exp(draws), extent[dim] // blocks).reshape((-1,) + (1,) * (len(extent) - 1 - dim))
    return level


def bell_draw(stream_key, extent, scale, reach, cuts=(), kind=jnp.bfloat16):
    level = shard_levels(stream_key, extent, cuts, -0.22, 0.18) if cuts else 1.0
    array = jax.random.normal(stream_key, extent, jnp.float32) * scale * level
    return jnp.minimum(jnp.maximum(array, -reach), reach).astype(kind)


def heavy_noise(key, extent, spread, bound, cuts, heavy, held_as=jnp.bfloat16):
    array = spread * jax.random.normal(key, extent, jnp.float32)
    if cuts:
        array = array * shard_levels(key, extent, cuts, -0.22, 0.18)
    return jnp.clip(strengthened(array, jax.random.fold_in(key, 3), *heavy), -bound, bound).astype(held_as)


def setup_inputs(seed: int = 0) -> dict:
    key_of = jax.random.split(jax.random.key(seed), 13)
    tokens = heavy_noise(key_of[0], (SEQS, LEN, D), 1.0, 6.0, ((0, 8), (1, 4)), (0, 2, 8, 2.0))
    positions = draw_positions(jax.random.fold_in(key_of[12], 71), 0)
    query_weight = bell_draw(key_of[2], (LAYERS, D, HQ), D ** -0.5, 0.25, ((1, 8),))
    key_matrix = bell_draw(key_of[3], (LAYERS, D, KVW), D ** -0.5, 0.25, ((1, 8),))
    value_weight = bell_draw(key_of[4], (LAYERS, D, KVW), D ** -0.5, 0.25, ((1, 8),))
    out_weight = bell_draw(key_of[5], (LAYERS, HQ, D), (HQ // 16) ** -0.5, 1.0, ((1, 8),))
    gate_weight = bell_draw(key_of[6], (LAYERS, D, FF), D ** -0.5, 0.25, ((1, 8),))
    up_weight = bell_draw(key_of[7], (LAYERS, D, FF), D ** -0.5, 0.25, ((1, 8),))
    down_weight = bell_draw(key_of[8], (LAYERS, FF, D), FF ** -0.5, 0.15625, ((1, 8),))
    attn_gain = jnp.clip(1.0 + 0.1 * jax.random.normal(key_of[9], (LAYERS, D), jnp.float32), 0.5, 1.5).astype(jnp.bfloat16)
    mlp_gain = jnp.clip(1.0 + 0.1 * jax.random.normal(key_of[10], (LAYERS, D), jnp.float32), 0.5, 1.5).astype(jnp.bfloat16)
    cotangent = bell_draw(key_of[11], (SEQS, LEN, D), 1.0, 6.0, ((0, 8), (1, 4)))
    return {"tokens": tokens, "positions": positions, "query_weight": query_weight, "key_matrix": key_matrix, "value_weight": value_weight, "out_weight": out_weight, "gate_weight": gate_weight, "up_weight": up_weight, "down_weight": down_weight, "attn_gain": attn_gain, "mlp_gain": mlp_gain, "cotangent": cotangent}


@jax.custom_vjp
def low(v):
    return lax.optimization_barrier(v.astype(jnp.bfloat16)).astype(jnp.float32)

@jax.custom_vjp
def low_back(v):
    return v

def low_keep(v):
    return (low(v), None)

def low_pass(kept, grad):
    return (grad,)

def back_keep(v):
    return (v, None)

def back_low(kept, grad):
    return (low(grad),)
low.defvjp(low_keep, low_pass)
low_back.defvjp(back_keep, back_low)
epsilon = 1e-05
theta = 100000.0
log_two_e = 1.4426950408889634
mask_filler = -1e+30

def highest(left, right):
    return jnp.dot(left, right, precision=lax.Precision.HIGHEST)

def rms_norm(hidden, gain):
    scale = lax.rsqrt(lax.optimization_barrier(jnp.mean(hidden * hidden, axis=-1, keepdims=True)) + epsilon)
    return hidden * scale * gain

def rope_tables(positions, head_size):
    half = head_size // 2
    freq = theta ** (-(jnp.arange(half, dtype=jnp.float32) * 2.0 / head_size))
    angle = positions.astype(jnp.float32)[..., None] * freq
    return (jnp.cos(angle), jnp.sin(angle))

def rotate(values, cosine, sine):
    half = values.shape[-1] // 2
    first = values[..., :half]
    second = values[..., half:]
    cosine = cosine[..., None, :]
    sine = sine[..., None, :]
    return jnp.concatenate([first * cosine - second * sine, second * cosine + first * sine], axis=-1)

def attend(queries, key_rows, value_rows, positions):
    length = queries.shape[0]
    block_rows = min(512, length)
    count = length // block_rows
    index = jnp.arange(length, dtype=jnp.int32)
    doc_start = index - positions
    grouped = queries.reshape(count, block_rows, KV_HEADS, HEADS // KV_HEADS, HD)

    def one_block(item):
        query_block, first = item
        query_index = first * block_rows + jnp.arange(block_rows, dtype=jnp.int32)
        start = lax.dynamic_slice_in_dim(doc_start, first * block_rows, block_rows)
        visible = (index[None, :] <= query_index[:, None]) & (index[None, :] >= start[:, None])
        raw = jnp.einsum('qgjd,kgd->gjqk', query_block, key_rows, precision=lax.Precision.HIGHEST)
        scores = low_back(raw * 0.125) * log_two_e
        scores = jnp.where(visible, scores, mask_filler)
        row_top = jnp.floor(lax.optimization_barrier(jnp.max(scores, axis=-1, keepdims=True)))
        probs = jnp.where(visible, jnp.exp2(scores - row_top), 0.0)
        row_total = lax.optimization_barrier(jnp.sum(probs, axis=-1))
        numerator = low_back(jnp.einsum('gjqk,kgd->qgjd', low(probs), value_rows, precision=lax.Precision.HIGHEST))
        return numerator / jnp.transpose(row_total, (2, 0, 1))[..., None]
    blocks = lax.map(jax.checkpoint(one_block), (grouped, jnp.arange(count, dtype=jnp.int32)))
    return blocks.reshape(length, HEADS * HD)

def layer(hidden, positions, cosine, sine, weights):
    query_w, key_w, value_w, out_w, gate_w, up_w, down_w, first_gain, second_gain = weights
    length = hidden.shape[0]
    normed = low(rms_norm(hidden, first_gain))
    query_pre = low_back(highest(normed, query_w))
    key_pre = low_back(highest(normed, key_w))
    value_rows = low(low_back(highest(normed, value_w))).reshape(length, KV_HEADS, HD)
    queries = low(rotate(query_pre.reshape(length, HEADS, HD), cosine, sine))
    key_rows = low(rotate(key_pre.reshape(length, KV_HEADS, HD), cosine, sine))
    attention = attend(queries, key_rows, value_rows, positions)
    middle = hidden + low_back(highest(low(attention), out_w))
    mixed = low(rms_norm(middle, second_gain))
    gate = low_back(highest(mixed, gate_w))
    upward = low_back(highest(mixed, up_w))
    inner = low(jax.nn.silu(gate) * upward)
    return middle + low_back(highest(inner, down_w))

def forward(hidden, positions, weights):
    cosine, sine = rope_tables(positions, HD)
    for layer_index in range(LAYERS):
        hidden = layer(hidden, positions, cosine, sine, tuple((piece[layer_index] for piece in weights)))
    return hidden

def reference(tokens, positions, query_weight, key_matrix, value_weight, out_weight, gate_weight, up_weight, down_weight, attn_gain, mlp_gain, cotangent):
    weights = tuple((piece.astype(jnp.float32) for piece in (query_weight, key_matrix, value_weight, out_weight, gate_weight, up_weight, down_weight, attn_gain, mlp_gain)))

    def one_sequence(carry, item):
        seq_tokens, seq_positions, seq_cot = item
        output, pull = jax.vjp(lambda hidden, params: forward(hidden, seq_positions, params), seq_tokens.astype(jnp.float32), weights)
        grad_in, grad_params = pull(seq_cot.astype(jnp.float32))
        carry = tuple((total + part for total, part in zip(carry, grad_params)))
        return (carry, (output.astype(jnp.bfloat16), grad_in))
    zeros = tuple((jnp.zeros(piece.shape, jnp.float32) for piece in weights))
    gradient_tree, (outputs, input_grads) = lax.scan(one_sequence, zeros, (tokens, positions, cotangent))
    return (outputs, input_grads, gradient_tree[0], gradient_tree[1], gradient_tree[2], gradient_tree[3], gradient_tree[4], gradient_tree[5], gradient_tree[6], gradient_tree[7], gradient_tree[8])
```

```python
import jax
import jax.numpy as jnp
from jax import lax
from jax.experimental import pallas as pl
from jax.experimental.pallas import tpu as pltpu
from jax.sharding import PartitionSpec as P

HEADS = 9
KV_HEADS = 3
HD = 64
LAYERS = 2


epsilon = 1e-05
theta = 100000.0
log_two_e = 1.4426950408889634
mask_filler = -1e30


def flip(block, axis, mask):
    route = [(i, i ^ mask) for i in range(lax.axis_size(axis))]
    return lax.ppermute(block, axis, route)


def swap_halves(x):
    half = x.shape[1] // 2
    return jnp.concatenate(
        [x[:, :half], flip(x[:, half:], "ctx", lax.axis_size("ctx") - 1)], axis=1
    )


def tied(first, *then):
    return lax.optimization_barrier((first, then))[0]


def low(x):
    return x.astype(jnp.bfloat16)


def wide(x):
    return x.astype(jnp.float32)


PIECE = 384
VMEM_LIMIT = 48 * 1024 * 1024


def fold_down(shard):
    rows = shard.shape[0]
    right = shard[:, PIECE:]
    tall = jnp.concatenate(
        [shard[:, :PIECE], jnp.concatenate([right[: rows // 2], right[rows // 2 :]], axis=1)],
        axis=0,
    )
    return jnp.concatenate(jnp.split(tall, 4, axis=0), axis=1)


def unfold_down(folded):
    tall = jnp.concatenate(jnp.split(folded, 4, axis=-1), axis=-2)
    rows = tall.shape[-2] * 2 // 3
    left = tall[..., :rows, :]
    rest = tall[..., rows:, :]
    right = jnp.concatenate(jnp.split(rest, 2, axis=-1), axis=-2)
    return jnp.concatenate([left, right], axis=-1)


def assemble_kernel(count, own, own_flip, mine, theirs, out, sems):
    j = lax.axis_index("ctx")
    f = lax.axis_index("fsdp")
    copies = []

    def copy(src, dst):
        made = pltpu.make_async_copy(src, dst, sems.at[len(copies)])
        made.start()
        copies.append(made)

    copy(own, out.at[:, f])
    copy(own_flip, out.at[:, f ^ 1])
    for core, pieces in ((0, mine), (1, theirs)):
        for jrel in range(4):
            for zrel in range(1, 4):
                row = f ^ (core + 2 * zrel)
                column = pl.multiple_of((j ^ jrel) * PIECE, 128)
                copy(
                    pieces.at[jrel * 3 + zrel - 1],
                    out.at[:, row, :, pl.ds(column, PIECE)],
                )
    for made in copies:
        made.wait()


def assemble(own, own_flip, mine, theirs):
    count, rows, columns = own.shape
    fsdp = lax.axis_size("fsdp")
    return pl.pallas_call(
        lambda *refs: assemble_kernel(count, *refs),
        out_shape=jax.ShapeDtypeStruct((count, fsdp, rows, columns), own.dtype),
        in_specs=[pl.BlockSpec(memory_space=pl.ANY)] * 4,
        out_specs=pl.BlockSpec(memory_space=pltpu.VMEM),
        scratch_shapes=[pltpu.SemaphoreType.DMA((26,))],
        compiler_params=pltpu.CompilerParams(vmem_limit_bytes=VMEM_LIMIT),
        name="assemble",
    )(own, own_flip, mine, theirs)


def gather_line(own):
    j = lax.axis_index("ctx")
    piece = lax.dynamic_slice_in_dim(own, j * PIECE, PIECE, axis=2)
    return jnp.stack([flip(piece, "fsdp", 2 * k) for k in (1, 2, 3)])


def gather_rest(own, line):
    count, rows, columns = own.shape
    by_x = flip(line, "ctx", 1)
    by_y = flip(line, "ctx", 2)
    diag = jnp.concatenate([flip(by_x[:2], "ctx", 2), flip(by_y[2:], "ctx", 1)])
    mine = jnp.concatenate([line, by_x, by_y, diag])
    theirs = flip(mine, "fsdp", 1)
    own_flip = flip(own, "fsdp", 1)
    whole = assemble(own, own_flip, mine, theirs)
    return whole.reshape(count, -1, columns)


def gather_plain(own):
    return lax.all_gather(own, "fsdp", axis=1, tiled=True)


def scatter_kernel(whole, keep, send, sems):
    j = lax.axis_index("ctx")
    f = lax.axis_index("fsdp")
    copies = []
    for core, pieces in ((0, keep), (1, send)):
        for jrel in range(4):
            for zrel in range(4):
                row = f ^ (core + 2 * zrel)
                column = pl.multiple_of((j ^ jrel) * PIECE, 128)
                made = pltpu.make_async_copy(
                    whole.at[:, row, :, pl.ds(column, PIECE)],
                    pieces.at[jrel, zrel],
                    sems.at[len(copies)],
                )
                made.start()
                copies.append(made)
    for made in copies:
        made.wait()


def cut(whole):
    count, fsdp, rows, columns = whole.shape
    piece = jax.ShapeDtypeStruct((4, 4, count, rows, PIECE), whole.dtype)
    return pl.pallas_call(
        scatter_kernel,
        out_shape=(piece, piece),
        in_specs=[pl.BlockSpec(memory_space=pltpu.VMEM)],
        out_specs=[pl.BlockSpec(memory_space=pl.ANY)] * 2,
        scratch_shapes=[pltpu.SemaphoreType.DMA((32,))],
        compiler_params=pltpu.CompilerParams(vmem_limit_bytes=VMEM_LIMIT),
        name="cut",
    )(whole)


def reduce_fast(whole):
    keep, send = cut(whole)
    total = wide(keep) + wide(flip(send, "fsdp", 1))
    a = total[:, :2]
    b = total[:, 2:]
    x1 = wide(flip(low(jnp.stack([a[1], a[3]])), "ctx", 1))
    y1 = wide(flip(low(jnp.stack([b[2], b[3]])), "ctx", 2))
    a0, a2 = a[0] + x1[0], a[2] + x1[1]
    b0, b1 = b[0] + y1[0], b[1] + y1[1]
    a0 = a0 + wide(flip(low(a2), "ctx", 2))
    b0 = b0 + wide(flip(low(b1), "ctx", 1))
    return (
        a0[0]
        + wide(flip(low(a0[1]), "fsdp", 2))
        + wide(flip(low(b0[0]), "fsdp", 4))
        + wide(flip(low(b0[1]), "fsdp", 6))
    )


def spread_fast(piece):
    j = lax.axis_index("ctx")
    own = low(piece)
    parts = [own] + [flip(own, "ctx", k) for k in (1, 2, 3)]
    for bit in (1, 2):
        odd = (j & bit) != 0
        parts = [jnp.where(odd, parts[i ^ bit], parts[i]) for i in range(4)]
    return wide(jnp.concatenate(parts, axis=2))


def reduce_line(whole):
    part = lax.psum_scatter(whole, "fsdp", scatter_dimension=0, tiled=True)
    rows, columns = part.shape
    count = columns // (4 * PIECE)
    j = lax.axis_index("ctx")

    def piece(k):
        return jnp.stack(
            [
                lax.dynamic_slice_in_dim(part, m * 4 * PIECE + (j ^ k) * PIECE, PIECE, axis=1)
                for m in range(count)
            ]
        )

    return sum((wide(flip(piece(k), "ctx", k)) for k in (1, 2, 3)), wide(piece(0)))


def reduce_plain(whole):
    part = lax.psum_scatter(whole, "fsdp", scatter_dimension=1, tiled=True)
    return wide(lax.psum(part, "ctx"))


def dot_nn(a, b):
    return jnp.dot(a, b, preferred_element_type=jnp.float32)


def dot_nt(a, b):
    return lax.dot_general(a, b, (((1,), (1,)), ((), ())), preferred_element_type=jnp.float32)


def chunks_of(source, slots):
    return (2 * source, 2 * slots - 1 - 2 * source)


def stack_heads(ref, dst, half):
    group = HEADS // KV_HEADS
    for g in range(KV_HEADS):
        for part in range(2):
            for i in range(group):
                h = g * group + i
                dst[g, part, i * half : (i + 1) * half] = ref[
                    part * half : (part + 1) * half, h * HD : (h + 1) * HD
                ]


def thrice(row):
    return jnp.concatenate([row] * (HEADS // KV_HEADS), axis=1)


def attend_kernel(slots, *refs):
    q_ref, start_ref = refs[:2]
    kv_refs = refs[2 : 2 + slots]
    o_ref, lse_ref, qs, ks, vt, top_s, acc_s, ot = refs[2 + slots :]
    rank = lax.axis_index("ctx")
    half = q_ref.shape[0] // 2
    group = HEADS // KV_HEADS
    wide_cols = group * half
    stack_heads(q_ref, qs, half)
    ones = jnp.ones((16, half), jnp.bfloat16)
    for k in range(slots):
        values_t = low(jnp.transpose(wide(kv_refs[k][:, 128:])))
        for g in range(KV_HEADS):
            row = KV_HEADS * HD - 128 + g * HD
            for part in range(2):
                rows = slice(part * half, (part + 1) * half)
                ks[k, g, part] = kv_refs[k][rows, g * HD : (g + 1) * HD]
                vt[k, g, part, :HD] = values_t[row : row + HD, rows]
                vt[k, g, part, HD:] = ones
    lse_ref[...] = jnp.zeros_like(lse_ref)
    mine = chunks_of(rank, slots)

    def one_group(g, carry):
        for part in range(2):
            cols = slice(part * half, (part + 1) * half)
            start = thrice(start_ref[:, cols])
            q = qs[g, part]

            def scores(k, other, first):
                s = dot_nt(ks[k, g, other], q)
                key = lax.broadcasted_iota(jnp.int32, s.shape, 0)
                visible = key >= start - first
                return s, key, visible

            s, key, visible = scores(0, part, mine[part] * half)
            query = thrice(lax.broadcasted_iota(jnp.int32, (half, half), 1))
            s = jnp.where(visible & (key <= query), s, mask_filler)
            top = jnp.floor(jnp.max(s, axis=0, keepdims=True))
            top_s[...] = top
            acc_s[...] = dot_nn(vt[0, g, part], low(jnp.exp2(s - top)))

            def tile(k, other, chunk):
                @pl.when(chunk < mine[part])
                def _():
                    s, _, visible = scores(k, other, chunk * half)
                    s = jnp.where(visible, s, mask_filler)
                    old = top_s[...]
                    top = jnp.maximum(old, jnp.floor(jnp.max(s, axis=0, keepdims=True)))
                    top_s[...] = top
                    acc_s[...] = acc_s[...] * jnp.exp2(old - top) + dot_nn(
                        vt[k, g, other], low(jnp.exp2(s - top))
                    )

            tile(0, 1 - part, mine[1 - part])

            def slot(k, carry):
                theirs = chunks_of(rank ^ k, slots)
                for other in range(2):
                    tile(k, other, theirs[other])
                return carry

            lax.fori_loop(1, slots, slot, 0)
            total = acc_s[HD : HD + 1]
            out = acc_s[:HD] / total
            level = top_s[...] + jnp.log2(total)
            for i in range(group):
                inner = slice(i * half, (i + 1) * half)
                ot[g, i, :, cols] = out[:, inner]
                lse_ref[pl.ds(g * group + i, 1), cols] = level[:, inner]
        return carry

    lax.fori_loop(0, KV_HEADS, one_group, 0)
    o_ref[...] = low(jnp.transpose(ot[...].reshape(HEADS * HD, 2 * half)))


def attend(q, start, kvs):
    block = q.shape[0]
    half = block // 2
    slots = len(kvs)
    group = HEADS // KV_HEADS
    vmem = pl.BlockSpec(memory_space=pltpu.VMEM)
    return pl.pallas_call(
        lambda *refs: attend_kernel(slots, *refs),
        out_shape=(
            jax.ShapeDtypeStruct((block, HEADS * HD), jnp.bfloat16),
            jax.ShapeDtypeStruct((16, block), jnp.float32),
        ),
        in_specs=[vmem] * (2 + slots),
        out_specs=[vmem] * 2,
        scratch_shapes=[
            pltpu.VMEM((KV_HEADS, 2, group * half, HD), jnp.bfloat16),
            pltpu.VMEM((slots, KV_HEADS, 2, half, HD), jnp.bfloat16),
            pltpu.VMEM((slots, KV_HEADS, 2, HD + 16, half), jnp.bfloat16),
            pltpu.VMEM((1, group * half), jnp.float32),
            pltpu.VMEM((HD + 16, group * half), jnp.float32),
            pltpu.VMEM((KV_HEADS, group, HD, block), jnp.float32),
        ],
        compiler_params=pltpu.CompilerParams(vmem_limit_bytes=VMEM_LIMIT),
        cost_estimate=pl.CostEstimate(flops=15_000_000_000, bytes_accessed=4_000_000, transcendentals=0),
        name="attend",
    )(q, start, *kvs)


def attend_back_kernel(slots, *refs):
    q_ref, o_ref, do_ref, lse_ref, start_ref = refs[:5]
    kv_refs = refs[5 : 5 + slots]
    dq_ref = refs[5 + slots]
    dkv_refs = refs[6 + slots : 6 + 2 * slots]
    qs, dos, ks, kt, vs, dk_s, dv_s, dqt_s, delta_s, dqt_all = refs[6 + 2 * slots :]
    rank = lax.axis_index("ctx")
    half = q_ref.shape[0] // 2
    group = HEADS // KV_HEADS
    stack_heads(q_ref, qs, half)
    stack_heads(do_ref, dos, half)
    for k in range(slots):
        keys_t = low(jnp.transpose(wide(kv_refs[k][:, : 2 * 128])))
        for g in range(KV_HEADS):
            for part in range(2):
                rows = slice(part * half, (part + 1) * half)
                ks[k, g, part] = kv_refs[k][rows, g * HD : (g + 1) * HD]
                kt[k, g, part] = keys_t[g * HD : (g + 1) * HD, rows]
                vs[k, g, part] = kv_refs[k][rows, (KV_HEADS + g) * HD : (KV_HEADS + g + 1) * HD]
    product = wide(do_ref[...]) * wide(o_ref[...])
    coarse = low(product)
    fine = low(product - wide(coarse))
    shape = (16, HEADS * HD)
    owner = lax.div(lax.broadcasted_iota(jnp.int32, shape, 1), HD)
    pick = jnp.where(owner == lax.broadcasted_iota(jnp.int32, shape, 0), 1.0, 0.0)
    pick = pick.astype(jnp.bfloat16)
    delta_s[...] = dot_nt(pick, coarse) + dot_nt(pick, fine)
    dk_s[...] = jnp.zeros_like(dk_s)
    dv_s[...] = jnp.zeros_like(dv_s)
    mine = chunks_of(rank, slots)

    def one_group(g, carry):
        for part in range(2):
            cols = slice(part * half, (part + 1) * half)
            start = thrice(start_ref[:, cols])
            heads = [pl.ds(g * group + i, 1) for i in range(group)]
            lse = jnp.concatenate([lse_ref[h, cols] for h in heads], axis=1)
            delta = jnp.concatenate([delta_s[h, cols] for h in heads], axis=1)

            def tile(k, other, first, diagonal):
                q = qs[g, part]
                do = dos[g, part]
                s = dot_nt(ks[k, g, other], q)
                key = lax.broadcasted_iota(jnp.int32, s.shape, 0)
                visible = key >= start - first
                if diagonal:
                    query = thrice(lax.broadcasted_iota(jnp.int32, (half, half), 1))
                    visible = visible & (key <= query)
                p = jnp.where(visible, jnp.exp2(s - lse), 0.0)
                dv = dot_nn(low(p), do)
                dp = dot_nt(vs[k, g, other], do)
                ds = low(p * (dp - delta))
                dk_s[k, g, other] += dot_nn(ds, q)
                dv_s[k, g, other] += dv
                dq = dot_nn(kt[k, g, other], ds)
                if diagonal:
                    dqt_s[...] = dq
                else:
                    dqt_s[...] += dq

            tile(0, part, mine[part] * half, True)

            @pl.when(mine[1 - part] < mine[part])
            def _():
                tile(0, 1 - part, mine[1 - part] * half, False)

            def slot(k, carry):
                theirs = chunks_of(rank ^ k, slots)
                for other in range(2):

                    @pl.when(theirs[other] < mine[part])
                    def _():
                        tile(k, other, theirs[other] * half, False)

                return carry

            lax.fori_loop(1, slots, slot, 0)
            for i in range(group):
                dqt_all[g, i, :, cols] = dqt_s[:, i * half : (i + 1) * half]
        return carry

    lax.fori_loop(0, KV_HEADS, one_group, 0)
    dq_ref[...] = jnp.transpose(dqt_all[...].reshape(HEADS * HD, 2 * half)) * 0.125
    for k in range(slots):
        for part in range(2):
            dkv = jnp.concatenate(
                [dk_s[k, g, part] * (1.0 / log_two_e) for g in range(KV_HEADS)]
                + [dv_s[k, g, part] for g in range(KV_HEADS)],
                axis=1,
            )
            dkv_refs[k][part * half : (part + 1) * half] = dkv.astype(dkv_refs[k].dtype)


def attend_back(q, o, do, lse, start_row, kvs):
    block = q.shape[0]
    half = block // 2
    slots = len(kvs)
    group = HEADS // KV_HEADS
    vmem = pl.BlockSpec(memory_space=pltpu.VMEM)
    pair = lambda kind: jax.ShapeDtypeStruct((block, 2 * KV_HEADS * HD), kind)
    return pl.pallas_call(
        lambda *refs: attend_back_kernel(slots, *refs),
        out_shape=(
            jax.ShapeDtypeStruct((block, HEADS * HD), jnp.float32),
            pair(jnp.float32),
            *[pair(jnp.bfloat16)] * (slots - 1),
        ),
        in_specs=[vmem] * (5 + slots),
        out_specs=[vmem] * (1 + slots),
        scratch_shapes=[
            pltpu.VMEM((KV_HEADS, 2, group * half, HD), jnp.bfloat16),
            pltpu.VMEM((KV_HEADS, 2, group * half, HD), jnp.bfloat16),
            pltpu.VMEM((slots, KV_HEADS, 2, half, HD), jnp.bfloat16),
            pltpu.VMEM((slots, KV_HEADS, 2, HD, half), jnp.bfloat16),
            pltpu.VMEM((slots, KV_HEADS, 2, half, HD), jnp.bfloat16),
            pltpu.VMEM((slots, KV_HEADS, 2, half, HD), jnp.float32),
            pltpu.VMEM((slots, KV_HEADS, 2, half, HD), jnp.float32),
            pltpu.VMEM((HD, group * half), jnp.float32),
            pltpu.VMEM((16, block), jnp.float32),
            pltpu.VMEM((KV_HEADS, group, HD, block), jnp.float32),
        ],
        compiler_params=pltpu.CompilerParams(vmem_limit_bytes=VMEM_LIMIT),
        cost_estimate=pl.CostEstimate(flops=20_000_000_000, bytes_accessed=4_000_000, transcendentals=0),
        name="attend_back",
    )(q, o, do, lse, start_row, *kvs)


def rms_norm(hidden, gain):
    scale = lax.rsqrt(jnp.mean(hidden * hidden, axis=-1, keepdims=True) + epsilon)
    return hidden * scale * gain


def rope_tables(positions, head_size):
    half = head_size // 2
    freq = theta ** (-(jnp.arange(half, dtype=jnp.float32) * 2.0 / head_size))
    angle = positions.astype(jnp.float32)[..., None] * freq
    return (jnp.cos(angle), jnp.sin(angle))


def rotate(values, cosine, sine):
    half = values.shape[-1] // 2
    first = values[..., :half]
    second = values[..., half:]
    cosine = cosine[..., None, :]
    sine = sine[..., None, :]
    return jnp.concatenate(
        [first * cosine - second * sine, second * cosine + first * sine], axis=-1
    )


def project(input_tokens, weight_matrix):
    return jnp.einsum(
        "vnk,kp->vnp", input_tokens, weight_matrix, preferred_element_type=jnp.float32
    )


def project_back(gradient_tree, weight_matrix):
    return jnp.einsum(
        "qzy,gy->qzg", gradient_tree, weight_matrix, preferred_element_type=jnp.float32
    )


def outer_sum(input_tokens, gradient_tree):
    return jnp.einsum(
        "cwu,cwf->uf", input_tokens, gradient_tree, preferred_element_type=jnp.float32
    )


def body(
    tokens,
    positions,
    query_weight,
    key_matrix,
    value_weight,
    out_weight,
    gate_weight,
    up_weight,
    down_weight,
    attn_gain,
    mlp_gain,
    cotangent,
):
    cycle_size = lax.axis_size("ctx")
    cycle_rank = lax.axis_index("ctx")
    sequence_count, block, width = tokens.shape
    kv_heads = KV_HEADS
    group = HEADS // KV_HEADS
    head_size = HD
    tokens = swap_halves(tokens)
    positions = swap_halves(positions)
    cosine, sine = rope_tables(positions, head_size)
    half = block // 2
    first_row, second_row = chunks_of(cycle_rank, cycle_size)
    offsets = jnp.arange(half, dtype=jnp.int32)
    row_index = jnp.concatenate([first_row * half + offsets, second_row * half + offsets])
    doc_start = row_index[None, :] - positions

    def backward_layer(grad_out, full, kept):
        (
            query_full,
            key_full,
            value_full,
            out_full,
            gate_full,
            up_full,
            down_full,
            first_gain,
            second_gain,
        ) = full
        (
            hidden,
            normed_low,
            queries,
            kvs,
            lse,
            attn_low,
            middle,
            mixed_low,
            gate,
            upward,
            inner,
        ) = kept
        down_in = grad_out.astype(jnp.bfloat16)
        grad_down = outer_sum(inner, down_in)
        d_inner = project_back(down_in, down_full)
        unused, pull_gate = jax.vjp(
            lambda gate_in, up_in: jax.nn.silu(gate_in) * up_in, gate, upward
        )
        d_gate, d_up = pull_gate(d_inner)
        d_gate = d_gate.astype(jnp.bfloat16)
        d_up = d_up.astype(jnp.bfloat16)
        grad_gate = outer_sum(mixed_low, d_gate)
        grad_up = outer_sum(mixed_low, d_up)
        d_mixed = project_back(d_gate, gate_full) + project_back(d_up, up_full)
        unused, pull_second = jax.vjp(rms_norm, middle, second_gain.astype(jnp.float32))
        d_middle, grad_second = pull_second(d_mixed)
        grad_mid = grad_out + d_middle
        mid_low = grad_mid.astype(jnp.bfloat16)
        grad_out_proj = outer_sum(attn_low, mid_low)
        d_attention = low(project_back(mid_low, out_full)[0])
        d_query, *d_pairs = attend_back(
            queries, attn_low[0], d_attention, lse, doc_start, kvs
        )
        d_pair = d_pairs[0]
        for k, part in enumerate(d_pairs[1:]):
            d_pair = d_pair + wide(flip(part, "ctx", k + 1))
        travel = (
            d_pair[:, : kv_heads * head_size].reshape(1, block, kv_heads, head_size),
            d_pair[:, kv_heads * head_size :],
        )
        dq_low = (
            rotate(d_query.reshape(sequence_count, block, HEADS, head_size), cosine, -sine)
            .astype(jnp.bfloat16)
            .reshape(sequence_count, block, HEADS * head_size)
        )
        dk_low = (
            rotate(travel[0], cosine, -sine)
            .astype(jnp.bfloat16)
            .reshape(sequence_count, block, kv_heads * head_size)
        )
        dv_low = travel[1].astype(jnp.bfloat16).reshape(sequence_count, block, kv_heads * head_size)
        grad_query = outer_sum(normed_low, dq_low)
        grad_key = outer_sum(normed_low, dk_low)
        grad_value = outer_sum(normed_low, dv_low)
        normed_gradient = (
            project_back(dq_low, query_full)
            + project_back(dk_low, key_full)
            + project_back(dv_low, value_full)
        )
        unused, pull_first = jax.vjp(rms_norm, hidden, first_gain.astype(jnp.float32))
        d_hidden, grad_first = pull_first(normed_gradient)
        grad_in = grad_mid + d_hidden
        return (
            grad_in,
            (
                grad_query,
                grad_key,
                grad_value,
                grad_out_proj,
                grad_gate,
                grad_up,
                grad_down,
                grad_first,
                grad_second,
            ),
        )

    fast = cycle_size == 4 and lax.axis_size("fsdp") == 8
    heads_width = HEADS * head_size
    kv_width = kv_heads * head_size
    packs = [
        jnp.stack(
            [
                jnp.concatenate(
                    [query_weight[i], key_matrix[i], value_weight[i], out_weight[i]], axis=1
                ),
                gate_weight[i],
                up_weight[i],
                fold_down(down_weight[i]),
            ]
        )
        for i in range(LAYERS)
    ]
    gains = lax.all_gather(jnp.concatenate([attn_gain, mlp_gain]), "fsdp", axis=1, tiled=True)
    if fast:
        own_first = packs[0][:1]
        own_second = jnp.concatenate([packs[0][1:], packs[1][:1]])
        first_line = gather_line(own_first)
        second_line = gather_line(tied(own_second, first_line))
        third = gather_plain(tied(packs[1][1:], second_line))
        first = gather_rest(own_first, first_line)
        whole = [(first[0], None, None, None), (None, third[0], third[1], third[2])]
    else:
        third = [gather_plain(packs[i]) for i in range(LAYERS)]
        whole = [tuple(third[i][m] for m in range(4)) for i in range(LAYERS)]

    def attention_weights(i):
        attn = whole[i][0]
        ends = (heads_width, heads_width + kv_width, heads_width + 2 * kv_width)
        return (
            attn[:, : ends[0]],
            attn[:, ends[0] : ends[1]],
            attn[:, ends[1] : ends[2]],
            attn[:, ends[2] :],
        )

    def mlp_weights(i):
        _, gate_full, up_full, folded = whole[i]
        fsdp = lax.axis_size("fsdp")
        down_full = unfold_down(folded.reshape(fsdp, -1, folded.shape[1])).reshape(-1, width)
        return (gate_full, up_full, down_full)

    fulls = []
    hidden = tokens.astype(jnp.float32)
    saved = []
    for index in range(LAYERS):
        (
            forward_query_full,
            forward_key_full,
            forward_value_full,
            forward_out_full,
        ) = attention_weights(index)
        forward_first_gain, forward_second_gain = gains[index], gains[LAYERS + index]
        forward_normed_low = rms_norm(hidden, forward_first_gain.astype(jnp.float32)).astype(
            jnp.bfloat16
        )
        query_pre = project(forward_normed_low, forward_query_full)
        key_pre = project(forward_normed_low, forward_key_full)
        forward_value_low = low(project(forward_normed_low, forward_value_full))[0]
        forward_queries = rotate(
            query_pre.reshape(sequence_count, block, HEADS, head_size), cosine, sine
        )
        forward_queries = low(forward_queries * (0.125 * log_two_e)).reshape(block, -1)
        forward_key_rows = rotate(
            key_pre.reshape(sequence_count, block, kv_heads, head_size), cosine, sine
        )
        forward_key_rows = low(forward_key_rows).reshape(block, -1)
        pair = jnp.concatenate([forward_key_rows, forward_value_low], axis=1)
        kvs = [pair] + [flip(pair, "ctx", k) for k in range(1, cycle_size)]
        if fast and index == 0:
            second = gather_rest(own_second, tied(second_line, kvs))
            whole = [(first[0], *second[:3]), (second[3], *third)]
        forward_attn_low, lse = attend(forward_queries, doc_start, kvs)
        forward_attn_low = forward_attn_low[None]
        forward_gate_full, forward_up_full, forward_down_full = mlp_weights(index)
        fulls.append(
            (
                forward_query_full,
                forward_key_full,
                forward_value_full,
                forward_out_full,
                forward_gate_full,
                forward_up_full,
                forward_down_full,
                forward_first_gain,
                forward_second_gain,
            )
        )
        forward_middle = hidden + project(forward_attn_low, forward_out_full)
        forward_mixed_low = rms_norm(
            forward_middle, forward_second_gain.astype(jnp.float32)
        ).astype(jnp.bfloat16)
        forward_gate = project(forward_mixed_low, forward_gate_full)
        forward_upward = project(forward_mixed_low, forward_up_full)
        forward_inner = (jax.nn.silu(forward_gate) * forward_upward).astype(jnp.bfloat16)
        output = forward_middle + project(forward_inner, forward_down_full)
        forward_kept = (
            hidden,
            forward_normed_low,
            forward_queries,
            kvs,
            lse,
            forward_attn_low,
            forward_middle,
            forward_mixed_low,
            forward_gate,
            forward_upward,
            forward_inner,
        )
        hidden = output
        kept = forward_kept
        saved.append(kept)
    layer_out = swap_halves(low(hidden))
    grad = wide(swap_halves(tied(cotangent, saved[0][0])))
    matrix_grads = [None] * LAYERS
    gain_grads = [None] * LAYERS
    fsdp = lax.axis_size("fsdp")
    gain_rows = attn_gain.shape[1]
    for index in reversed(range(LAYERS)):
        grad, tree = backward_layer(grad, fulls[index], saved[index])
        gain_grads[index] = (tree[7], tree[8])
        down_rows = low(tree[6]).reshape(fsdp, -1, width)
        folded = jax.vmap(fold_down)(down_rows).reshape(width, -1)
        attn = jnp.concatenate([low(part) for part in tree[:4]], axis=1)
        rest = (low(tree[4]), low(tree[5]), folded)
        if fast and index == 0:
            by_shard = lambda x: x.reshape(fsdp, gain_rows, -1)
            rest_piece = reduce_fast(jnp.stack([by_shard(part) for part in rest]))
            rest_grads = spread_fast(rest_piece)
            gain_parts = jnp.stack([gain_grads[i][m] for m in range(2) for i in range(LAYERS)])
            gain_parts = low(gain_parts).reshape(2 * LAYERS, fsdp, gain_rows).transpose(1, 0, 2)
            gain_parts = gain_parts.reshape(fsdp, 1, -1)
            gain_parts = jnp.pad(gain_parts, ((0, 0), (0, 7), (0, PIECE - gain_parts.shape[2])))
            last = jnp.concatenate([by_shard(attn), jnp.tile(gain_parts, (1, 1, 4))], axis=1)
            attn_piece = reduce_fast(last[None])
            all_gains = attn_piece[0, gain_rows, : 2 * LAYERS * gain_rows]
            all_gains = all_gains.reshape(2 * LAYERS, gain_rows)
            attn_grads = spread_fast(attn_piece[:, :gain_rows])
            matrix_grads[index] = jnp.concatenate([attn_grads, rest_grads])
        elif fast:
            rest_piece = reduce_line(jnp.concatenate(rest, axis=1))
            attn_piece = reduce_line(attn)
            matrix_grads[index] = spread_fast(jnp.concatenate([attn_piece, rest_piece]))
        else:
            matrix_grads[index] = reduce_plain(jnp.stack([attn, *rest]))
    if not fast:
        all_gains = jnp.stack([gain_grads[i][m] for m in range(2) for i in range(LAYERS)])
        all_gains = lax.psum(all_gains, ("ctx", "fsdp"))
        all_gains = lax.dynamic_slice_in_dim(
            all_gains, lax.axis_index("fsdp") * gain_rows, gain_rows, axis=1
        )
    grad = wide(swap_halves(low(grad)))
    stacked = jnp.stack(matrix_grads)
    ends = (heads_width, heads_width + kv_width, heads_width + 2 * kv_width)
    results = (
        stacked[:, 0, :, : ends[0]],
        stacked[:, 0, :, ends[0] : ends[1]],
        stacked[:, 0, :, ends[1] : ends[2]],
        stacked[:, 0, :, ends[2] :],
        stacked[:, 1],
        stacked[:, 2],
        unfold_down(stacked[:, 3]),
        all_gains[:LAYERS],
        all_gains[LAYERS:],
    )
    return (
        layer_out,
        grad,
        results[0],
        results[1],
        results[2],
        results[3],
        results[4],
        results[5],
        results[6],
        results[7],
        results[8],
    )


def solution(mesh):
    return jax.shard_map(
        body,
        mesh=mesh,
        in_specs=(
            P("fsdp", "ctx", None),
            P("fsdp", "ctx"),
            P(None, "fsdp", None),
            P(None, "fsdp", None),
            P(None, "fsdp", None),
            P(None, "fsdp", None),
            P(None, "fsdp", None),
            P(None, "fsdp", None),
            P(None, "fsdp", None),
            P(None, "fsdp"),
            P(None, "fsdp"),
            P("fsdp", "ctx", None),
        ),
        out_specs=(
            P("fsdp", "ctx", None),
            P("fsdp", "ctx", None),
            P(None, "fsdp", None),
            P(None, "fsdp", None),
            P(None, "fsdp", None),
            P(None, "fsdp", None),
            P(None, "fsdp", None),
            P(None, "fsdp", None),
            P(None, "fsdp", None),
            P(None, "fsdp"),
            P(None, "fsdp"),
        ),
        check_vma=False,
    )
```

```python
import jax
import jax.numpy as jnp
from jax import lax
from jax.experimental import pallas as pl
from jax.experimental.pallas import tpu as pltpu
from jax.sharding import PartitionSpec as P

HEADS = 9
KV_HEADS = 3
HD = 64
LAYERS = 2


epsilon = 1e-05
theta = 100000.0
log_two_e = 1.4426950408889634
mask_filler = -1e30


def flip(block, axis, mask):
    route = [(i, i ^ mask) for i in range(lax.axis_size(axis))]
    return lax.ppermute(block, axis, route)


def swap_halves(x):
    half = x.shape[1] // 2
    return jnp.concatenate(
        [x[:, :half], flip(x[:, half:], "ctx", lax.axis_size("ctx") - 1)], axis=1
    )


def tied(first, *then):
    return lax.optimization_barrier((first, then))[0]


def low(x):
    return x.astype(jnp.bfloat16)


def wide(x):
    return x.astype(jnp.float32)


PIECE = 384
VMEM_LIMIT = 48 * 1024 * 1024


def fold_down(shard):
    step = shard.shape[0] // 4
    pieces = []
    for j in range(4):
        rows = shard[j * step : (j + 1) * step]
        rest = rows[:, PIECE:]
        rest = jnp.concatenate([rest[: step // 2], rest[step // 2 :]], axis=1)
        pieces.append(jnp.concatenate([rows[:, :PIECE], rest], axis=0))
    return jnp.concatenate(pieces, axis=1)


def unfold_down(folded):
    step = folded.shape[-2] * 2 // 3
    pieces = []
    for piece in jnp.split(folded, 4, axis=-1):
        rest = piece[..., step:, :]
        rest = jnp.concatenate(jnp.split(rest, 2, axis=-1), axis=-2)
        pieces.append(jnp.concatenate([piece[..., :step, :], rest], axis=-1))
    return jnp.concatenate(pieces, axis=-2)


def assemble_kernel(rows, own, own_flip, mine, theirs, out, *rest):
    sems = rest[-1]
    j = lax.axis_index("ctx")
    f = lax.axis_index("fsdp")
    copies = []

    def copy(src, dst):
        made = pltpu.make_async_copy(src, dst, sems.at[len(copies)])
        made.start()
        copies.append(made)

    for core, shard in ((0, own), (1, own_flip)):
        copy(shard.at[:, :rows], out.at[:, f ^ core])
        if len(rest) > 1:
            copy(shard.at[0, rows:, :PIECE], rest[0].at[f ^ core])
    for core, pieces in ((0, mine), (1, theirs)):
        for jrel in range(4):
            for zrel in range(1, 4):
                row = f ^ (core + 2 * zrel)
                column = pl.multiple_of((j ^ jrel) * PIECE, 128)
                piece = pieces.at[jrel * 3 + zrel - 1]
                copy(piece.at[:, :rows], out.at[:, row, :, pl.ds(column, PIECE)])
                if jrel == 0 and len(rest) > 1:
                    copy(piece.at[0, rows:], rest[0].at[row])
    for made in copies:
        made.wait()


def assemble(rows, own, own_flip, mine, theirs):
    count, all_rows, columns = own.shape
    fsdp = lax.axis_size("fsdp")
    shapes = [jax.ShapeDtypeStruct((count, fsdp, rows, columns), own.dtype)]
    if all_rows > rows:
        shapes.append(jax.ShapeDtypeStruct((fsdp, all_rows - rows, PIECE), own.dtype))
    return pl.pallas_call(
        lambda *refs: assemble_kernel(rows, *refs),
        out_shape=tuple(shapes),
        in_specs=[pl.BlockSpec(memory_space=pl.ANY)] * 4,
        out_specs=[pl.BlockSpec(memory_space=pltpu.VMEM)] * len(shapes),
        scratch_shapes=[pltpu.SemaphoreType.DMA((34,))],
        compiler_params=pltpu.CompilerParams(vmem_limit_bytes=VMEM_LIMIT),
        name="assemble",
    )(own, own_flip, mine, theirs)


def gather_line(own):
    j = lax.axis_index("ctx")
    piece = lax.dynamic_slice_in_dim(own, j * PIECE, PIECE, axis=2)
    return jnp.stack([flip(piece, "fsdp", 2 * k) for k in (1, 2, 3)])


def gather_sides(line):
    return flip(line, "ctx", 1), flip(line, "ctx", 2)


def gather_rest(rows, own, own_flip, line, sides):
    by_x, by_y = sides
    diag = jnp.concatenate([flip(by_x[:2], "ctx", 2), flip(by_y[2:], "ctx", 1)])
    mine = jnp.concatenate([line, by_x, by_y, diag])
    theirs = flip(mine, "fsdp", 1)
    return assemble(rows, own, own_flip, mine, theirs), mine


def gather_plain(own):
    return lax.all_gather(own, "fsdp", axis=1, tiled=True)


def scatter_kernel(whole, keep, send, sems):
    j = lax.axis_index("ctx")
    f = lax.axis_index("fsdp")
    copies = []
    for core, pieces in ((0, keep), (1, send)):
        for jrel in range(4):
            for zrel in range(4):
                row = f ^ (core + 2 * zrel)
                column = pl.multiple_of((j ^ jrel) * PIECE, 128)
                made = pltpu.make_async_copy(
                    whole.at[row, :, :, pl.ds(column, PIECE)],
                    pieces.at[jrel, zrel],
                    sems.at[len(copies)],
                )
                made.start()
                copies.append(made)
    for made in copies:
        made.wait()


def cut(whole):
    fsdp, count, rows, columns = whole.shape
    piece = jax.ShapeDtypeStruct((4, 4, count, rows, PIECE), whole.dtype)
    return pl.pallas_call(
        scatter_kernel,
        out_shape=(piece, piece),
        in_specs=[pl.BlockSpec(memory_space=pltpu.VMEM)],
        out_specs=[pl.BlockSpec(memory_space=pl.ANY)] * 2,
        scratch_shapes=[pltpu.SemaphoreType.DMA((32,))],
        compiler_params=pltpu.CompilerParams(vmem_limit_bytes=VMEM_LIMIT),
        name="cut",
    )(whole)


def reduce_begin(whole):
    keep, send = cut(whole)
    total = wide(keep) + wide(flip(send, "fsdp", 1))
    a = total[:, :2]
    b = total[:, 2:]
    return (a[0], a[2], b[0], b[1]), (low(jnp.stack([a[1], a[3]])), low(jnp.stack([b[2], b[3]])))


def reduce_sides(sends):
    return flip(sends[0], "ctx", 1), flip(sends[1], "ctx", 2)


def reduce_end(sums, sides):
    a0, a2, b0, b1 = sums
    x1, y1 = wide(sides[0]), wide(sides[1])
    a0, a2 = a0 + x1[0], a2 + x1[1]
    b0, b1 = b0 + y1[0], b1 + y1[1]
    a0 = a0 + wide(flip(low(a2), "ctx", 2))
    b0 = b0 + wide(flip(low(b1), "ctx", 1))
    return (
        a0[0]
        + wide(flip(low(a0[1]), "fsdp", 2))
        + wide(flip(low(b0[0]), "fsdp", 4))
        + wide(flip(low(b0[1]), "fsdp", 6))
    )


def spread_fast(piece):
    j = lax.axis_index("ctx")
    own = low(piece)
    parts = [own] + [flip(own, "ctx", k) for k in (1, 2, 3)]
    for bit in (1, 2):
        odd = (j & bit) != 0
        parts = [jnp.where(odd, parts[i ^ bit], parts[i]) for i in range(4)]
    return wide(jnp.concatenate(parts, axis=2))


def line_pieces(whole):
    part = lax.psum_scatter(whole, "fsdp", scatter_dimension=0, tiled=True)[0]
    j = lax.axis_index("ctx")
    return [
        lax.dynamic_slice_in_dim(part, (j ^ k) * PIECE, PIECE, axis=2) for k in range(4)
    ]


def line_sum(pieces):
    return sum(
        (wide(flip(pieces[k], "ctx", k)) for k in (1, 2, 3)), wide(pieces[0])
    )


def reduce_plain(whole, dim):
    part = lax.psum_scatter(whole, "fsdp", scatter_dimension=dim, tiled=True)
    return wide(lax.psum(part, "ctx"))


def dot_nn(a, b):
    return jnp.dot(a, b, preferred_element_type=jnp.float32)


def dot_nt(a, b):
    return lax.dot_general(a, b, (((1,), (1,)), ((), ())), preferred_element_type=jnp.float32)


def dot_tn(a, b):
    return lax.dot_general(a, b, (((0,), (0,)), ((), ())), preferred_element_type=jnp.float32)


def run_kernel(body, inputs, outputs, scratch=(), cost=0, name=None):
    count = len(inputs)

    def kernel(*refs):
        sources = refs[:count]
        outs = refs[count : count + len(outputs)]
        rest = refs[count + len(outputs) :]
        buffers, extra, sems = rest[:count], rest[count:-1], rest[-1]
        copies = [
            pltpu.make_async_copy(source, buffer, sems.at[i])
            for i, (source, buffer) in enumerate(zip(sources, buffers))
        ]
        for copy in copies:
            copy.start()
        waited = set()

        def get(i):
            if i not in waited:
                waited.add(i)
                copies[i].wait()
            return buffers[i]

        body(get, outs, extra)
        for i in range(count):
            get(i)

    return pl.pallas_call(
        kernel,
        out_shape=tuple(outputs),
        in_specs=[pl.BlockSpec(memory_space=pl.ANY)] * count,
        out_specs=[pl.BlockSpec(memory_space=pltpu.VMEM)] * len(outputs),
        scratch_shapes=[
            *[pltpu.VMEM(x.shape, x.dtype) for x in inputs],
            *scratch,
            pltpu.SemaphoreType.DMA((count,)),
        ],
        compiler_params=pltpu.CompilerParams(vmem_limit_bytes=VMEM_LIMIT),
        cost_estimate=pl.CostEstimate(flops=cost, bytes_accessed=4_000_000, transcendentals=0),
        name=name,
    )(*inputs)


def like(shape, kind):
    return jax.ShapeDtypeStruct(shape, kind)


def chunks_of(source, slots):
    return (2 * source, 2 * slots - 1 - 2 * source)


def stack_heads(ref, dst, half):
    group = HEADS // KV_HEADS
    for g in range(KV_HEADS):
        for part in range(2):
            for i in range(group):
                h = g * group + i
                dst[g, part, i * half : (i + 1) * half] = ref[
                    part * half : (part + 1) * half, h * HD : (h + 1) * HD
                ]


def thrice(row):
    return jnp.concatenate([row] * (HEADS // KV_HEADS), axis=1)


def attend_kernel(slots, *refs):
    q_ref, start_ref = refs[:2]
    kv_refs = refs[2 : 2 + slots]
    o_ref, lse_ref, qs, ks, vt, top_s, acc_s, ot = refs[2 + slots :]
    rank = lax.axis_index("ctx")
    half = q_ref.shape[0] // 2
    group = HEADS // KV_HEADS
    wide_cols = group * half
    stack_heads(q_ref, qs, half)
    ones = jnp.ones((16, half), jnp.bfloat16)
    for k in range(slots):
        values_t = low(jnp.transpose(wide(kv_refs[k][:, 128:])))
        for g in range(KV_HEADS):
            row = KV_HEADS * HD - 128 + g * HD
            for part in range(2):
                rows = slice(part * half, (part + 1) * half)
                ks[k, g, part] = kv_refs[k][rows, g * HD : (g + 1) * HD]
                vt[k, g, part, :HD] = values_t[row : row + HD, rows]
                vt[k, g, part, HD:] = ones
    lse_ref[...] = jnp.zeros_like(lse_ref)
    mine = chunks_of(rank, slots)

    def one_group(g, carry):
        for part in range(2):
            cols = slice(part * half, (part + 1) * half)
            start = thrice(start_ref[:, cols])
            q = qs[g, part]

            def scores(k, other, first):
                s = dot_nt(ks[k, g, other], q)
                key = lax.broadcasted_iota(jnp.int32, s.shape, 0)
                visible = key >= start - first
                return s, key, visible

            s, key, visible = scores(0, part, mine[part] * half)
            query = thrice(lax.broadcasted_iota(jnp.int32, (half, half), 1))
            s = jnp.where(visible & (key <= query), s, mask_filler)
            top = jnp.floor(jnp.max(s, axis=0, keepdims=True))
            top_s[...] = top
            acc_s[...] = dot_nn(vt[0, g, part], low(jnp.exp2(s - top)))

            def tile(k, other, chunk):
                @pl.when(chunk < mine[part])
                def _():
                    s, _, visible = scores(k, other, chunk * half)
                    s = jnp.where(visible, s, mask_filler)
                    old = top_s[...]
                    top = jnp.maximum(old, jnp.floor(jnp.max(s, axis=0, keepdims=True)))
                    top_s[...] = top
                    acc_s[...] = acc_s[...] * jnp.exp2(old - top) + dot_nn(
                        vt[k, g, other], low(jnp.exp2(s - top))
                    )

            tile(0, 1 - part, mine[1 - part])

            def slot(k, carry):
                theirs = chunks_of(rank ^ k, slots)
                for other in range(2):
                    tile(k, other, theirs[other])
                return carry

            lax.fori_loop(1, slots, slot, 0)
            total = acc_s[HD : HD + 1]
            out = acc_s[:HD] / total
            level = top_s[...] + jnp.log2(total)
            for i in range(group):
                inner = slice(i * half, (i + 1) * half)
                ot[g, i, :, cols] = out[:, inner]
                lse_ref[pl.ds(g * group + i, 1), cols] = level[:, inner]
        return carry

    lax.fori_loop(0, KV_HEADS, one_group, 0)
    o_ref[...] = low(jnp.transpose(ot[...].reshape(HEADS * HD, 2 * half)))


def attend(q, start, kvs):
    block = q.shape[0]
    half = block // 2
    slots = len(kvs)
    group = HEADS // KV_HEADS
    inputs = (q, start, *kvs)

    def body(get, outs, extra):
        attend_kernel(slots, *[get(i) for i in range(len(inputs))], *outs, *extra)

    return run_kernel(
        body,
        inputs,
        (like((block, HEADS * HD), jnp.bfloat16), like((16, block), jnp.float32)),
        scratch=(
            pltpu.VMEM((KV_HEADS, 2, group * half, HD), jnp.bfloat16),
            pltpu.VMEM((slots, KV_HEADS, 2, half, HD), jnp.bfloat16),
            pltpu.VMEM((slots, KV_HEADS, 2, HD + 16, half), jnp.bfloat16),
            pltpu.VMEM((1, group * half), jnp.float32),
            pltpu.VMEM((HD + 16, group * half), jnp.float32),
            pltpu.VMEM((KV_HEADS, group, HD, block), jnp.float32),
        ),
        cost=15_000_000_000,
        name="attend",
    )


def attend_back_kernel(slots, *refs):
    q_ref, o_ref, do_ref, lse_ref, start_ref = refs[:5]
    kv_refs = refs[5 : 5 + slots]
    dq_ref = refs[5 + slots]
    dkv_refs = refs[6 + slots : 6 + 2 * slots]
    qs, dos, ks, kt, vs, dk_s, dv_s, dqt_s, delta_s, dqt_all = refs[6 + 2 * slots :]
    rank = lax.axis_index("ctx")
    half = q_ref.shape[0] // 2
    group = HEADS // KV_HEADS
    stack_heads(q_ref, qs, half)
    stack_heads(do_ref, dos, half)
    for k in range(slots):
        keys_t = low(jnp.transpose(wide(kv_refs[k][:, : 2 * 128])))
        for g in range(KV_HEADS):
            for part in range(2):
                rows = slice(part * half, (part + 1) * half)
                ks[k, g, part] = kv_refs[k][rows, g * HD : (g + 1) * HD]
                kt[k, g, part] = keys_t[g * HD : (g + 1) * HD, rows]
                vs[k, g, part] = kv_refs[k][rows, (KV_HEADS + g) * HD : (KV_HEADS + g + 1) * HD]
    product = wide(do_ref[...]) * wide(o_ref[...])
    coarse = low(product)
    fine = low(product - wide(coarse))
    shape = (16, HEADS * HD)
    owner = lax.div(lax.broadcasted_iota(jnp.int32, shape, 1), HD)
    pick = jnp.where(owner == lax.broadcasted_iota(jnp.int32, shape, 0), 1.0, 0.0)
    pick = pick.astype(jnp.bfloat16)
    delta_s[...] = dot_nt(pick, coarse) + dot_nt(pick, fine)
    dk_s[...] = jnp.zeros_like(dk_s)
    dv_s[...] = jnp.zeros_like(dv_s)
    mine = chunks_of(rank, slots)

    def one_group(g, carry):
        for part in range(2):
            cols = slice(part * half, (part + 1) * half)
            start = thrice(start_ref[:, cols])
            heads = [pl.ds(g * group + i, 1) for i in range(group)]
            lse = jnp.concatenate([lse_ref[h, cols] for h in heads], axis=1)
            delta = jnp.concatenate([delta_s[h, cols] for h in heads], axis=1)

            def tile(k, other, first, diagonal):
                q = qs[g, part]
                do = dos[g, part]
                s = dot_nt(ks[k, g, other], q)
                key = lax.broadcasted_iota(jnp.int32, s.shape, 0)
                visible = key >= start - first
                if diagonal:
                    query = thrice(lax.broadcasted_iota(jnp.int32, (half, half), 1))
                    visible = visible & (key <= query)
                p = jnp.where(visible, jnp.exp2(s - lse), 0.0)
                dv = dot_nn(low(p), do)
                dp = dot_nt(vs[k, g, other], do)
                ds = low(p * (dp - delta))
                dk_s[k, g, other] += dot_nn(ds, q)
                dv_s[k, g, other] += dv
                dq = dot_nn(kt[k, g, other], ds)
                if diagonal:
                    dqt_s[...] = dq
                else:
                    dqt_s[...] += dq

            tile(0, part, mine[part] * half, True)

            @pl.when(mine[1 - part] < mine[part])
            def _():
                tile(0, 1 - part, mine[1 - part] * half, False)

            def slot(k, carry):
                theirs = chunks_of(rank ^ k, slots)
                for other in range(2):

                    @pl.when(theirs[other] < mine[part])
                    def _():
                        tile(k, other, theirs[other] * half, False)

                return carry

            lax.fori_loop(1, slots, slot, 0)
            for i in range(group):
                dqt_all[g, i, :, cols] = dqt_s[:, i * half : (i + 1) * half]
        return carry

    lax.fori_loop(0, KV_HEADS, one_group, 0)
    dq_ref[...] = jnp.transpose(dqt_all[...].reshape(HEADS * HD, 2 * half)) * 0.125
    for k in range(slots):
        for part in range(2):
            dkv = jnp.concatenate(
                [dk_s[k, g, part] * (1.0 / log_two_e) for g in range(KV_HEADS)]
                + [dv_s[k, g, part] for g in range(KV_HEADS)],
                axis=1,
            )
            dkv_refs[k][part * half : (part + 1) * half] = dkv.astype(dkv_refs[k].dtype)


def attend_back(q, o, do, lse, start_row, kvs):
    block = q.shape[0]
    half = block // 2
    slots = len(kvs)
    group = HEADS // KV_HEADS
    inputs = (q, o, do, lse, start_row, *kvs)
    pair = lambda kind: like((block, 2 * KV_HEADS * HD), kind)

    def body(get, outs, extra):
        attend_back_kernel(slots, *[get(i) for i in range(len(inputs))], *outs, *extra)

    return run_kernel(
        body,
        inputs,
        (
            like((block, HEADS * HD), jnp.float32),
            pair(jnp.float32),
            *[pair(jnp.bfloat16)] * (slots - 1),
        ),
        scratch=(
            pltpu.VMEM((KV_HEADS, 2, group * half, HD), jnp.bfloat16),
            pltpu.VMEM((KV_HEADS, 2, group * half, HD), jnp.bfloat16),
            pltpu.VMEM((slots, KV_HEADS, 2, half, HD), jnp.bfloat16),
            pltpu.VMEM((slots, KV_HEADS, 2, HD, half), jnp.bfloat16),
            pltpu.VMEM((slots, KV_HEADS, 2, half, HD), jnp.bfloat16),
            pltpu.VMEM((slots, KV_HEADS, 2, half, HD), jnp.float32),
            pltpu.VMEM((slots, KV_HEADS, 2, half, HD), jnp.float32),
            pltpu.VMEM((HD, group * half), jnp.float32),
            pltpu.VMEM((16, block), jnp.float32),
            pltpu.VMEM((KV_HEADS, group, HD, block), jnp.float32),
        ),
        cost=20_000_000_000,
        name="attend_back",
    )


def scale_of(x):
    return lax.rsqrt(jnp.mean(x * x, axis=1, keepdims=True) + epsilon)


def tiled_lanes(table, columns):
    full = [table] * (columns // 128)
    if columns % 128:
        full.append(table[:, : columns % 128])
    return jnp.concatenate(full, axis=1)


def swapped(x):
    columns = x.shape[1]
    row = lax.broadcasted_iota(jnp.int32, (columns, columns), 0)
    col = lax.broadcasted_iota(jnp.int32, (columns, columns), 1)
    partner = jnp.where((col & (HD - 1)) < HD // 2, col + HD // 2, col - HD // 2)
    exchange = jnp.where(row == partner, 1.0, 0.0).astype(jnp.bfloat16)
    coarse = low(x)
    rest = x - wide(coarse)
    fine = low(rest)
    return dot_nn(coarse, exchange) + dot_nn(fine, exchange)


def turned(x, cosine, sine, sign):
    columns = x.shape[1]
    return x * tiled_lanes(cosine, columns) + swapped(x) * (sign * tiled_lanes(sine, columns))


QUERY = HEADS * HD
KVW = KV_HEADS * HD
QKV = QUERY + 2 * KVW


def project_in(hidden, gains, which, weights, cosine, sine):
    tokens, width = hidden.shape

    def body(get, outs, extra):
        normed_ref, q_ref, pair_ref = outs
        h = get(0)[...]
        normed = low(h * scale_of(h) * get(1)[which : which + 1])
        normed_ref[...] = normed
        out = dot_nn(normed, get(2)[:, :QKV])
        cos, sin = get(3)[...], get(4)[...]
        q_ref[...] = low(turned(out[:, :QUERY], cos, sin, 1.0) * (0.125 * log_two_e))
        keys = turned(out[:, QUERY : QUERY + KVW], cos, sin, 1.0)
        pair_ref[...] = low(jnp.concatenate([keys, out[:, QUERY + KVW :]], axis=1))

    return run_kernel(
        body,
        (hidden, gains, weights, cosine, sine),
        (
            like((tokens, width), jnp.bfloat16),
            like((tokens, QUERY), jnp.bfloat16),
            like((tokens, 2 * KVW), jnp.bfloat16),
        ),
        cost=4_000_000_000,
        name="project_in",
    )


def down_scratch(hidden):
    return (
        pltpu.VMEM((hidden, PIECE), jnp.bfloat16),
        pltpu.VMEM((hidden, PIECE // 2), jnp.bfloat16),
        pltpu.VMEM((hidden, PIECE // 2), jnp.float32),
    )


def open_down(down, left, right, wide_right):
    if len(down.shape) == 2:
        left[...] = down[:, :PIECE]
        right[...] = down[:, PIECE:]
        return
    shards, rows, columns = down.shape
    step = rows * 2 // 3
    for f in range(shards):
        for j in range(columns // PIECE):
            at = (f * (columns // PIECE) + j) * step
            lanes = slice(j * PIECE, (j + 1) * PIECE)
            left[at : at + step] = down[f, :step, lanes]
            rest = wide(down[f, step:, lanes])
            wide_right[at : at + step // 2] = rest[:, : PIECE // 2]
            wide_right[at + step // 2 : at + step] = rest[:, PIECE // 2 :]
    right[...] = low(wide_right[...])


def mlp(hidden, attention, gains, which, attn_weights, gate_w, up_w, down_w):
    tokens, width = hidden.shape
    ff = gate_w.shape[1]
    chunk = 512

    def body(get, outs, extra):
        middle_ref, mixed_ref, gate_ref, up_ref, inner_ref, out_ref = outs
        left, right, wide_right = extra
        middle = get(0)[...] + dot_nn(get(1)[...], get(3)[:, QKV:])
        middle_ref[...] = middle
        mixed = low(middle * scale_of(middle) * get(2)[which : which + 1])
        mixed_ref[...] = mixed
        open_down(get(6), left, right, wide_right)
        gate_weight, up_weight = get(4), get(5)
        sums = [0.0, 0.0]
        for c in range(ff // chunk):
            cols = slice(c * chunk, (c + 1) * chunk)
            gate = dot_nn(mixed, gate_weight[:, cols])
            up = dot_nn(mixed, up_weight[:, cols])
            gate_ref[:, cols] = low(gate)
            up_ref[:, cols] = low(up)
            inner = low(gate * jax.nn.sigmoid(gate) * up)
            inner_ref[:, cols] = inner
            sums[0] = sums[0] + dot_nn(inner, left[cols])
            sums[1] = sums[1] + dot_nn(inner, right[cols])
        out_ref[...] = middle + jnp.concatenate(sums, axis=1)

    return run_kernel(
        body,
        (hidden, attention, gains, attn_weights, gate_w, up_w, down_w),
        (
            like((tokens, width), jnp.float32),
            like((tokens, width), jnp.bfloat16),
            like((tokens, ff), jnp.bfloat16),
            like((tokens, ff), jnp.bfloat16),
            like((tokens, ff), jnp.bfloat16),
            like((tokens, width), jnp.float32),
        ),
        scratch=down_scratch(ff),
        cost=8_000_000_000,
        name="mlp",
    )


def norm_back(x, gain, grad):
    scale = scale_of(x)
    unit = x * scale
    e = grad * gain
    dx = scale * (e - unit * jnp.mean(e * unit, axis=1, keepdims=True))
    return dx, jnp.sum(grad * unit, axis=0, keepdims=True)


def put_rows(ref, index, value, shards):
    if shards is None:
        ref[index] = low(value)
        return
    rows = value.shape[0] // shards
    for f in range(shards):
        ref[f, index] = low(value[f * rows : (f + 1) * rows])


def mlp_back(grad, kept, gains, which, attn_weights, gate_w, up_w, down_w, shards):
    middle, mixed, gate, up, inner, attention = kept
    tokens, width = grad.shape
    ff = gate_w.shape[1]
    chunk = 512

    def body(get, outs, extra):
        datt_ref, mid_ref, gain_ref, out_grad_ref, weights_ref = outs[:5]
        left, right, wide_right, grad_s, total = extra
        open_down(get(11), left, right, wide_right)
        grad = get(0)[...]
        grad_low = low(grad)
        mixed = get(2)[...]
        d_mixed = 0.0
        for c in range(ff // chunk):
            cols = slice(c * chunk, (c + 1) * chunk)
            d_inner = dot_nt(grad_low[:, :PIECE], left[cols]) + dot_nt(
                grad_low[:, PIECE:], right[cols]
            )
            g = wide(get(3)[:, cols])
            sig = jax.nn.sigmoid(g)
            d_gate = low(d_inner * wide(get(4)[:, cols]) * (sig * (1.0 + g * (1.0 - sig))))
            d_up = low(d_inner * (g * sig))
            grad_s[0, :, cols] = dot_tn(mixed, d_gate)
            grad_s[1, :, cols] = dot_tn(mixed, d_up)
            part = dot_nt(d_gate, get(9)[:, cols]) + dot_nt(d_up, get(10)[:, cols])
            d_mixed = part + d_mixed
            d_down = dot_tn(get(5)[:, cols], grad_low)
            if shards is None:
                outs[5][cols] = low(d_down)
            else:
                total[cols] = d_down
        for index in range(2):
            put_rows(weights_ref, index, grad_s[index], shards)
        if shards is not None:
            rows = width // shards
            step = rows * 2 // 3
            for f in range(shards):
                for j in range(ff // PIECE):
                    at = (f * (ff // PIECE) + j) * step
                    rest = total[at : at + step, PIECE:]
                    value = jnp.concatenate(
                        [
                            total[at : at + step, :PIECE],
                            jnp.concatenate([rest[: step // 2], rest[step // 2 :]], axis=1),
                        ],
                        axis=0,
                    )
                    weights_ref[f, 2, :, j * PIECE : (j + 1) * PIECE] = low(value)
        dx, gain_grad = norm_back(get(1)[...], get(7)[which : which + 1], d_mixed)
        gain_ref[...] = jnp.broadcast_to(gain_grad, gain_ref.shape)
        mid = grad + dx
        mid_ref[...] = mid
        mid_low = low(mid)
        out_grad_ref[...] = low(dot_tn(get(6)[...], mid_low))
        datt_ref[...] = low(dot_nt(mid_low, get(8)[:, QKV:]))

    if shards is None:
        weight_outs = (like((2, width, ff), jnp.bfloat16), like((ff, width), jnp.bfloat16))
    else:
        weight_outs = (like((shards, 3, width // shards, ff), jnp.bfloat16),)
    return run_kernel(
        body,
        (
            grad, middle, mixed, gate, up, inner, attention, gains,
            attn_weights, gate_w, up_w, down_w,
        ),
        (
            like((tokens, width), jnp.bfloat16),
            like((tokens, width), jnp.float32),
            like((8, width), jnp.float32),
            like((width, width), jnp.bfloat16),
            *weight_outs,
        ),
        scratch=(
            *down_scratch(ff),
            pltpu.VMEM((2, width, ff), jnp.float32),
            pltpu.VMEM((ff, width), jnp.float32),
        ),
        cost=15_000_000_000,
        name="mlp_back",
    )


def project_back(d_query, pairs, cosine, sine, kept, gains, which, weights, out_grad, mid, shards, riders):
    hidden, normed = kept
    tokens, width = hidden.shape
    count = len(pairs)
    columns = weights.shape[1]
    extra_rows = 0 if riders is None else 8

    def body(get, outs, extra):
        grad_ref, gain_ref, weights_ref = outs
        cos, sin = get(1)[...], get(2)[...]
        dq = turned(get(0)[...], cos, sin, -1.0)
        pair = get(9)[...]
        for k in range(1, count):
            pair = pair + wide(get(9 + k)[...])
        dk = turned(pair[:, :KVW], cos, sin, -1.0)
        d_all = low(jnp.concatenate([dq, dk, pair[:, KVW:]], axis=1))
        normed_grad = dot_nt(d_all, get(6)[:, :QKV])
        dx, gain_grad = norm_back(get(3)[...], get(5)[which : which + 1], normed_grad)
        gain_ref[...] = jnp.broadcast_to(gain_grad, gain_ref.shape)
        grad_ref[...] = get(8)[...] + dx
        d_weights = dot_tn(get(4)[...], d_all)
        value = jnp.concatenate([d_weights, wide(get(7)[...])], axis=1)
        if riders is None:
            put_rows(weights_ref, 0, value, shards)
        else:
            rows = width // shards
            lines = [get(9 + count)[...], gain_grad]
            lines.append(jnp.zeros((8 - 1 - lines[0].shape[0], width), jnp.float32))
            ride = jnp.concatenate(lines, axis=0)
            ride = jnp.concatenate(
                [ride, jnp.zeros((8, columns - width), jnp.float32)], axis=1
            )
            for f in range(shards):
                weights_ref[f, 0] = low(
                    jnp.concatenate([value[f * rows : (f + 1) * rows], ride], axis=0)
                )

    if shards is None:
        shape = (1, width, columns)
    else:
        shape = (shards, 1, width // shards + extra_rows, columns)
    inputs = (d_query, cosine, sine, hidden, normed, gains, weights, out_grad, mid, *pairs)
    if riders is not None:
        inputs = (*inputs, riders)
    return run_kernel(
        body,
        inputs,
        (
            like((tokens, width), jnp.float32),
            like((8, width), jnp.float32),
            like(shape, jnp.bfloat16),
        ),
        cost=6_000_000_000,
        name="project_back",
    )


def rope_tables(positions, head_size):
    half = head_size // 2
    freq = theta ** (-(jnp.arange(half, dtype=jnp.float32) * 2.0 / head_size))
    angle = positions.astype(jnp.float32)[..., None] * freq
    return (jnp.cos(angle), jnp.sin(angle))


def body(
    tokens,
    positions,
    query_weight,
    key_matrix,
    value_weight,
    out_weight,
    gate_weight,
    up_weight,
    down_weight,
    attn_gain,
    mlp_gain,
    cotangent,
):
    slots = lax.axis_size("ctx")
    rank = lax.axis_index("ctx")
    shard = lax.axis_index("fsdp")
    shards = lax.axis_size("fsdp")
    fast = slots == 4 and shards == 8
    tokens = swap_halves(tokens)
    positions = swap_halves(positions)
    half = tokens.shape[1] // 2
    rows = attn_gain.shape[1]
    gain_count = 2 * LAYERS
    own_gains = jnp.concatenate([attn_gain, mlp_gain])
    attn_own = [
        jnp.concatenate([query_weight[i], key_matrix[i], value_weight[i], out_weight[i]], axis=1)
        for i in range(LAYERS)
    ]
    mlp_own = [[gate_weight[i], up_weight[i]] for i in range(LAYERS)]
    if fast:
        for i in range(LAYERS):
            mlp_own[i].append(fold_down(down_weight[i]))
        ride = jnp.pad(own_gains, ((0, 8 - gain_count), (0, PIECE - rows)))
        own_first = jnp.concatenate([attn_own[0], jnp.tile(ride, (1, 4))], axis=0)[None]
        own_second = jnp.stack([*mlp_own[0], attn_own[1]])
        own_third = jnp.stack(mlp_own[1])
        first_line = gather_line(own_first)
        second_line = gather_line(tied(own_second, first_line))
        third = gather_plain(tied(own_third, second_line))
        third = third.reshape(3, shards, rows, -1)
        first_sides = gather_sides(first_line)
        first_flip = flip(own_first, "fsdp", 1)
        (first, gains), first_mine = gather_rest(
            rows, own_first, first_flip, first_line, first_sides
        )
        gains = wide(gains[:, :gain_count, :rows]).transpose(1, 0, 2).reshape(gain_count, -1)
        second_flip = flip(tied(own_second, first_mine), "fsdp", 1)
        second_line = tied(second_line, first_mine)
        second_sides = gather_sides(second_line)
        merge = lambda x: x.reshape(-1, x.shape[-1])
        attn_full = [merge(first[0]), None]
        mlp_full = [None, (merge(third[0]), merge(third[1]), third[2])]
    else:
        gains = wide(lax.all_gather(own_gains, "fsdp", axis=1, tiled=True))
        gather = lambda x: lax.all_gather(x, "fsdp", axis=0, tiled=True)
        attn_full = [gather(x) for x in attn_own]
        mlp_full = [
            (gather(gate_weight[i]), gather(up_weight[i]), gather(down_weight[i]))
            for i in range(LAYERS)
        ]
    gains = jnp.pad(gains, ((0, 8 - gain_count), (0, 0)))
    cosine, sine = rope_tables(positions[0], HD)
    cosine = jnp.concatenate([cosine] * 4, axis=1)
    sine = jnp.concatenate([-sine, sine] * 2, axis=1)
    first_row, second_row = chunks_of(rank, slots)
    offsets = jnp.arange(half, dtype=jnp.int32)
    row_index = jnp.concatenate([first_row * half + offsets, second_row * half + offsets])
    doc_start = row_index[None, :] - positions

    hidden = wide(tokens[0])
    saved = []
    for i in range(LAYERS):
        normed, q, pair = project_in(hidden, gains, i, attn_full[i], cosine, sine)
        kvs = [pair] + [flip(pair, "ctx", k) for k in range(1, slots)]
        attention, lse = attend(q, doc_start, kvs)
        if fast and i == 0:
            second_sides, cotangent = tied((second_sides, cotangent), attention)
            (second,), _ = gather_rest(
                rows, own_second, second_flip, second_line, second_sides
            )
            mlp_full[0] = (merge(second[0]), merge(second[1]), second[2])
            attn_full[1] = merge(second[3])
        middle, mixed, gate, up, inner, out = mlp(
            hidden, attention, gains, LAYERS + i, attn_full[i], *mlp_full[i]
        )
        saved.append((hidden, normed, q, kvs, attention, lse, middle, mixed, gate, up, inner))
        hidden = out
    layer_out = swap_halves(low(hidden)[None])
    grad = wide(swap_halves(cotangent)[0])

    gain_grads = {}
    mlp_grads = [None] * LAYERS
    attn_grads = [None] * LAYERS
    by_shard = shards if fast else None
    for i in reversed(range(LAYERS)):
        hidden, normed, q, kvs, attention, lse, middle, mixed, gate, up, inner = saved[i]
        d_attention, mid, gain_grads[LAYERS + i], out_grad, *weight_grads = mlp_back(
            grad,
            (middle, mixed, gate, up, inner, attention),
            gains,
            LAYERS + i,
            attn_full[i],
            *mlp_full[i],
            by_shard,
        )
        if fast and i == 0:
            sums, sends = reduce_begin(weight_grads[0])
            d_attention, sends, pieces = lax.optimization_barrier(
                (d_attention, sends, mlp_grads[1])
            )
            sides = reduce_sides(sends)
            moved = [pieces[0]] + [flip(pieces[k], "ctx", k) for k in (1, 2, 3)]
        elif fast:
            mlp_grads[i] = line_pieces(weight_grads[0])
        else:
            mlp_grads[i] = (
                reduce_plain(weight_grads[0], 1),
                reduce_plain(weight_grads[1], 0),
            )
        d_query, *pairs = attend_back(q, attention, d_attention, lse, doc_start, kvs)
        pairs = [pairs[0]] + [flip(pairs[k], "ctx", k) for k in range(1, slots)]
        riders = None
        if fast and i == 0:
            riders = jnp.concatenate([gain_grads[v][:1] for v in (1, 2, 3)])
        grad, gain_grads[i], attn_grad = project_back(
            d_query,
            pairs,
            cosine,
            sine,
            (hidden, normed),
            gains,
            i,
            attn_full[i],
            out_grad,
            mid,
            by_shard,
            riders,
        )
        if fast and i == 0:
            sides, moved, pieces = tied((sides, moved, attn_grads[1]), pairs)
            mlp_sum = sum((wide(part) for part in moved[1:]), wide(moved[0]))
            early = jnp.concatenate([mlp_sum, line_sum(pieces)])
            early = spread_fast(early)
            rest = spread_fast(reduce_end(sums, sides))
            sums, sends = reduce_begin(attn_grad)
            last = reduce_end(sums, reduce_sides(sends))
            last = spread_fast(last)
            all_gains = lax.dynamic_slice_in_dim(last[0, rows:], shard * rows, rows, axis=1)
            order = (3, 0, 1, 2)
            all_gains = jnp.stack([all_gains[v] for v in order])
            attn_rows = jnp.stack([last[0, :rows], early[3]])
            gate_rows = jnp.stack([rest[0], early[0]])
            up_rows = jnp.stack([rest[1], early[1]])
            down_rows = unfold_down(jnp.stack([rest[2], early[2]]))
        elif fast:
            attn_grads[i] = line_pieces(attn_grad)
        else:
            attn_grads[i] = reduce_plain(attn_grad[0], 0)
    if not fast:
        attn_rows = jnp.stack(attn_grads)
        gate_rows = jnp.stack([part[0][0] for part in mlp_grads])
        up_rows = jnp.stack([part[0][1] for part in mlp_grads])
        down_rows = jnp.stack([part[1] for part in mlp_grads])
        all_gains = jnp.concatenate([gain_grads[v][:1] for v in range(gain_count)])
        all_gains = lax.psum(all_gains, ("ctx", "fsdp"))
        all_gains = lax.dynamic_slice_in_dim(all_gains, shard * rows, rows, axis=1)
    far = wide(flip(low(grad[half:]), "ctx", slots - 1))
    grad = jnp.concatenate([grad[:half], far])[None]
    return (
        layer_out,
        grad,
        attn_rows[..., :QUERY],
        attn_rows[..., QUERY : QUERY + KVW],
        attn_rows[..., QUERY + KVW : QKV],
        attn_rows[..., QKV:],
        gate_rows,
        up_rows,
        down_rows,
        all_gains[:LAYERS],
        all_gains[LAYERS:],
    )


def solution(mesh):
    return jax.shard_map(
        body,
        mesh=mesh,
        in_specs=(
            P("fsdp", "ctx", None),
            P("fsdp", "ctx"),
            P(None, "fsdp", None),
            P(None, "fsdp", None),
            P(None, "fsdp", None),
            P(None, "fsdp", None),
            P(None, "fsdp", None),
            P(None, "fsdp", None),
            P(None, "fsdp", None),
            P(None, "fsdp"),
            P(None, "fsdp"),
            P("fsdp", "ctx", None),
        ),
        out_specs=(
            P("fsdp", "ctx", None),
            P("fsdp", "ctx", None),
            P(None, "fsdp", None),
            P(None, "fsdp", None),
            P(None, "fsdp", None),
            P(None, "fsdp", None),
            P(None, "fsdp", None),
            P(None, "fsdp", None),
            P(None, "fsdp", None),
            P(None, "fsdp"),
            P(None, "fsdp"),
        ),
        check_vma=False,
    )
```

```python
import jax
import jax.numpy as jnp
from jax import lax
from jax.experimental import pallas as pl
from jax.experimental.pallas import tpu as pltpu
from jax.sharding import PartitionSpec as P

HEADS = 9
KV_HEADS = 3
HD = 64
LAYERS = 2


epsilon = 1e-05
theta = 100000.0
log_two_e = 1.4426950408889634
mask_filler = -1e30


def flip(block, axis, mask):
    route = [(i, i ^ mask) for i in range(lax.axis_size(axis))]
    return lax.ppermute(block, axis, route)


def swap_halves(x):
    half = x.shape[1] // 2
    return jnp.concatenate(
        [x[:, :half], flip(x[:, half:], "ctx", lax.axis_size("ctx") - 1)], axis=1
    )


def tied(first, *then):
    return lax.optimization_barrier((first, then))[0]


def low(x):
    return x.astype(jnp.bfloat16)


def wide(x):
    return x.astype(jnp.float32)


PIECE = 384
VMEM_LIMIT = 48 * 1024 * 1024


def fold_down(shard):
    step = shard.shape[0] // 4
    pieces = []
    for j in range(4):
        rows = shard[j * step : (j + 1) * step]
        rest = rows[:, PIECE:]
        rest = jnp.concatenate([rest[: step // 2], rest[step // 2 :]], axis=1)
        pieces.append(jnp.concatenate([rows[:, :PIECE], rest], axis=0))
    return jnp.concatenate(pieces, axis=1)


def unfold_down(folded):
    step = folded.shape[-2] * 2 // 3
    pieces = []
    for piece in jnp.split(folded, 4, axis=-1):
        rest = piece[..., step:, :]
        rest = jnp.concatenate(jnp.split(rest, 2, axis=-1), axis=-2)
        pieces.append(jnp.concatenate([piece[..., :step, :], rest], axis=-1))
    return jnp.concatenate(pieces, axis=-2)


def assemble_kernel(rows, own, own_flip, mine, theirs, out, *rest):
    sems = rest[-1]
    j = lax.axis_index("ctx")
    f = lax.axis_index("fsdp")
    copies = []

    def copy(src, dst):
        made = pltpu.make_async_copy(src, dst, sems.at[len(copies)])
        made.start()
        copies.append(made)

    for core, shard in ((0, own), (1, own_flip)):
        copy(shard.at[:, :rows], out.at[:, f ^ core])
        if len(rest) > 1:
            copy(shard.at[0, rows:, :PIECE], rest[0].at[f ^ core])
    for core, pieces in ((0, mine), (1, theirs)):
        for jrel in range(4):
            for zrel in range(1, 4):
                row = f ^ (core + 2 * zrel)
                column = pl.multiple_of((j ^ jrel) * PIECE, 128)
                piece = pieces.at[jrel * 3 + zrel - 1]
                copy(piece.at[:, :rows], out.at[:, row, :, pl.ds(column, PIECE)])
                if jrel == 0 and len(rest) > 1:
                    copy(piece.at[0, rows:], rest[0].at[row])
    for made in copies:
        made.wait()


def assemble(rows, own, own_flip, mine, theirs):
    count, all_rows, columns = own.shape
    fsdp = lax.axis_size("fsdp")
    shapes = [jax.ShapeDtypeStruct((count, fsdp, rows, columns), own.dtype)]
    if all_rows > rows:
        shapes.append(jax.ShapeDtypeStruct((fsdp, all_rows - rows, PIECE), own.dtype))
    return pl.pallas_call(
        lambda *refs: assemble_kernel(rows, *refs),
        out_shape=tuple(shapes),
        in_specs=[pl.BlockSpec(memory_space=pl.ANY)] * 4,
        out_specs=[pl.BlockSpec(memory_space=pltpu.VMEM)] * len(shapes),
        scratch_shapes=[pltpu.SemaphoreType.DMA((34,))],
        compiler_params=pltpu.CompilerParams(vmem_limit_bytes=VMEM_LIMIT),
        name="assemble",
    )(own, own_flip, mine, theirs)


def gather_line(own):
    j = lax.axis_index("ctx")
    piece = lax.dynamic_slice_in_dim(own, j * PIECE, PIECE, axis=2)
    return jnp.stack([flip(piece, "fsdp", 2 * k) for k in (1, 2, 3)])


def gather_sides(line):
    return flip(line, "ctx", 1), flip(line, "ctx", 2)


def gather_rest(rows, own, own_flip, line, sides):
    by_x, by_y = sides
    diag = jnp.concatenate([flip(by_x[:2], "ctx", 2), flip(by_y[2:], "ctx", 1)])
    mine = jnp.concatenate([line, by_x, by_y, diag])
    theirs = flip(mine, "fsdp", 1)
    return assemble(rows, own, own_flip, mine, theirs), mine


def gather_plain(own):
    return lax.all_gather(own, "fsdp", axis=1, tiled=True)


def scatter_kernel(count, *refs):
    wholes, (keep, send, sems) = refs[:count], refs[count:]
    j = lax.axis_index("ctx")
    f = lax.axis_index("fsdp")
    copies = []
    for core, pieces in ((0, keep), (1, send)):
        for jrel in range(4):
            for zrel in range(4):
                row = (f ^ (core + 2 * zrel)) * 4 + (j ^ jrel)
                at = 0
                for whole in wholes:
                    made = pltpu.make_async_copy(
                        whole.at[row],
                        pieces.at[jrel, zrel, at : at + whole.shape[1]],
                        sems.at[len(copies)],
                    )
                    made.start()
                    copies.append(made)
                    at += whole.shape[1]
    for made in copies:
        made.wait()


def cut(wholes):
    rows = wholes[0].shape[2]
    total = sum(whole.shape[1] for whole in wholes)
    piece = jax.ShapeDtypeStruct((4, 4, total, rows, PIECE), wholes[0].dtype)
    return pl.pallas_call(
        lambda *refs: scatter_kernel(len(wholes), *refs),
        out_shape=(piece, piece),
        in_specs=[pl.BlockSpec(memory_space=pltpu.VMEM)] * len(wholes),
        out_specs=[pl.BlockSpec(memory_space=pl.ANY)] * 2,
        scratch_shapes=[pltpu.SemaphoreType.DMA((32 * len(wholes),))],
        compiler_params=pltpu.CompilerParams(vmem_limit_bytes=VMEM_LIMIT),
        name="cut",
    )(*wholes)


def reduce_begin(*wholes):
    keep, send = cut(wholes)
    other = flip(send, "fsdp", 1)
    total = wide(keep) + wide(other)
    a = low(total[:, :2])
    b = low(total[:, 2:])
    return (a[0], a[2], b[0], b[1]), (jnp.stack([a[1], a[3]]), jnp.stack([b[2], b[3]]))


def reduce_sides(sends):
    return flip(sends[0], "ctx", 1), flip(sends[1], "ctx", 2)


def reduce_middle(sums, sides):
    a0, a2, b0, b1 = (wide(part) for part in sums)
    x1, y1 = wide(sides[0]), wide(sides[1])
    return (a0 + x1[0], b0 + y1[0]), (low(a2 + x1[1]), low(b1 + y1[1]))


def reduce_across(sends):
    return flip(sends[0], "ctx", 2), flip(sends[1], "ctx", 1)


def reduce_turn(sums, across):
    a0 = sums[0] + wide(across[0])
    b0 = sums[1] + wide(across[1])
    return a0[0], (low(a0[1]), low(b0[0]), low(b0[1]))


def reduce_line(sends):
    return [flip(part, "fsdp", 2 * k + 2) for k, part in enumerate(sends)]


def reduce_end(line):
    return line[0] + sum(wide(part) for part in line[1:])


def spread_fast(piece):
    j = lax.axis_index("ctx")
    own = low(piece)
    parts = [own] + [flip(own, "ctx", k) for k in (1, 2, 3)]
    for bit in (1, 2):
        odd = (j & bit) != 0
        parts = [jnp.where(odd, parts[i ^ bit], parts[i]) for i in range(4)]
    return wide(jnp.concatenate(parts, axis=2))


def reduce_plain(whole, dim):
    part = lax.psum_scatter(whole, "fsdp", scatter_dimension=dim, tiled=True)
    return wide(lax.psum(part, "ctx"))


def dot_nn(a, b):
    return jnp.dot(a, b, preferred_element_type=jnp.float32)


def dot_nt(a, b):
    return lax.dot_general(a, b, (((1,), (1,)), ((), ())), preferred_element_type=jnp.float32)


def dot_tn(a, b):
    return lax.dot_general(a, b, (((0,), (0,)), ((), ())), preferred_element_type=jnp.float32)


def shape_of(x):
    return x[0].shape[1:] if isinstance(x, tuple) else x.shape


def run_kernel(body, inputs, outputs, scratch=(), cost=0, name=None):
    count = len(inputs)
    arrays = [x[0] if isinstance(x, tuple) else x for x in inputs]

    def kernel(*refs):
        sources = refs[:count]
        outs = refs[count : count + len(outputs)]
        rest = refs[count + len(outputs) :]
        buffers, extra, sems = rest[:count], rest[count:-1], rest[-1]
        copies = [
            pltpu.make_async_copy(
                source.at[x[1]] if isinstance(x, tuple) else source, buffer, sems.at[i]
            )
            for i, (x, source, buffer) in enumerate(zip(inputs, sources, buffers))
        ]
        for copy in copies:
            copy.start()
        waited = set()

        def get(i):
            if i not in waited:
                waited.add(i)
                copies[i].wait()
            return buffers[i]

        body(get, outs, extra)
        for i in range(count):
            get(i)

    return pl.pallas_call(
        kernel,
        out_shape=tuple(outputs),
        in_specs=[pl.BlockSpec(memory_space=pl.ANY)] * count,
        out_specs=[pl.BlockSpec(memory_space=pltpu.VMEM)] * len(outputs),
        scratch_shapes=[
            *[pltpu.VMEM(shape_of(x), array.dtype) for x, array in zip(inputs, arrays)],
            *scratch,
            pltpu.SemaphoreType.DMA((count,)),
        ],
        compiler_params=pltpu.CompilerParams(vmem_limit_bytes=VMEM_LIMIT),
        cost_estimate=pl.CostEstimate(flops=cost, bytes_accessed=4_000_000, transcendentals=0),
        name=name,
    )(*arrays)


def like(shape, kind):
    return jax.ShapeDtypeStruct(shape, kind)


def chunks_of(source, slots):
    return (2 * source, 2 * slots - 1 - 2 * source)


def stack_heads(ref, dst, half, groups=range(KV_HEADS)):
    group = HEADS // KV_HEADS
    for g in groups:
        for part in range(2):
            for i in range(group):
                h = g * group + i
                dst[g, part, i * half : (i + 1) * half] = ref[
                    part * half : (part + 1) * half, h * HD : (h + 1) * HD
                ]


def thrice(row):
    return jnp.concatenate([row] * (HEADS // KV_HEADS), axis=1)


def attend_kernel(slots, *refs):
    q_ref, start_ref = refs[:2]
    kv_refs = refs[2 : 2 + slots]
    o_ref, lse_ref, qs, ks, vt, top_s, acc_s, ot = refs[2 + slots :]
    rank = lax.axis_index("ctx")
    half = q_ref.shape[0] // 2
    group = HEADS // KV_HEADS
    wide_cols = group * half
    stack_heads(q_ref, qs, half)
    ones = jnp.ones((16, half), jnp.bfloat16)
    for k in range(slots):
        values_t = low(jnp.transpose(wide(kv_refs[k][:, 128:])))
        for g in range(KV_HEADS):
            row = KV_HEADS * HD - 128 + g * HD
            for part in range(2):
                rows = slice(part * half, (part + 1) * half)
                ks[k, g, part] = kv_refs[k][rows, g * HD : (g + 1) * HD]
                vt[k, g, part, :HD] = values_t[row : row + HD, rows]
                vt[k, g, part, HD:] = ones
    lse_ref[...] = jnp.zeros_like(lse_ref)
    mine = chunks_of(rank, slots)

    def one_group(g, carry):
        for part in range(2):
            cols = slice(part * half, (part + 1) * half)
            start = thrice(start_ref[:, cols])
            q = qs[g, part]

            def scores(k, other, first):
                s = dot_nt(ks[k, g, other], q)
                key = lax.broadcasted_iota(jnp.int32, s.shape, 0)
                visible = key >= start - first
                return s, key, visible

            s, key, visible = scores(0, part, mine[part] * half)
            query = thrice(lax.broadcasted_iota(jnp.int32, (half, half), 1))
            s = jnp.where(visible & (key <= query), s, mask_filler)
            top = jnp.floor(jnp.max(s, axis=0, keepdims=True))
            top_s[...] = top
            acc_s[...] = dot_nn(vt[0, g, part], low(jnp.exp2(s - top)))

            def tile(k, other, chunk):
                @pl.when(chunk < mine[part])
                def _():
                    s, _, visible = scores(k, other, chunk * half)
                    s = jnp.where(visible, s, mask_filler)
                    old = top_s[...]
                    top = jnp.maximum(old, jnp.floor(jnp.max(s, axis=0, keepdims=True)))
                    top_s[...] = top
                    acc_s[...] = acc_s[...] * jnp.exp2(old - top) + dot_nn(
                        vt[k, g, other], low(jnp.exp2(s - top))
                    )

            tile(0, 1 - part, mine[1 - part])

            def slot(k, carry):
                theirs = chunks_of(rank ^ k, slots)
                for other in range(2):
                    tile(k, other, theirs[other])
                return carry

            lax.fori_loop(1, slots, slot, 0)
            total = acc_s[HD : HD + 1]
            out = acc_s[:HD] / total
            level = top_s[...] + jnp.log2(total)
            for i in range(group):
                inner = slice(i * half, (i + 1) * half)
                ot[g, i, :, cols] = out[:, inner]
                lse_ref[pl.ds(g * group + i, 1), cols] = level[:, inner]
        return carry

    lax.fori_loop(0, KV_HEADS, one_group, 0)
    o_ref[...] = low(jnp.transpose(ot[...].reshape(HEADS * HD, 2 * half)))


def attend(q, start, kvs):
    block = q.shape[0]
    half = block // 2
    slots = len(kvs)
    group = HEADS // KV_HEADS
    inputs = (q, start, *kvs)

    def body(get, outs, extra):
        attend_kernel(slots, *[get(i) for i in range(len(inputs))], *outs, *extra)

    return run_kernel(
        body,
        inputs,
        (like((block, HEADS * HD), jnp.bfloat16), like((16, block), jnp.float32)),
        scratch=(
            pltpu.VMEM((KV_HEADS, 2, group * half, HD), jnp.bfloat16),
            pltpu.VMEM((slots, KV_HEADS, 2, half, HD), jnp.bfloat16),
            pltpu.VMEM((slots, KV_HEADS, 2, HD + 16, half), jnp.bfloat16),
            pltpu.VMEM((1, group * half), jnp.float32),
            pltpu.VMEM((HD + 16, group * half), jnp.float32),
            pltpu.VMEM((KV_HEADS, group, HD, block), jnp.float32),
        ),
        cost=15_000_000_000,
        name="attend",
    )


def attend_back_kernel(slots, groups, *refs):
    q_ref, o_ref, do_ref, lse_ref, start_ref = refs[:5]
    kv_refs = refs[5 : 5 + slots]
    dq_ref = refs[5 + slots]
    dkv_refs = refs[6 + slots : 6 + 2 * slots]
    qs, dos, ks, kt, vs, dk_s, dv_s, dqt_s, delta_s, dqt_all = refs[6 + 2 * slots :]
    rank = lax.axis_index("ctx")
    half = q_ref.shape[0] // 2
    group = HEADS // KV_HEADS
    stack_heads(q_ref, qs, half, groups)
    stack_heads(do_ref, dos, half, groups)
    for k in range(slots):
        keys_t = low(jnp.transpose(wide(kv_refs[k][:, : 2 * 128])))
        for g in groups:
            for part in range(2):
                rows = slice(part * half, (part + 1) * half)
                ks[k, g, part] = kv_refs[k][rows, g * HD : (g + 1) * HD]
                kt[k, g, part] = keys_t[g * HD : (g + 1) * HD, rows]
                vs[k, g, part] = kv_refs[k][rows, (KV_HEADS + g) * HD : (KV_HEADS + g + 1) * HD]
    product = wide(do_ref[...]) * wide(o_ref[...])
    coarse = low(product)
    fine = low(product - wide(coarse))
    shape = (16, HEADS * HD)
    owner = lax.div(lax.broadcasted_iota(jnp.int32, shape, 1), HD)
    pick = jnp.where(owner == lax.broadcasted_iota(jnp.int32, shape, 0), 1.0, 0.0)
    pick = pick.astype(jnp.bfloat16)
    delta_s[...] = dot_nt(pick, coarse) + dot_nt(pick, fine)
    dk_s[...] = jnp.zeros_like(dk_s)
    dv_s[...] = jnp.zeros_like(dv_s)
    mine = chunks_of(rank, slots)

    def one_group(g, carry):
        for part in range(2):
            cols = slice(part * half, (part + 1) * half)
            start = thrice(start_ref[:, cols])
            heads = [pl.ds(g * group + i, 1) for i in range(group)]
            lse = jnp.concatenate([lse_ref[h, cols] for h in heads], axis=1)
            delta = jnp.concatenate([delta_s[h, cols] for h in heads], axis=1)

            def tile(k, other, first, diagonal):
                q = qs[g, part]
                do = dos[g, part]
                s = dot_nt(ks[k, g, other], q)
                key = lax.broadcasted_iota(jnp.int32, s.shape, 0)
                visible = key >= start - first
                if diagonal:
                    query = thrice(lax.broadcasted_iota(jnp.int32, (half, half), 1))
                    visible = visible & (key <= query)
                p = jnp.where(visible, jnp.exp2(s - lse), 0.0)
                dv = dot_nn(low(p), do)
                dp = dot_nt(vs[k, g, other], do)
                ds = low(p * (dp - delta))
                dk_s[k, g, other] += dot_nn(ds, q)
                dv_s[k, g, other] += dv
                dq = dot_nn(kt[k, g, other], ds)
                if diagonal:
                    dqt_s[...] = dq
                else:
                    dqt_s[...] += dq

            tile(0, part, mine[part] * half, True)

            @pl.when(mine[1 - part] < mine[part])
            def _():
                tile(0, 1 - part, mine[1 - part] * half, False)

            def slot(k, carry):
                theirs = chunks_of(rank ^ k, slots)
                for other in range(2):

                    @pl.when(theirs[other] < mine[part])
                    def _():
                        tile(k, other, theirs[other] * half, False)

                return carry

            lax.fori_loop(1, slots, slot, 0)
            for i in range(group):
                dqt_all[g, i, :, cols] = dqt_s[:, i * half : (i + 1) * half]
        return carry

    lax.fori_loop(groups.start, groups.stop, one_group, 0)
    dqt = dqt_all[groups.start : groups.stop]
    dq_ref[...] = jnp.transpose(dqt.reshape(len(groups) * group * HD, 2 * half)) * 0.125
    for k in range(slots):
        for part in range(2):
            dkv = jnp.concatenate(
                [
                    x
                    for g in groups
                    for x in (dk_s[k, g, part] * (1.0 / log_two_e), dv_s[k, g, part])
                ],
                axis=1,
            )
            dkv_refs[k][part * half : (part + 1) * half] = dkv.astype(dkv_refs[k].dtype)


def attend_back(q, o, do, lse, start_row, kvs, groups):
    block = q.shape[0]
    half = block // 2
    slots = len(kvs)
    group = HEADS // KV_HEADS
    inputs = (q, o, do, lse, start_row, *kvs)
    pair = lambda kind: like((block, 2 * len(groups) * HD), kind)

    def body(get, outs, extra):
        attend_back_kernel(slots, groups, *[get(i) for i in range(len(inputs))], *outs, *extra)

    return run_kernel(
        body,
        inputs,
        (
            like((block, len(groups) * group * HD), jnp.float32),
            pair(jnp.float32),
            *[pair(jnp.bfloat16)] * (slots - 1),
        ),
        scratch=(
            pltpu.VMEM((KV_HEADS, 2, group * half, HD), jnp.bfloat16),
            pltpu.VMEM((KV_HEADS, 2, group * half, HD), jnp.bfloat16),
            pltpu.VMEM((slots, KV_HEADS, 2, half, HD), jnp.bfloat16),
            pltpu.VMEM((slots, KV_HEADS, 2, HD, half), jnp.bfloat16),
            pltpu.VMEM((slots, KV_HEADS, 2, half, HD), jnp.bfloat16),
            pltpu.VMEM((slots, KV_HEADS, 2, half, HD), jnp.float32),
            pltpu.VMEM((slots, KV_HEADS, 2, half, HD), jnp.float32),
            pltpu.VMEM((HD, group * half), jnp.float32),
            pltpu.VMEM((16, block), jnp.float32),
            pltpu.VMEM((KV_HEADS, group, HD, block), jnp.float32),
        ),
        cost=7_000_000_000 * len(groups),
        name="attend_back",
    )


def scale_of(x):
    return lax.rsqrt(jnp.mean(x * x, axis=1, keepdims=True) + epsilon)


def tiled_lanes(table, columns):
    full = [table] * (columns // 128)
    if columns % 128:
        full.append(table[:, : columns % 128])
    return jnp.concatenate(full, axis=1)


def swapped(x):
    columns = x.shape[1]
    row = lax.broadcasted_iota(jnp.int32, (columns, columns), 0)
    col = lax.broadcasted_iota(jnp.int32, (columns, columns), 1)
    partner = jnp.where((col & (HD - 1)) < HD // 2, col + HD // 2, col - HD // 2)
    exchange = jnp.where(row == partner, 1.0, 0.0).astype(jnp.bfloat16)
    coarse = low(x)
    rest = x - wide(coarse)
    fine = low(rest)
    return dot_nn(coarse, exchange) + dot_nn(fine, exchange)


def turned(x, cosine, sine, sign):
    columns = x.shape[1]
    return x * tiled_lanes(cosine, columns) + swapped(x) * (sign * tiled_lanes(sine, columns))


QUERY = HEADS * HD
KVW = KV_HEADS * HD
QKV = QUERY + 2 * KVW


def project_in(hidden, gains, which, weights, cosine, sine):
    tokens, width = hidden.shape

    def body(get, outs, extra):
        normed_ref, q_ref, pair_ref = outs
        h = get(0)[...]
        normed = low(h * scale_of(h) * get(1)[which : which + 1])
        normed_ref[...] = normed
        out = dot_nn(normed, get(2)[:, :QKV])
        cos, sin = get(3)[...], get(4)[...]
        q_ref[...] = low(turned(out[:, :QUERY], cos, sin, 1.0) * (0.125 * log_two_e))
        keys = turned(out[:, QUERY : QUERY + KVW], cos, sin, 1.0)
        pair_ref[...] = low(jnp.concatenate([keys, out[:, QUERY + KVW :]], axis=1))

    return run_kernel(
        body,
        (hidden, gains, weights, cosine, sine),
        (
            like((tokens, width), jnp.bfloat16),
            like((tokens, QUERY), jnp.bfloat16),
            like((tokens, 2 * KVW), jnp.bfloat16),
        ),
        cost=4_000_000_000,
        name="project_in",
    )


def down_scratch(hidden):
    return (
        pltpu.VMEM((hidden, PIECE), jnp.bfloat16),
        pltpu.VMEM((hidden, PIECE // 2), jnp.bfloat16),
        pltpu.VMEM((hidden, PIECE // 2), jnp.float32),
    )


def open_down(down, left, right, wide_right):
    if len(down.shape) == 2:
        left[...] = down[:, :PIECE]
        right[...] = down[:, PIECE:]
        return
    shards, rows, columns = down.shape
    step = rows * 2 // 3
    for f in range(shards):
        for j in range(columns // PIECE):
            at = (f * (columns // PIECE) + j) * step
            lanes = slice(j * PIECE, (j + 1) * PIECE)
            left[at : at + step] = down[f, :step, lanes]
            rest = wide(down[f, step:, lanes])
            wide_right[at : at + step // 2] = rest[:, : PIECE // 2]
            wide_right[at + step // 2 : at + step] = rest[:, PIECE // 2 :]
    right[...] = low(wide_right[...])


def mlp(hidden, attention, gains, which, attn_weights, gate_w, up_w, down_w):
    tokens, width = hidden.shape
    ff = shape_of(gate_w)[1]
    chunk = 512

    def body(get, outs, extra):
        middle_ref, mixed_ref, gate_ref, up_ref, inner_ref, out_ref = outs
        left, right, wide_right = extra
        middle = get(0)[...] + dot_nn(get(1)[...], get(3)[:, QKV:])
        middle_ref[...] = middle
        mixed = low(middle * scale_of(middle) * get(2)[which : which + 1])
        mixed_ref[...] = mixed
        open_down(get(6), left, right, wide_right)
        gate_weight, up_weight = get(4), get(5)
        sums = [0.0, 0.0]
        for c in range(ff // chunk):
            cols = slice(c * chunk, (c + 1) * chunk)
            gate = dot_nn(mixed, gate_weight[:, cols])
            up = dot_nn(mixed, up_weight[:, cols])
            gate_ref[:, cols] = low(gate)
            up_ref[:, cols] = low(up)
            inner = low(gate * jax.nn.sigmoid(gate) * up)
            inner_ref[:, cols] = inner
            sums[0] = sums[0] + dot_nn(inner, left[cols])
            sums[1] = sums[1] + dot_nn(inner, right[cols])
        out_ref[...] = middle + jnp.concatenate(sums, axis=1)

    return run_kernel(
        body,
        (hidden, attention, gains, attn_weights, gate_w, up_w, down_w),
        (
            like((tokens, width), jnp.float32),
            like((tokens, width), jnp.bfloat16),
            like((tokens, ff), jnp.bfloat16),
            like((tokens, ff), jnp.bfloat16),
            like((tokens, ff), jnp.bfloat16),
            like((tokens, width), jnp.float32),
        ),
        scratch=down_scratch(ff),
        cost=8_000_000_000,
        name="mlp",
    )


def norm_back(x, gain, grad):
    scale = scale_of(x)
    unit = x * scale
    e = grad * gain
    dx = scale * (e - unit * jnp.mean(e * unit, axis=1, keepdims=True))
    return dx, jnp.sum(grad * unit, axis=0, keepdims=True)


def put_rows(ref, index, value, shards):
    if shards is None:
        ref[index] = low(value)
        return
    rows = value.shape[0] // shards
    ranks = value.shape[1] // PIECE
    for j in range(ranks):
        for f in range(shards):
            ref[f * ranks + j, index] = low(
                value[f * rows : (f + 1) * rows, j * PIECE : (j + 1) * PIECE]
            )


def mlp_back(grad, kept, gains, which, attn_weights, gate_w, up_w, down_w, shards):
    middle, mixed, gate, up, inner, attention = kept
    tokens, width = grad.shape
    ff = shape_of(gate_w)[1]
    chunk = 512

    def body(get, outs, extra):
        datt_ref, mid_ref, gain_ref, out_grad_ref, weights_ref = outs[:5]
        left, right, wide_right, grad_s, total = extra
        open_down(get(11), left, right, wide_right)
        grad = get(0)[...]
        grad_low = low(grad)
        mixed = get(2)[...]
        d_mixed = 0.0
        for c in range(ff // chunk):
            cols = slice(c * chunk, (c + 1) * chunk)
            d_inner = dot_nt(grad_low[:, :PIECE], left[cols]) + dot_nt(
                grad_low[:, PIECE:], right[cols]
            )
            g = wide(get(3)[:, cols])
            sig = jax.nn.sigmoid(g)
            d_gate = low(d_inner * wide(get(4)[:, cols]) * (sig * (1.0 + g * (1.0 - sig))))
            d_up = low(d_inner * (g * sig))
            grad_s[0, :, cols] = dot_tn(mixed, d_gate)
            grad_s[1, :, cols] = dot_tn(mixed, d_up)
            part = dot_nt(d_gate, get(9)[:, cols]) + dot_nt(d_up, get(10)[:, cols])
            d_mixed = part + d_mixed
            d_down = dot_tn(get(5)[:, cols], grad_low)
            if shards is None:
                outs[5][cols] = low(d_down)
            else:
                total[cols] = d_down
        for index in range(2):
            put_rows(weights_ref, index, grad_s[index], shards)
        if shards is not None:
            rows = width // shards
            step = rows * 2 // 3
            ranks = ff // PIECE
            for f in range(shards):
                for j in range(ranks):
                    at = (f * ranks + j) * step
                    rest = total[at : at + step, PIECE:]
                    value = jnp.concatenate(
                        [
                            total[at : at + step, :PIECE],
                            jnp.concatenate([rest[: step // 2], rest[step // 2 :]], axis=1),
                        ],
                        axis=0,
                    )
                    weights_ref[f * ranks + j, 2] = low(value)
        dx, gain_grad = norm_back(get(1)[...], get(7)[which : which + 1], d_mixed)
        gain_ref[...] = jnp.broadcast_to(gain_grad, gain_ref.shape)
        mid = grad + dx
        mid_ref[...] = mid
        mid_low = low(mid)
        out_grad_ref[...] = low(dot_tn(get(6)[...], mid_low))
        datt_ref[...] = low(dot_nt(mid_low, get(8)[:, QKV:]))

    if shards is None:
        weight_outs = (like((2, width, ff), jnp.bfloat16), like((ff, width), jnp.bfloat16))
    else:
        weight_outs = (like((ff // PIECE * shards, 3, width // shards, PIECE), jnp.bfloat16),)
    return run_kernel(
        body,
        (
            grad, middle, mixed, gate, up, inner, attention, gains,
            attn_weights, gate_w, up_w, down_w,
        ),
        (
            like((tokens, width), jnp.bfloat16),
            like((tokens, width), jnp.float32),
            like((8, width), jnp.float32),
            like((width, width), jnp.bfloat16),
            *weight_outs,
        ),
        scratch=(
            *down_scratch(ff),
            pltpu.VMEM((2, width, ff), jnp.float32),
            pltpu.VMEM((ff, width), jnp.float32),
        ),
        cost=15_000_000_000,
        name="mlp_back",
    )


def project_back(d_queries, pairs, cosine, sine, kept, gains, which, weights, out_grad, mid, shards, riders):
    hidden, normed = kept
    tokens, width = hidden.shape
    parts = len(d_queries)
    slots = len(pairs[0])
    fixed = 8 + parts
    pair_at = lambda part, k: fixed + part * slots + k
    columns = shape_of(weights)[1]
    extra_rows = 0 if riders is None else 8

    def body(get, outs, extra):
        grad_ref, gain_ref, weights_ref = outs
        cos, sin = get(0)[...], get(1)[...]
        d_query = jnp.concatenate([get(8 + part)[...] for part in range(parts)], axis=1)
        dq = turned(d_query, cos, sin, -1.0)
        keys, values = [], []
        for part in range(parts):
            pair = get(pair_at(part, 0))[...]
            for k in range(1, slots):
                pair = pair + wide(get(pair_at(part, k))[...])
            for at in range(0, pair.shape[1], 2 * HD):
                keys.append(pair[:, at : at + HD])
                values.append(pair[:, at + HD : at + 2 * HD])
        dk = turned(jnp.concatenate(keys, axis=1), cos, sin, -1.0)
        d_all = low(jnp.concatenate([dq, dk, *values], axis=1))
        normed_grad = dot_nt(d_all, get(5)[:, :QKV])
        dx, gain_grad = norm_back(get(2)[...], get(4)[which : which + 1], normed_grad)
        gain_ref[...] = jnp.broadcast_to(gain_grad, gain_ref.shape)
        grad_ref[...] = get(7)[...] + dx
        d_weights = dot_tn(get(3)[...], d_all)
        value = jnp.concatenate([d_weights, wide(get(6)[...])], axis=1)
        if riders is None:
            put_rows(weights_ref, 0, value, shards)
        else:
            rows = width // shards
            lines = [get(fixed + parts * slots)[...], gain_grad]
            lines.append(jnp.zeros((8 - 1 - lines[0].shape[0], width), jnp.float32))
            ride = jnp.concatenate(lines, axis=0)
            ride = jnp.concatenate(
                [ride, jnp.zeros((8, columns - width), jnp.float32)], axis=1
            )
            ranks = columns // PIECE
            for j in range(ranks):
                cols = slice(j * PIECE, (j + 1) * PIECE)
                for f in range(shards):
                    weights_ref[f * ranks + j, 0] = low(
                        jnp.concatenate(
                            [value[f * rows : (f + 1) * rows, cols], ride[:, cols]], axis=0
                        )
                    )

    if shards is None:
        shape = (1, width, columns)
    else:
        shape = (columns // PIECE * shards, 1, width // shards + extra_rows, PIECE)
    inputs = (cosine, sine, hidden, normed, gains, weights, out_grad, mid, *d_queries)
    inputs = (*inputs, *[x for pair in pairs for x in pair])
    if riders is not None:
        inputs = (*inputs, riders)
    return run_kernel(
        body,
        inputs,
        (
            like((tokens, width), jnp.float32),
            like((8, width), jnp.float32),
            like(shape, jnp.bfloat16),
        ),
        cost=6_000_000_000,
        name="project_back",
    )


def rope_tables(positions, head_size):
    half = head_size // 2
    freq = theta ** (-(jnp.arange(half, dtype=jnp.float32) * 2.0 / head_size))
    angle = positions.astype(jnp.float32)[..., None] * freq
    return (jnp.cos(angle), jnp.sin(angle))


def body(
    tokens,
    positions,
    query_weight,
    key_matrix,
    value_weight,
    out_weight,
    gate_weight,
    up_weight,
    down_weight,
    attn_gain,
    mlp_gain,
    cotangent,
):
    slots = lax.axis_size("ctx")
    rank = lax.axis_index("ctx")
    shard = lax.axis_index("fsdp")
    shards = lax.axis_size("fsdp")
    fast = slots == 4 and shards == 8
    tokens = swap_halves(tokens)
    positions = swap_halves(positions)
    half = tokens.shape[1] // 2
    rows = attn_gain.shape[1]
    gain_count = 2 * LAYERS
    own_gains = jnp.concatenate([attn_gain, mlp_gain])
    attn_own = [
        jnp.concatenate([query_weight[i], key_matrix[i], value_weight[i], out_weight[i]], axis=1)
        for i in range(LAYERS)
    ]
    mlp_own = [[gate_weight[i], up_weight[i]] for i in range(LAYERS)]
    if fast:
        for i in range(LAYERS):
            mlp_own[i].append(fold_down(down_weight[i]))
        ride = jnp.pad(own_gains, ((0, 8 - gain_count), (0, PIECE - rows)))
        own_first = jnp.concatenate([attn_own[0], jnp.tile(ride, (1, 4))], axis=0)[None]
        own_second = jnp.stack([*mlp_own[0], attn_own[1]])
        own_third = jnp.stack(mlp_own[1])
        first_line = gather_line(own_first)
        second_line = gather_line(own_second)
        third = gather_plain(tied(own_third, second_line))
        first_sides = gather_sides(first_line)
        first_flip = flip(own_first, "fsdp", 1)
        (first, gains), first_mine = gather_rest(
            rows, own_first, first_flip, first_line, first_sides
        )
        gains = wide(gains[:, :gain_count, :rows]).transpose(1, 0, 2).reshape(gain_count, -1)
        second_flip = flip(tied(own_second, first_mine), "fsdp", 1)
        merge = lambda x: x.reshape(x.shape[0], -1, x.shape[-1])
        attn_full = [(merge(first), 0), None]
        by_row = third.reshape(3, shards, rows, -1)
        mlp_full = [None, ((third, 0), (third, 1), (by_row, 2))]
    else:
        gains = wide(lax.all_gather(own_gains, "fsdp", axis=1, tiled=True))
        gather = lambda x: lax.all_gather(x, "fsdp", axis=0, tiled=True)
        attn_full = [gather(x) for x in attn_own]
        mlp_full = [
            (gather(gate_weight[i]), gather(up_weight[i]), gather(down_weight[i]))
            for i in range(LAYERS)
        ]
    gains = jnp.pad(gains, ((0, 8 - gain_count), (0, 0)))
    cosine, sine = rope_tables(positions[0], HD)
    cosine = jnp.concatenate([cosine] * 4, axis=1)
    sine = jnp.concatenate([-sine, sine] * 2, axis=1)
    first_row, second_row = chunks_of(rank, slots)
    offsets = jnp.arange(half, dtype=jnp.int32)
    row_index = jnp.concatenate([first_row * half + offsets, second_row * half + offsets])
    doc_start = row_index[None, :] - positions

    hidden = wide(tokens[0])
    saved = []
    for i in range(LAYERS):
        normed, q, pair = project_in(hidden, gains, i, attn_full[i], cosine, sine)
        if fast and i == 0:
            second_line, pair = lax.optimization_barrier((second_line, pair))
        kvs = [pair] + [flip(pair, "ctx", k) for k in range(1, slots)]
        if fast and i == 0:
            second_sides = gather_sides(second_line)
        attention, lse = attend(q, doc_start, kvs)
        if fast and i == 0:
            second_sides, cotangent = tied((second_sides, cotangent), attention)
            (second,), _ = gather_rest(
                rows, own_second, second_flip, second_line, second_sides
            )
            merged = merge(second)
            mlp_full[0] = ((merged, 0), (merged, 1), (second, 2))
            attn_full[1] = (merged, 3)
        middle, mixed, gate, up, inner, out = mlp(
            hidden, attention, gains, LAYERS + i, attn_full[i], *mlp_full[i]
        )
        saved.append((hidden, normed, q, kvs, attention, lse, middle, mixed, gate, up, inner))
        hidden = out
    layer_out = swap_halves(low(hidden)[None])
    grad = wide(swap_halves(cotangent)[0])

    gain_grads = {}
    mlp_grads = [None] * LAYERS
    attn_grads = [None] * LAYERS
    by_shard = shards if fast else None
    for i in reversed(range(LAYERS)):
        hidden, normed, q, kvs, attention, lse, middle, mixed, gate, up, inner = saved[i]
        d_attention, mid, gain_grads[LAYERS + i], out_grad, *weight_grads = mlp_back(
            grad,
            (middle, mixed, gate, up, inner, attention),
            gains,
            LAYERS + i,
            attn_full[i],
            *mlp_full[i],
            by_shard,
        )
        if fast and i == 0:
            sums, sends = reduce_begin(weight_grads[0], attn_grads[1])
            d_attention, sends, early = lax.optimization_barrier((d_attention, sends, early))
            sides = reduce_sides(sends)
        elif fast:
            early = lax.psum_scatter(
                weight_grads[0], "fsdp", scatter_dimension=0, tiled=True
            )
        else:
            mlp_grads[i] = (
                reduce_plain(weight_grads[0], 1),
                reduce_plain(weight_grads[1], 0),
            )
        d_queries, pairs = [], []
        for groups in (range(KV_HEADS - 1), range(KV_HEADS - 1, KV_HEADS)):
            d_query, *pair = attend_back(
                q, attention, d_attention, lse, doc_start, kvs, groups
            )
            d_queries.append(d_query)
            if pairs:
                pair, pairs = lax.optimization_barrier((pair, pairs))
            d_attention, pair = lax.optimization_barrier((d_attention, pair))
            pairs.append([pair[0]] + [flip(pair[k], "ctx", k) for k in range(1, slots)])
            if fast and i == 0 and groups.start == 0:
                sides = tied(sides, d_query)
                sums, sends = reduce_middle(sums, sides)
                d_attention, sends = lax.optimization_barrier((d_attention, sends))
                across = reduce_across(sends)
            elif fast and i == 0:
                sums, sends = reduce_turn(sums, tied(across, d_query))
                d_queries, sends = lax.optimization_barrier((d_queries, sends))
                line = (sums, *reduce_line(sends))
        riders = None
        if fast and i == 0:
            riders = jnp.concatenate([gain_grads[v][:1] for v in (1, 2, 3)])
        grad, gain_grads[i], attn_grad = project_back(
            d_queries,
            pairs,
            cosine,
            sine,
            (hidden, normed),
            gains,
            i,
            attn_full[i],
            out_grad,
            mid,
            by_shard,
            riders,
        )
        if fast and i == 0:
            moved = [
                lax.dynamic_index_in_dim(early, rank ^ k, axis=0, keepdims=False)
                for k in range(4)
            ]
            moved = [moved[0]] + [flip(moved[k], "ctx", k) for k in (1, 2, 3)]
            sums, sends = reduce_begin(attn_grad)
            line, sends, grad, moved = lax.optimization_barrier((line, sends, grad, moved))
            early = low(sum((wide(part) for part in moved[1:]), wide(moved[0])))
            sides = reduce_sides(sends)
            rest = spread_fast(jnp.concatenate([low(reduce_end(line)), early]))
            sums, sends = reduce_middle(sums, sides)
            sums, sends = reduce_turn(sums, reduce_across(sends))
            last = spread_fast(reduce_end((sums, *reduce_line(sends))))
            early = rest[4:]
            all_gains = lax.dynamic_slice_in_dim(last[0, rows:], shard * rows, rows, axis=1)
            order = (3, 0, 1, 2)
            all_gains = jnp.stack([all_gains[v] for v in order])
            attn_rows = jnp.stack([last[0, :rows], rest[3]])
            gate_rows = jnp.stack([rest[0], early[0]])
            up_rows = jnp.stack([rest[1], early[1]])
            down_rows = unfold_down(jnp.stack([rest[2], early[2]]))
        elif fast:
            attn_grads[i] = attn_grad
        else:
            attn_grads[i] = reduce_plain(attn_grad[0], 0)
    if not fast:
        attn_rows = jnp.stack(attn_grads)
        gate_rows = jnp.stack([part[0][0] for part in mlp_grads])
        up_rows = jnp.stack([part[0][1] for part in mlp_grads])
        down_rows = jnp.stack([part[1] for part in mlp_grads])
        all_gains = jnp.concatenate([gain_grads[v][:1] for v in range(gain_count)])
        all_gains = lax.psum(all_gains, ("ctx", "fsdp"))
        all_gains = lax.dynamic_slice_in_dim(all_gains, shard * rows, rows, axis=1)
    far = wide(flip(low(grad[half:]), "ctx", slots - 1))
    grad = jnp.concatenate([grad[:half], far])[None]
    return (
        layer_out,
        grad,
        attn_rows[..., :QUERY],
        attn_rows[..., QUERY : QUERY + KVW],
        attn_rows[..., QUERY + KVW : QKV],
        attn_rows[..., QKV:],
        gate_rows,
        up_rows,
        down_rows,
        all_gains[:LAYERS],
        all_gains[LAYERS:],
    )


def solution(mesh):
    return jax.shard_map(
        body,
        mesh=mesh,
        in_specs=(
            P("fsdp", "ctx", None),
            P("fsdp", "ctx"),
            P(None, "fsdp", None),
            P(None, "fsdp", None),
            P(None, "fsdp", None),
            P(None, "fsdp", None),
            P(None, "fsdp", None),
            P(None, "fsdp", None),
            P(None, "fsdp", None),
            P(None, "fsdp"),
            P(None, "fsdp"),
            P("fsdp", "ctx", None),
        ),
        out_specs=(
            P("fsdp", "ctx", None),
            P("fsdp", "ctx", None),
            P(None, "fsdp", None),
            P(None, "fsdp", None),
            P(None, "fsdp", None),
            P(None, "fsdp", None),
            P(None, "fsdp", None),
            P(None, "fsdp", None),
            P(None, "fsdp", None),
            P(None, "fsdp"),
            P(None, "fsdp"),
        ),
        check_vma=False,
    )
```

```python
import jax
import jax.numpy as jnp
from jax import lax
from jax.experimental import pallas as pl
from jax.experimental.pallas import tpu as pltpu
from jax.sharding import PartitionSpec as P

HEADS = 9
KV_HEADS = 3
HD = 64
LAYERS = 2


epsilon = 1e-05
theta = 100000.0
log_two_e = 1.4426950408889634
mask_filler = -1e30


def flip(block, axis, mask):
    route = [(i, i ^ mask) for i in range(lax.axis_size(axis))]
    return lax.ppermute(block, axis, route)


def swap_halves(x):
    half = x.shape[1] // 2
    return jnp.concatenate(
        [x[:, :half], flip(x[:, half:], "ctx", lax.axis_size("ctx") - 1)], axis=1
    )


def tied(first, *then):
    return lax.optimization_barrier((first, then))[0]


def low(x):
    return x.astype(jnp.bfloat16)


def wide(x):
    return x.astype(jnp.float32)


PIECE = 384
VMEM_LIMIT = 48 * 1024 * 1024


def fold_down(shard):
    step = shard.shape[0] // 4
    pieces = []
    for j in range(4):
        rows = shard[j * step : (j + 1) * step]
        rest = rows[:, PIECE:]
        rest = jnp.concatenate([rest[: step // 2], rest[step // 2 :]], axis=1)
        pieces.append(jnp.concatenate([rows[:, :PIECE], rest], axis=0))
    return jnp.concatenate(pieces, axis=1)


def unfold_down(folded):
    step = folded.shape[-2] * 2 // 3
    pieces = []
    for piece in jnp.split(folded, 4, axis=-1):
        rest = piece[..., step:, :]
        rest = jnp.concatenate(jnp.split(rest, 2, axis=-1), axis=-2)
        pieces.append(jnp.concatenate([piece[..., :step, :], rest], axis=-1))
    return jnp.concatenate(pieces, axis=-2)


def assemble_kernel(rows, own, own_flip, mine, theirs, out, *rest):
    sems = rest[-1]
    j = lax.axis_index("ctx")
    f = lax.axis_index("fsdp")
    copies = []

    def copy(src, dst):
        made = pltpu.make_async_copy(src, dst, sems.at[len(copies)])
        made.start()
        copies.append(made)

    for core, shard in ((0, own), (1, own_flip)):
        copy(shard.at[:, :rows], out.at[:, f ^ core])
        if len(rest) > 1:
            copy(shard.at[0, rows:, :PIECE], rest[0].at[f ^ core])
    for core, pieces in ((0, mine), (1, theirs)):
        for jrel in range(4):
            for zrel in range(1, 4):
                row = f ^ (core + 2 * zrel)
                column = pl.multiple_of((j ^ jrel) * PIECE, 128)
                piece = pieces.at[jrel * 3 + zrel - 1]
                copy(piece.at[:, :rows], out.at[:, row, :, pl.ds(column, PIECE)])
                if jrel == 0 and len(rest) > 1:
                    copy(piece.at[0, rows:], rest[0].at[row])
    for made in copies:
        made.wait()


def assemble(rows, own, own_flip, mine, theirs):
    count, all_rows, columns = own.shape
    fsdp = lax.axis_size("fsdp")
    shapes = [jax.ShapeDtypeStruct((count, fsdp, rows, columns), own.dtype)]
    if all_rows > rows:
        shapes.append(jax.ShapeDtypeStruct((fsdp, all_rows - rows, PIECE), own.dtype))
    return pl.pallas_call(
        lambda *refs: assemble_kernel(rows, *refs),
        out_shape=tuple(shapes),
        in_specs=[pl.BlockSpec(memory_space=pl.ANY)] * 4,
        out_specs=[pl.BlockSpec(memory_space=pltpu.VMEM)] * len(shapes),
        scratch_shapes=[pltpu.SemaphoreType.DMA((34,))],
        compiler_params=pltpu.CompilerParams(vmem_limit_bytes=VMEM_LIMIT),
        name="assemble",
    )(own, own_flip, mine, theirs)


def gather_line(own):
    j = lax.axis_index("ctx")
    piece = lax.dynamic_slice_in_dim(own, j * PIECE, PIECE, axis=2)
    return jnp.stack([flip(piece, "fsdp", 2 * k) for k in (1, 2, 3)])


def gather_sides(line):
    return flip(line, "ctx", 1), flip(line, "ctx", 2)


def gather_rest(rows, own, own_flip, line, sides):
    by_x, by_y = sides
    diag = jnp.concatenate([flip(by_x[:2], "ctx", 2), flip(by_y[2:], "ctx", 1)])
    mine = jnp.concatenate([line, by_x, by_y, diag])
    theirs = flip(mine, "fsdp", 1)
    return assemble(rows, own, own_flip, mine, theirs), mine


def gather_plain(own):
    return lax.all_gather(own, "fsdp", axis=1, tiled=True)


def reduce_start(whole):
    by_core = whole.reshape(2, 4, 4, *whole.shape[1:])
    return by_core[0], flip(by_core[1], "fsdp", 1)


def reduce_begin(*halves):
    total = jnp.concatenate([wide(keep) + wide(other) for keep, other in halves], axis=2)
    a = low(total[:, :2])
    b = low(total[:, 2:])
    return (a[0], a[2], b[0], b[1]), (jnp.stack([a[1], a[3]]), jnp.stack([b[2], b[3]]))


def reduce_sides(sends):
    return flip(sends[0], "ctx", 1), flip(sends[1], "ctx", 2)


def reduce_middle(sums, sides):
    a0, a2, b0, b1 = (wide(part) for part in sums)
    x1, y1 = wide(sides[0]), wide(sides[1])
    return (a0 + x1[0], b0 + y1[0]), (low(a2 + x1[1]), low(b1 + y1[1]))


def reduce_across(sends):
    return flip(sends[0], "ctx", 2), flip(sends[1], "ctx", 1)


def reduce_turn(sums, across):
    a0 = sums[0] + wide(across[0])
    b0 = sums[1] + wide(across[1])
    return a0[0], (low(a0[1]), low(b0[0]), low(b0[1]))


def reduce_line(sends):
    return [flip(part, "fsdp", 2 * k + 2) for k, part in enumerate(sends)]


def reduce_end(line):
    return line[0] + sum(wide(part) for part in line[1:])


def spread_fast(piece):
    j = lax.axis_index("ctx")
    own = low(piece)
    parts = [own] + [flip(own, "ctx", k) for k in (1, 2, 3)]
    for bit in (1, 2):
        odd = (j & bit) != 0
        parts = [jnp.where(odd, parts[i ^ bit], parts[i]) for i in range(4)]
    return wide(jnp.concatenate(parts, axis=2))


def reduce_plain(whole, dim):
    part = lax.psum_scatter(whole, "fsdp", scatter_dimension=dim, tiled=True)
    return wide(lax.psum(part, "ctx"))


def dot_nn(a, b):
    return jnp.dot(a, b, preferred_element_type=jnp.float32)


def dot_nt(a, b):
    return lax.dot_general(a, b, (((1,), (1,)), ((), ())), preferred_element_type=jnp.float32)


def dot_tn(a, b):
    return lax.dot_general(a, b, (((0,), (0,)), ((), ())), preferred_element_type=jnp.float32)


def shape_of(x):
    return x[0].shape[1:] if isinstance(x, tuple) else x.shape


def run_kernel(body, inputs, outputs, scratch=(), cost=0, name=None):
    count = len(inputs)
    arrays = [x[0] if isinstance(x, tuple) else x for x in inputs]

    def kernel(*refs):
        sources = refs[:count]
        outs = refs[count : count + len(outputs)]
        rest = refs[count + len(outputs) :]
        buffers, extra, sems = rest[:count], rest[count:-1], rest[-1]
        copies = [
            pltpu.make_async_copy(
                source.at[x[1]] if isinstance(x, tuple) else source, buffer, sems.at[i]
            )
            for i, (x, source, buffer) in enumerate(zip(inputs, sources, buffers))
        ]
        for copy in copies:
            copy.start()
        waited = set()

        def get(i):
            if i not in waited:
                waited.add(i)
                copies[i].wait()
            return buffers[i]

        body(get, outs, extra)
        for i in range(count):
            get(i)

    return pl.pallas_call(
        kernel,
        out_shape=tuple(outputs),
        in_specs=[pl.BlockSpec(memory_space=pl.ANY)] * count,
        out_specs=[pl.BlockSpec(memory_space=pltpu.VMEM)] * len(outputs),
        scratch_shapes=[
            *[pltpu.VMEM(shape_of(x), array.dtype) for x, array in zip(inputs, arrays)],
            *scratch,
            pltpu.SemaphoreType.DMA((count,)),
        ],
        compiler_params=pltpu.CompilerParams(vmem_limit_bytes=VMEM_LIMIT),
        cost_estimate=pl.CostEstimate(flops=cost, bytes_accessed=4_000_000, transcendentals=0),
        name=name,
    )(*arrays)


def like(shape, kind):
    return jax.ShapeDtypeStruct(shape, kind)


def chunks_of(source, slots):
    return (2 * source, 2 * slots - 1 - 2 * source)


def stack_heads(ref, dst, half, groups=range(KV_HEADS)):
    group = HEADS // KV_HEADS
    for g in groups:
        for part in range(2):
            for i in range(group):
                h = g * group + i
                dst[g, part, i * half : (i + 1) * half] = ref[
                    part * half : (part + 1) * half, h * HD : (h + 1) * HD
                ]


def thrice(row):
    return jnp.concatenate([row] * (HEADS // KV_HEADS), axis=1)


def attend_kernel(slots, *refs):
    q_ref, start_ref = refs[:2]
    kv_refs = refs[2 : 2 + slots]
    o_ref, lse_ref, qs, ks, vt, top_s, acc_s, ot = refs[2 + slots :]
    rank = lax.axis_index("ctx")
    half = q_ref.shape[0] // 2
    group = HEADS // KV_HEADS
    wide_cols = group * half
    stack_heads(q_ref, qs, half)
    ones = jnp.ones((16, half), jnp.bfloat16)
    for k in range(slots):
        values_t = low(jnp.transpose(wide(kv_refs[k][:, 128:])))
        for g in range(KV_HEADS):
            row = KV_HEADS * HD - 128 + g * HD
            for part in range(2):
                rows = slice(part * half, (part + 1) * half)
                ks[k, g, part] = kv_refs[k][rows, g * HD : (g + 1) * HD]
                vt[k, g, part, :HD] = values_t[row : row + HD, rows]
                vt[k, g, part, HD:] = ones
    lse_ref[...] = jnp.zeros_like(lse_ref)
    mine = chunks_of(rank, slots)

    def one_group(g, carry):
        for part in range(2):
            cols = slice(part * half, (part + 1) * half)
            start = thrice(start_ref[:, cols])
            q = qs[g, part]

            def scores(k, other, first):
                s = dot_nt(ks[k, g, other], q)
                key = lax.broadcasted_iota(jnp.int32, s.shape, 0)
                visible = key >= start - first
                return s, key, visible

            s, key, visible = scores(0, part, mine[part] * half)
            query = thrice(lax.broadcasted_iota(jnp.int32, (half, half), 1))
            s = jnp.where(visible & (key <= query), s, mask_filler)
            top = jnp.floor(jnp.max(s, axis=0, keepdims=True))
            top_s[...] = top
            acc_s[...] = dot_nn(vt[0, g, part], low(jnp.exp2(s - top)))

            def tile(k, other, chunk):
                @pl.when(chunk < mine[part])
                def _():
                    s, _, visible = scores(k, other, chunk * half)
                    s = jnp.where(visible, s, mask_filler)
                    old = top_s[...]
                    top = jnp.maximum(old, jnp.floor(jnp.max(s, axis=0, keepdims=True)))
                    top_s[...] = top
                    acc_s[...] = acc_s[...] * jnp.exp2(old - top) + dot_nn(
                        vt[k, g, other], low(jnp.exp2(s - top))
                    )

            tile(0, 1 - part, mine[1 - part])

            def slot(k, carry):
                theirs = chunks_of(rank ^ k, slots)
                for other in range(2):
                    tile(k, other, theirs[other])
                return carry

            lax.fori_loop(1, slots, slot, 0)
            total = acc_s[HD : HD + 1]
            out = acc_s[:HD] / total
            level = top_s[...] + jnp.log2(total)
            for i in range(group):
                inner = slice(i * half, (i + 1) * half)
                ot[g, i, :, cols] = out[:, inner]
                lse_ref[pl.ds(g * group + i, 1), cols] = level[:, inner]
        return carry

    lax.fori_loop(0, KV_HEADS, one_group, 0)
    o_ref[...] = low(jnp.transpose(ot[...].reshape(HEADS * HD, 2 * half)))


def attend(q, start, kvs):
    block = q.shape[0]
    half = block // 2
    slots = len(kvs)
    group = HEADS // KV_HEADS
    inputs = (q, start, *kvs)

    def body(get, outs, extra):
        attend_kernel(slots, *[get(i) for i in range(len(inputs))], *outs, *extra)

    return run_kernel(
        body,
        inputs,
        (like((block, HEADS * HD), jnp.bfloat16), like((16, block), jnp.float32)),
        scratch=(
            pltpu.VMEM((KV_HEADS, 2, group * half, HD), jnp.bfloat16),
            pltpu.VMEM((slots, KV_HEADS, 2, half, HD), jnp.bfloat16),
            pltpu.VMEM((slots, KV_HEADS, 2, HD + 16, half), jnp.bfloat16),
            pltpu.VMEM((1, group * half), jnp.float32),
            pltpu.VMEM((HD + 16, group * half), jnp.float32),
            pltpu.VMEM((KV_HEADS, group, HD, block), jnp.float32),
        ),
        cost=15_000_000_000,
        name="attend",
    )


def attend_back_kernel(slots, groups, *refs):
    q_ref, o_ref, do_ref, lse_ref, start_ref = refs[:5]
    kv_refs = refs[5 : 5 + slots]
    dq_ref = refs[5 + slots]
    dkv_refs = refs[6 + slots : 6 + 2 * slots]
    qs, dos, ks, kt, vs, dk_s, dv_s, dqt_s, delta_s, dqt_all = refs[6 + 2 * slots :]
    rank = lax.axis_index("ctx")
    half = q_ref.shape[0] // 2
    group = HEADS // KV_HEADS
    stack_heads(q_ref, qs, half, groups)
    stack_heads(do_ref, dos, half, groups)
    for k in range(slots):
        keys_t = low(jnp.transpose(wide(kv_refs[k][:, : 2 * 128])))
        for g in groups:
            for part in range(2):
                rows = slice(part * half, (part + 1) * half)
                ks[k, g, part] = kv_refs[k][rows, g * HD : (g + 1) * HD]
                kt[k, g, part] = keys_t[g * HD : (g + 1) * HD, rows]
                vs[k, g, part] = kv_refs[k][rows, (KV_HEADS + g) * HD : (KV_HEADS + g + 1) * HD]
    product = wide(do_ref[...]) * wide(o_ref[...])
    coarse = low(product)
    fine = low(product - wide(coarse))
    shape = (16, HEADS * HD)
    owner = lax.div(lax.broadcasted_iota(jnp.int32, shape, 1), HD)
    pick = jnp.where(owner == lax.broadcasted_iota(jnp.int32, shape, 0), 1.0, 0.0)
    pick = pick.astype(jnp.bfloat16)
    delta_s[...] = dot_nt(pick, coarse) + dot_nt(pick, fine)
    dk_s[...] = jnp.zeros_like(dk_s)
    dv_s[...] = jnp.zeros_like(dv_s)
    mine = chunks_of(rank, slots)

    def one_group(g, carry):
        for part in range(2):
            cols = slice(part * half, (part + 1) * half)
            start = thrice(start_ref[:, cols])
            heads = [pl.ds(g * group + i, 1) for i in range(group)]
            lse = jnp.concatenate([lse_ref[h, cols] for h in heads], axis=1)
            delta = jnp.concatenate([delta_s[h, cols] for h in heads], axis=1)

            def tile(k, other, first, diagonal):
                q = qs[g, part]
                do = dos[g, part]
                s = dot_nt(ks[k, g, other], q)
                key = lax.broadcasted_iota(jnp.int32, s.shape, 0)
                visible = key >= start - first
                if diagonal:
                    query = thrice(lax.broadcasted_iota(jnp.int32, (half, half), 1))
                    visible = visible & (key <= query)
                p = jnp.where(visible, jnp.exp2(s - lse), 0.0)
                dv = dot_nn(low(p), do)
                dp = dot_nt(vs[k, g, other], do)
                ds = low(p * (dp - delta))
                dk_s[k, g, other] += dot_nn(ds, q)
                dv_s[k, g, other] += dv
                dq = dot_nn(kt[k, g, other], ds)
                if diagonal:
                    dqt_s[...] = dq
                else:
                    dqt_s[...] += dq

            tile(0, part, mine[part] * half, True)

            @pl.when(mine[1 - part] < mine[part])
            def _():
                tile(0, 1 - part, mine[1 - part] * half, False)

            def slot(k, carry):
                theirs = chunks_of(rank ^ k, slots)
                for other in range(2):

                    @pl.when(theirs[other] < mine[part])
                    def _():
                        tile(k, other, theirs[other] * half, False)

                return carry

            lax.fori_loop(1, slots, slot, 0)
            for i in range(group):
                dqt_all[g, i, :, cols] = dqt_s[:, i * half : (i + 1) * half]
        return carry

    lax.fori_loop(groups.start, groups.stop, one_group, 0)
    dqt = dqt_all[groups.start : groups.stop]
    dq_ref[...] = jnp.transpose(dqt.reshape(len(groups) * group * HD, 2 * half)) * 0.125
    for k in range(slots):
        for part in range(2):
            dkv = jnp.concatenate(
                [
                    x
                    for g in groups
                    for x in (dk_s[k, g, part] * (1.0 / log_two_e), dv_s[k, g, part])
                ],
                axis=1,
            )
            dkv_refs[k][part * half : (part + 1) * half] = dkv.astype(dkv_refs[k].dtype)


def attend_back(q, o, do, lse, start_row, kvs, groups):
    block = q.shape[0]
    half = block // 2
    slots = len(kvs)
    group = HEADS // KV_HEADS
    inputs = (q, o, do, lse, start_row, *kvs)
    pair = lambda kind: like((block, 2 * len(groups) * HD), kind)

    def body(get, outs, extra):
        attend_back_kernel(slots, groups, *[get(i) for i in range(len(inputs))], *outs, *extra)

    return run_kernel(
        body,
        inputs,
        (
            like((block, len(groups) * group * HD), jnp.float32),
            pair(jnp.float32),
            *[pair(jnp.bfloat16)] * (slots - 1),
        ),
        scratch=(
            pltpu.VMEM((KV_HEADS, 2, group * half, HD), jnp.bfloat16),
            pltpu.VMEM((KV_HEADS, 2, group * half, HD), jnp.bfloat16),
            pltpu.VMEM((slots, KV_HEADS, 2, half, HD), jnp.bfloat16),
            pltpu.VMEM((slots, KV_HEADS, 2, HD, half), jnp.bfloat16),
            pltpu.VMEM((slots, KV_HEADS, 2, half, HD), jnp.bfloat16),
            pltpu.VMEM((slots, KV_HEADS, 2, half, HD), jnp.float32),
            pltpu.VMEM((slots, KV_HEADS, 2, half, HD), jnp.float32),
            pltpu.VMEM((HD, group * half), jnp.float32),
            pltpu.VMEM((16, block), jnp.float32),
            pltpu.VMEM((KV_HEADS, group, HD, block), jnp.float32),
        ),
        cost=7_000_000_000 * len(groups),
        name="attend_back",
    )


def scale_of(x):
    return lax.rsqrt(jnp.mean(x * x, axis=1, keepdims=True) + epsilon)


def tiled_lanes(table, columns):
    full = [table] * (columns // 128)
    if columns % 128:
        full.append(table[:, : columns % 128])
    return jnp.concatenate(full, axis=1)


def swapped(x):
    columns = x.shape[1]
    row = lax.broadcasted_iota(jnp.int32, (columns, columns), 0)
    col = lax.broadcasted_iota(jnp.int32, (columns, columns), 1)
    partner = jnp.where((col & (HD - 1)) < HD // 2, col + HD // 2, col - HD // 2)
    exchange = jnp.where(row == partner, 1.0, 0.0).astype(jnp.bfloat16)
    coarse = low(x)
    rest = x - wide(coarse)
    fine = low(rest)
    return dot_nn(coarse, exchange) + dot_nn(fine, exchange)


def turned(x, cosine, sine, sign):
    columns = x.shape[1]
    return x * tiled_lanes(cosine, columns) + swapped(x) * (sign * tiled_lanes(sine, columns))


QUERY = HEADS * HD
KVW = KV_HEADS * HD
QKV = QUERY + 2 * KVW


def project_in(hidden, gains, which, weights, cosine, sine):
    tokens, width = hidden.shape

    def body(get, outs, extra):
        normed_ref, q_ref, pair_ref = outs
        h = get(0)[...]
        normed = low(h * scale_of(h) * get(1)[which : which + 1])
        normed_ref[...] = normed
        out = dot_nn(normed, get(2)[:, :QKV])
        cos, sin = get(3)[...], get(4)[...]
        q_ref[...] = low(turned(out[:, :QUERY], cos, sin, 1.0) * (0.125 * log_two_e))
        keys = turned(out[:, QUERY : QUERY + KVW], cos, sin, 1.0)
        pair_ref[...] = low(jnp.concatenate([keys, out[:, QUERY + KVW :]], axis=1))

    return run_kernel(
        body,
        (hidden, gains, weights, cosine, sine),
        (
            like((tokens, width), jnp.bfloat16),
            like((tokens, QUERY), jnp.bfloat16),
            like((tokens, 2 * KVW), jnp.bfloat16),
        ),
        cost=4_000_000_000,
        name="project_in",
    )


def down_scratch(hidden):
    return (
        pltpu.VMEM((hidden, PIECE), jnp.bfloat16),
        pltpu.VMEM((hidden, PIECE // 2), jnp.bfloat16),
        pltpu.VMEM((hidden, PIECE // 2), jnp.float32),
    )


def open_down(down, left, right, wide_right):
    if len(down.shape) == 2:
        left[...] = down[:, :PIECE]
        right[...] = down[:, PIECE:]
        return
    shards, rows, columns = down.shape
    step = rows * 2 // 3
    for f in range(shards):
        for j in range(columns // PIECE):
            at = (f * (columns // PIECE) + j) * step
            lanes = slice(j * PIECE, (j + 1) * PIECE)
            left[at : at + step] = down[f, :step, lanes]
            rest = wide(down[f, step:, lanes])
            wide_right[at : at + step // 2] = rest[:, : PIECE // 2]
            wide_right[at + step // 2 : at + step] = rest[:, PIECE // 2 :]
    right[...] = low(wide_right[...])


def mlp(hidden, attention, gains, which, attn_weights, gate_w, up_w, down_w):
    tokens, width = hidden.shape
    ff = shape_of(gate_w)[1]
    chunk = 512

    def body(get, outs, extra):
        middle_ref, mixed_ref, gate_ref, up_ref, inner_ref, out_ref = outs
        left, right, wide_right = extra
        middle = get(0)[...] + dot_nn(get(1)[...], get(3)[:, QKV:])
        middle_ref[...] = middle
        mixed = low(middle * scale_of(middle) * get(2)[which : which + 1])
        mixed_ref[...] = mixed
        open_down(get(6), left, right, wide_right)
        gate_weight, up_weight = get(4), get(5)
        sums = [0.0, 0.0]
        for c in range(ff // chunk):
            cols = slice(c * chunk, (c + 1) * chunk)
            gate = dot_nn(mixed, gate_weight[:, cols])
            up = dot_nn(mixed, up_weight[:, cols])
            gate_ref[:, cols] = low(gate)
            up_ref[:, cols] = low(up)
            inner = low(gate * jax.nn.sigmoid(gate) * up)
            inner_ref[:, cols] = inner
            sums[0] = sums[0] + dot_nn(inner, left[cols])
            sums[1] = sums[1] + dot_nn(inner, right[cols])
        out_ref[...] = middle + jnp.concatenate(sums, axis=1)

    return run_kernel(
        body,
        (hidden, attention, gains, attn_weights, gate_w, up_w, down_w),
        (
            like((tokens, width), jnp.float32),
            like((tokens, width), jnp.bfloat16),
            like((tokens, ff), jnp.bfloat16),
            like((tokens, ff), jnp.bfloat16),
            like((tokens, ff), jnp.bfloat16),
            like((tokens, width), jnp.float32),
        ),
        scratch=down_scratch(ff),
        cost=8_000_000_000,
        name="mlp",
    )


def norm_back(x, gain, grad):
    scale = scale_of(x)
    unit = x * scale
    e = grad * gain
    dx = scale * (e - unit * jnp.mean(e * unit, axis=1, keepdims=True))
    return dx, jnp.sum(grad * unit, axis=0, keepdims=True)


def place_of(relative, ranks, shards):
    if not relative:
        return lambda f, j: f * ranks + j
    me, rank = lax.axis_index("fsdp"), lax.axis_index("ctx")

    def place(f, j):
        apart = f ^ me
        return (apart & 1) * (ranks * shards // 2) + (j ^ rank) * (shards // 2) + (apart >> 1)

    return place


def put_rows(ref, index, value, shards, place):
    if shards is None:
        ref[index] = low(value)
        return
    rows = value.shape[0] // shards
    ranks = value.shape[1] // PIECE
    for j in range(ranks):
        for f in range(shards):
            ref[place(f, j), index] = low(
                value[f * rows : (f + 1) * rows, j * PIECE : (j + 1) * PIECE]
            )


def mlp_back(grad, kept, gains, which, attn_weights, gate_w, up_w, down_w, shards, relative):
    middle, mixed, gate, up, inner, attention = kept
    tokens, width = grad.shape
    ff = shape_of(gate_w)[1]
    chunk = 512

    def body(get, outs, extra):
        datt_ref, mid_ref, gain_ref, out_grad_ref, weights_ref = outs[:5]
        left, right, wide_right, grad_s, total = extra
        place = None if shards is None else place_of(relative, ff // PIECE, shards)
        open_down(get(11), left, right, wide_right)
        grad = get(0)[...]
        grad_low = low(grad)
        mixed_t = low(jnp.transpose(wide(get(2)[...])))
        d_mixed = 0.0
        for c in range(ff // chunk):
            cols = slice(c * chunk, (c + 1) * chunk)
            d_inner = dot_nt(grad_low[:, :PIECE], left[cols]) + dot_nt(
                grad_low[:, PIECE:], right[cols]
            )
            g = wide(get(3)[:, cols])
            sig = jax.nn.sigmoid(g)
            d_gate = low(d_inner * wide(get(4)[:, cols]) * (sig * (1.0 + g * (1.0 - sig))))
            d_up = low(d_inner * (g * sig))
            grad_s[0, :, cols] = dot_nn(mixed_t, d_gate)
            grad_s[1, :, cols] = dot_nn(mixed_t, d_up)
            part = dot_nt(d_gate, get(9)[:, cols]) + dot_nt(d_up, get(10)[:, cols])
            d_mixed = part + d_mixed
            d_down = dot_tn(get(5)[:, cols], grad_low)
            if shards is None:
                outs[5][cols] = low(d_down)
            else:
                total[cols] = d_down
        for index in range(2):
            put_rows(weights_ref, index, grad_s[index], shards, place)
        if shards is not None:
            rows = width // shards
            step = rows * 2 // 3
            ranks = ff // PIECE
            for f in range(shards):
                for j in range(ranks):
                    at = (f * ranks + j) * step
                    rest = total[at : at + step, PIECE:]
                    value = jnp.concatenate(
                        [
                            total[at : at + step, :PIECE],
                            jnp.concatenate([rest[: step // 2], rest[step // 2 :]], axis=1),
                        ],
                        axis=0,
                    )
                    weights_ref[place(f, j), 2] = low(value)
        dx, gain_grad = norm_back(get(1)[...], get(7)[which : which + 1], d_mixed)
        gain_ref[...] = jnp.broadcast_to(gain_grad, gain_ref.shape)
        mid = grad + dx
        mid_ref[...] = mid
        mid_low = low(mid)
        out_grad_ref[...] = low(dot_tn(get(6)[...], mid_low))
        datt_ref[...] = low(dot_nt(mid_low, get(8)[:, QKV:]))

    if shards is None:
        weight_outs = (like((2, width, ff), jnp.bfloat16), like((ff, width), jnp.bfloat16))
    else:
        weight_outs = (like((ff // PIECE * shards, 3, width // shards, PIECE), jnp.bfloat16),)
    return run_kernel(
        body,
        (
            grad, middle, mixed, gate, up, inner, attention, gains,
            attn_weights, gate_w, up_w, down_w,
        ),
        (
            like((tokens, width), jnp.bfloat16),
            like((tokens, width), jnp.float32),
            like((8, width), jnp.float32),
            like((width, width), jnp.bfloat16),
            *weight_outs,
        ),
        scratch=(
            *down_scratch(ff),
            pltpu.VMEM((2, width, ff), jnp.float32),
            pltpu.VMEM((ff, width), jnp.float32),
        ),
        cost=15_000_000_000,
        name="mlp_back",
    )


def project_back(d_queries, pairs, cosine, sine, kept, gains, which, weights, out_grad, mid, shards, riders, relative):
    hidden, normed = kept
    tokens, width = hidden.shape
    parts = len(d_queries)
    slots = len(pairs[0])
    fixed = 8 + parts
    pair_at = lambda part, k: fixed + part * slots + k
    columns = shape_of(weights)[1]
    extra_rows = 0 if riders is None else 8

    def body(get, outs, extra):
        grad_ref, gain_ref, weights_ref = outs
        cos, sin = get(0)[...], get(1)[...]
        d_query = jnp.concatenate([get(8 + part)[...] for part in range(parts)], axis=1)
        dq = turned(d_query, cos, sin, -1.0)
        keys, values = [], []
        for part in range(parts):
            pair = get(pair_at(part, 0))[...]
            for k in range(1, slots):
                pair = pair + wide(get(pair_at(part, k))[...])
            for at in range(0, pair.shape[1], 2 * HD):
                keys.append(pair[:, at : at + HD])
                values.append(pair[:, at + HD : at + 2 * HD])
        dk = turned(jnp.concatenate(keys, axis=1), cos, sin, -1.0)
        d_all = low(jnp.concatenate([dq, dk, *values], axis=1))
        normed_grad = dot_nt(d_all, get(5)[:, :QKV])
        dx, gain_grad = norm_back(get(2)[...], get(4)[which : which + 1], normed_grad)
        gain_ref[...] = jnp.broadcast_to(gain_grad, gain_ref.shape)
        grad_ref[...] = get(7)[...] + dx
        d_weights = dot_tn(get(3)[...], d_all)
        value = jnp.concatenate([d_weights, wide(get(6)[...])], axis=1)
        if riders is None:
            place = None if shards is None else place_of(relative, columns // PIECE, shards)
            put_rows(weights_ref, 0, value, shards, place)
        else:
            rows = width // shards
            lines = [get(fixed + parts * slots)[...], gain_grad]
            lines.append(jnp.zeros((8 - 1 - lines[0].shape[0], width), jnp.float32))
            ride = jnp.concatenate(lines, axis=0)
            ride = jnp.concatenate(
                [ride, jnp.zeros((8, columns - width), jnp.float32)], axis=1
            )
            ranks = columns // PIECE
            place = place_of(relative, ranks, shards)
            for j in range(ranks):
                cols = slice(j * PIECE, (j + 1) * PIECE)
                for f in range(shards):
                    weights_ref[place(f, j), 0] = low(
                        jnp.concatenate(
                            [value[f * rows : (f + 1) * rows, cols], ride[:, cols]], axis=0
                        )
                    )

    if shards is None:
        shape = (1, width, columns)
    else:
        shape = (columns // PIECE * shards, 1, width // shards + extra_rows, PIECE)
    inputs = (cosine, sine, hidden, normed, gains, weights, out_grad, mid, *d_queries)
    inputs = (*inputs, *[x for pair in pairs for x in pair])
    if riders is not None:
        inputs = (*inputs, riders)
    return run_kernel(
        body,
        inputs,
        (
            like((tokens, width), jnp.float32),
            like((8, width), jnp.float32),
            like(shape, jnp.bfloat16),
        ),
        cost=6_000_000_000,
        name="project_back",
    )


def rope_tables(positions, head_size):
    half = head_size // 2
    freq = theta ** (-(jnp.arange(half, dtype=jnp.float32) * 2.0 / head_size))
    angle = positions.astype(jnp.float32)[..., None] * freq
    return (jnp.cos(angle), jnp.sin(angle))


def body(
    tokens,
    positions,
    query_weight,
    key_matrix,
    value_weight,
    out_weight,
    gate_weight,
    up_weight,
    down_weight,
    attn_gain,
    mlp_gain,
    cotangent,
):
    slots = lax.axis_size("ctx")
    rank = lax.axis_index("ctx")
    shard = lax.axis_index("fsdp")
    shards = lax.axis_size("fsdp")
    fast = slots == 4 and shards == 8
    tokens = swap_halves(tokens)
    positions = swap_halves(positions)
    half = tokens.shape[1] // 2
    rows = attn_gain.shape[1]
    gain_count = 2 * LAYERS
    own_gains = jnp.concatenate([attn_gain, mlp_gain])
    attn_own = [
        jnp.concatenate([query_weight[i], key_matrix[i], value_weight[i], out_weight[i]], axis=1)
        for i in range(LAYERS)
    ]
    mlp_own = [[gate_weight[i], up_weight[i]] for i in range(LAYERS)]
    if fast:
        for i in range(LAYERS):
            mlp_own[i].append(fold_down(down_weight[i]))
        ride = jnp.pad(own_gains, ((0, 8 - gain_count), (0, PIECE - rows)))
        own_first = jnp.concatenate([attn_own[0], jnp.tile(ride, (1, 4))], axis=0)[None]
        own_second = jnp.stack([*mlp_own[0], attn_own[1]])
        own_third = jnp.stack(mlp_own[1])
        first_line = gather_line(own_first)
        second_line = gather_line(own_second)
        third = gather_plain(tied(own_third, second_line))
        first_sides = gather_sides(first_line)
        first_flip = flip(own_first, "fsdp", 1)
        (first, gains), first_mine = gather_rest(
            rows, own_first, first_flip, first_line, first_sides
        )
        gains = wide(gains[:, :gain_count, :rows]).transpose(1, 0, 2).reshape(gain_count, -1)
        second_flip = flip(tied(own_second, first_mine), "fsdp", 1)
        merge = lambda x: x.reshape(x.shape[0], -1, x.shape[-1])
        attn_full = [(merge(first), 0), None]
        by_row = third.reshape(3, shards, rows, -1)
        mlp_full = [None, ((third, 0), (third, 1), (by_row, 2))]
    else:
        gains = wide(lax.all_gather(own_gains, "fsdp", axis=1, tiled=True))
        gather = lambda x: lax.all_gather(x, "fsdp", axis=0, tiled=True)
        attn_full = [gather(x) for x in attn_own]
        mlp_full = [
            (gather(gate_weight[i]), gather(up_weight[i]), gather(down_weight[i]))
            for i in range(LAYERS)
        ]
    gains = jnp.pad(gains, ((0, 8 - gain_count), (0, 0)))
    cosine, sine = rope_tables(positions[0], HD)
    cosine = jnp.concatenate([cosine] * 4, axis=1)
    sine = jnp.concatenate([-sine, sine] * 2, axis=1)
    first_row, second_row = chunks_of(rank, slots)
    offsets = jnp.arange(half, dtype=jnp.int32)
    row_index = jnp.concatenate([first_row * half + offsets, second_row * half + offsets])
    doc_start = row_index[None, :] - positions

    hidden = wide(tokens[0])
    saved = []
    for i in range(LAYERS):
        normed, q, pair = project_in(hidden, gains, i, attn_full[i], cosine, sine)
        if fast and i == 0:
            second_line, pair = lax.optimization_barrier((second_line, pair))
        kvs = [pair] + [flip(pair, "ctx", k) for k in range(1, slots)]
        if fast and i == 0:
            second_sides = gather_sides(second_line)
        attention, lse = attend(q, doc_start, kvs)
        if fast and i == 0:
            second_sides, cotangent = tied((second_sides, cotangent), attention)
            (second,), _ = gather_rest(
                rows, own_second, second_flip, second_line, second_sides
            )
            merged = merge(second)
            mlp_full[0] = ((merged, 0), (merged, 1), (second, 2))
            attn_full[1] = (merged, 3)
        middle, mixed, gate, up, inner, out = mlp(
            hidden, attention, gains, LAYERS + i, attn_full[i], *mlp_full[i]
        )
        saved.append((hidden, normed, q, kvs, attention, lse, middle, mixed, gate, up, inner))
        hidden = out
    layer_out = swap_halves(low(hidden)[None])
    grad = wide(swap_halves(cotangent)[0])

    gain_grads = {}
    mlp_grads = [None] * LAYERS
    attn_grads = [None] * LAYERS
    by_shard = shards if fast else None
    for i in reversed(range(LAYERS)):
        hidden, normed, q, kvs, attention, lse, middle, mixed, gate, up, inner = saved[i]
        d_attention, mid, gain_grads[LAYERS + i], out_grad, *weight_grads = mlp_back(
            grad,
            (middle, mixed, gate, up, inner, attention),
            gains,
            LAYERS + i,
            attn_full[i],
            *mlp_full[i],
            by_shard,
            i == 0,
        )
        if fast and i == 0:
            moved = [
                lax.dynamic_index_in_dim(early, rank ^ k, axis=0, keepdims=False)
                for k in range(4)
            ]
            weight_grads[0], moved = lax.optimization_barrier((weight_grads[0], moved))
            begun = reduce_start(weight_grads[0])
            moved = [moved[0]] + [flip(moved[k], "ctx", k) for k in (1, 2, 3)]
            early = low(sum((wide(part) for part in moved[1:]), wide(moved[0])))
            sums, sends = reduce_begin(begun, attn_begun)
            d_attention, sends, early = lax.optimization_barrier((d_attention, sends, early))
            sides = reduce_sides(sends)
        elif fast:
            early = lax.psum_scatter(
                weight_grads[0], "fsdp", scatter_dimension=0, tiled=True
            )
        else:
            mlp_grads[i] = (
                reduce_plain(weight_grads[0], 1),
                reduce_plain(weight_grads[1], 0),
            )
        d_queries, pairs = [], []
        for groups in (range(KV_HEADS - 1), range(KV_HEADS - 1, KV_HEADS)):
            d_query, *pair = attend_back(
                q, attention, d_attention, lse, doc_start, kvs, groups
            )
            d_queries.append(d_query)
            if pairs:
                pair, pairs = lax.optimization_barrier((pair, pairs))
            d_attention, pair = lax.optimization_barrier((d_attention, pair))
            pairs.append([pair[0]] + [flip(pair[k], "ctx", k) for k in range(1, slots)])
            if fast and i == 0 and groups.start == 0:
                sides = tied(sides, d_query)
                sums, sends = reduce_middle(sums, sides)
                d_attention, sends = lax.optimization_barrier((d_attention, sends))
                across = reduce_across(sends)
            elif fast and i == 0:
                sums, sends = reduce_turn(sums, tied(across, d_query))
                d_queries, sends = lax.optimization_barrier((d_queries, sends))
                line = (sums, *reduce_line(sends))
        riders = None
        if fast and i == 0:
            riders = jnp.concatenate([gain_grads[v][:1] for v in (1, 2, 3)])
        grad, gain_grads[i], attn_grad = project_back(
            d_queries,
            pairs,
            cosine,
            sine,
            (hidden, normed),
            gains,
            i,
            attn_full[i],
            out_grad,
            mid,
            by_shard,
            riders,
            True,
        )
        if fast and i == 0:
            sums, sends = reduce_begin(reduce_start(attn_grad))
            line, sends, grad, early = lax.optimization_barrier((line, sends, grad, early))
            sides = reduce_sides(sends)
            rest = low(reduce_end(line))
            sums, sends = reduce_middle(sums, sides)
            sends, rest, early = lax.optimization_barrier((sends, rest, early))
            across = reduce_across(sends)
            rest = spread_fast(rest)
            sums, sends = reduce_turn(sums, across)
            last = spread_fast(reduce_end((sums, *reduce_line(sends))))
            early = spread_fast(early)
            far = tied(flip(low(grad[half:]), "ctx", slots - 1), last)
            all_gains = lax.dynamic_slice_in_dim(last[0, rows:], shard * rows, rows, axis=1)
            order = (3, 0, 1, 2)
            all_gains = jnp.stack([all_gains[v] for v in order])
            attn_rows = jnp.stack([last[0, :rows], rest[3]])
            gate_rows = jnp.stack([rest[0], early[0]])
            up_rows = jnp.stack([rest[1], early[1]])
            down_rows = unfold_down(jnp.stack([rest[2], early[2]]))
        elif fast:
            attn_begun = reduce_start(attn_grad)
            grad, layer_out = lax.optimization_barrier((grad, layer_out))
        else:
            attn_grads[i] = reduce_plain(attn_grad[0], 0)
    if not fast:
        attn_rows = jnp.stack(attn_grads)
        gate_rows = jnp.stack([part[0][0] for part in mlp_grads])
        up_rows = jnp.stack([part[0][1] for part in mlp_grads])
        down_rows = jnp.stack([part[1] for part in mlp_grads])
        all_gains = jnp.concatenate([gain_grads[v][:1] for v in range(gain_count)])
        all_gains = lax.psum(all_gains, ("ctx", "fsdp"))
        all_gains = lax.dynamic_slice_in_dim(all_gains, shard * rows, rows, axis=1)
    if not fast:
        far = flip(low(grad[half:]), "ctx", slots - 1)
    grad = jnp.concatenate([grad[:half], wide(far)])[None]
    return (
        layer_out,
        grad,
        attn_rows[..., :QUERY],
        attn_rows[..., QUERY : QUERY + KVW],
        attn_rows[..., QUERY + KVW : QKV],
        attn_rows[..., QKV:],
        gate_rows,
        up_rows,
        down_rows,
        all_gains[:LAYERS],
        all_gains[LAYERS:],
    )


def solution(mesh):
    return jax.shard_map(
        body,
        mesh=mesh,
        in_specs=(
            P("fsdp", "ctx", None),
            P("fsdp", "ctx"),
            P(None, "fsdp", None),
            P(None, "fsdp", None),
            P(None, "fsdp", None),
            P(None, "fsdp", None),
            P(None, "fsdp", None),
            P(None, "fsdp", None),
            P(None, "fsdp", None),
            P(None, "fsdp"),
            P(None, "fsdp"),
            P("fsdp", "ctx", None),
        ),
        out_specs=(
            P("fsdp", "ctx", None),
            P("fsdp", "ctx", None),
            P(None, "fsdp", None),
            P(None, "fsdp", None),
            P(None, "fsdp", None),
            P(None, "fsdp", None),
            P(None, "fsdp", None),
            P(None, "fsdp", None),
            P(None, "fsdp", None),
            P(None, "fsdp"),
            P(None, "fsdp"),
        ),
        check_vma=False,
    )
```

```python
import jax
import jax.numpy as jnp
from jax import lax
from jax.experimental import pallas as pl
from jax.experimental.pallas import tpu as pltpu
from jax.sharding import PartitionSpec as P

HEADS = 9
KV_HEADS = 3
HD = 64
LAYERS = 2


epsilon = 1e-05
theta = 100000.0
log_two_e = 1.4426950408889634
mask_filler = -1e30


def flip(block, axis, mask):
    route = [(i, i ^ mask) for i in range(lax.axis_size(axis))]
    return lax.ppermute(block, axis, route)


def swap_halves(x):
    half = x.shape[1] // 2
    return jnp.concatenate(
        [x[:, :half], flip(x[:, half:], "ctx", lax.axis_size("ctx") - 1)], axis=1
    )


def tied(first, *then):
    return lax.optimization_barrier((first, then))[0]


def low(x):
    return x.astype(jnp.bfloat16)


def wide(x):
    return x.astype(jnp.float32)


PIECE = 384
VMEM_LIMIT = 48 * 1024 * 1024


def fold_down(shard):
    step = shard.shape[0] // 4
    pieces = []
    for j in range(4):
        rows = shard[j * step : (j + 1) * step]
        rest = rows[:, PIECE:]
        rest = jnp.concatenate([rest[: step // 2], rest[step // 2 :]], axis=1)
        pieces.append(jnp.concatenate([rows[:, :PIECE], rest], axis=0))
    return jnp.concatenate(pieces, axis=1)


def unfold_down(folded):
    step = folded.shape[-2] * 2 // 3
    pieces = []
    for piece in jnp.split(folded, 4, axis=-1):
        rest = piece[..., step:, :]
        rest = jnp.concatenate(jnp.split(rest, 2, axis=-1), axis=-2)
        pieces.append(jnp.concatenate([piece[..., :step, :], rest], axis=-1))
    return jnp.concatenate(pieces, axis=-2)


def assemble_kernel(rows, own, own_flip, mine, theirs, out, *rest):
    sems = rest[-1]
    j = lax.axis_index("ctx")
    f = lax.axis_index("fsdp")
    copies = []

    def copy(src, dst):
        made = pltpu.make_async_copy(src, dst, sems.at[len(copies)])
        made.start()
        copies.append(made)

    for core, shard in ((0, own), (1, own_flip)):
        copy(shard.at[:, :rows], out.at[:, f ^ core])
        if len(rest) > 1:
            copy(shard.at[0, rows:, :PIECE], rest[0].at[f ^ core])
    for core, pieces in ((0, mine), (1, theirs)):
        for jrel in range(4):
            for zrel in range(1, 4):
                row = f ^ (core + 2 * zrel)
                column = pl.multiple_of((j ^ jrel) * PIECE, 128)
                piece = pieces.at[jrel * 3 + zrel - 1]
                copy(piece.at[:, :rows], out.at[:, row, :, pl.ds(column, PIECE)])
                if jrel == 0 and len(rest) > 1:
                    copy(piece.at[0, rows:], rest[0].at[row])
    for made in copies:
        made.wait()


def assemble(rows, own, own_flip, mine, theirs):
    count, all_rows, columns = own.shape
    fsdp = lax.axis_size("fsdp")
    shapes = [jax.ShapeDtypeStruct((count, fsdp, rows, columns), own.dtype)]
    if all_rows > rows:
        shapes.append(jax.ShapeDtypeStruct((fsdp, all_rows - rows, PIECE), own.dtype))
    return pl.pallas_call(
        lambda *refs: assemble_kernel(rows, *refs),
        out_shape=tuple(shapes),
        in_specs=[pl.BlockSpec(memory_space=pl.ANY)] * 4,
        out_specs=[pl.BlockSpec(memory_space=pltpu.VMEM)] * len(shapes),
        scratch_shapes=[pltpu.SemaphoreType.DMA((34,))],
        compiler_params=pltpu.CompilerParams(vmem_limit_bytes=VMEM_LIMIT),
        name="assemble",
    )(own, own_flip, mine, theirs)


def gather_line(own):
    j = lax.axis_index("ctx")
    piece = lax.dynamic_slice_in_dim(own, j * PIECE, PIECE, axis=2)
    return jnp.stack([flip(piece, "fsdp", 2 * k) for k in (1, 2, 3)])


def gather_sides(line):
    return flip(line, "ctx", 1), flip(line, "ctx", 2)


def gather_rest(rows, own, own_flip, line, sides):
    by_x, by_y = sides
    diag = jnp.concatenate([flip(by_x[:2], "ctx", 2), flip(by_y[2:], "ctx", 1)])
    mine = jnp.concatenate([line, by_x, by_y, diag])
    theirs = flip(mine, "fsdp", 1)
    return assemble(rows, own, own_flip, mine, theirs), mine


def gather_plain(own):
    return lax.all_gather(own, "fsdp", axis=1, tiled=True)


def reduce_start(whole):
    by_core = whole.reshape(2, 4, 4, *whole.shape[1:])
    return by_core[0], flip(by_core[1], "fsdp", 1)


def reduce_begin(*halves):
    total = jnp.concatenate([wide(keep) + wide(other) for keep, other in halves], axis=2)
    a = low(total[:, :2])
    b = low(total[:, 2:])
    return (a[0], a[2], b[0], b[1]), (jnp.stack([a[1], a[3]]), jnp.stack([b[2], b[3]]))


def reduce_sides(sends):
    return flip(sends[0], "ctx", 1), flip(sends[1], "ctx", 2)


def reduce_middle(sums, sides):
    a0, a2, b0, b1 = (wide(part) for part in sums)
    x1, y1 = wide(sides[0]), wide(sides[1])
    return (a0 + x1[0], b0 + y1[0]), (low(a2 + x1[1]), low(b1 + y1[1]))


def reduce_across(sends):
    return flip(sends[0], "ctx", 2), flip(sends[1], "ctx", 1)


def reduce_turn(sums, across):
    a0 = sums[0] + wide(across[0])
    b0 = sums[1] + wide(across[1])
    return a0[0], (low(a0[1]), low(b0[0]), low(b0[1]))


def reduce_line(sends):
    return [flip(part, "fsdp", 2 * k + 2) for k, part in enumerate(sends)]


def reduce_end(line):
    return line[0] + sum(wide(part) for part in line[1:])


def spread_fast(piece):
    j = lax.axis_index("ctx")
    own = low(piece)
    parts = [own] + [flip(own, "ctx", k) for k in (1, 2, 3)]
    for bit in (1, 2):
        odd = (j & bit) != 0
        parts = [jnp.where(odd, parts[i ^ bit], parts[i]) for i in range(4)]
    return wide(jnp.concatenate(parts, axis=2))


def reduce_plain(whole, dim):
    part = lax.psum_scatter(whole, "fsdp", scatter_dimension=dim, tiled=True)
    return wide(lax.psum(part, "ctx"))


def dot_nn(a, b):
    return jnp.dot(a, b, preferred_element_type=jnp.float32)


def dot_nt(a, b):
    return lax.dot_general(a, b, (((1,), (1,)), ((), ())), preferred_element_type=jnp.float32)


def dot_tn(a, b):
    return lax.dot_general(a, b, (((0,), (0,)), ((), ())), preferred_element_type=jnp.float32)


def shape_of(x):
    return x[0].shape[1:] if isinstance(x, tuple) else x.shape


def run_kernel(body, inputs, outputs, scratch=(), cost=0, name=None):
    count = len(inputs)
    arrays = [x[0] if isinstance(x, tuple) else x for x in inputs]

    def kernel(*refs):
        sources = refs[:count]
        outs = refs[count : count + len(outputs)]
        rest = refs[count + len(outputs) :]
        buffers, extra, sems = rest[:count], rest[count:-1], rest[-1]
        copies = [
            pltpu.make_async_copy(
                source.at[x[1]] if isinstance(x, tuple) else source, buffer, sems.at[i]
            )
            for i, (x, source, buffer) in enumerate(zip(inputs, sources, buffers))
        ]
        for copy in copies:
            copy.start()
        waited = set()

        def get(i):
            if i not in waited:
                waited.add(i)
                copies[i].wait()
            return buffers[i]

        body(get, outs, extra)
        for i in range(count):
            get(i)

    return pl.pallas_call(
        kernel,
        out_shape=tuple(outputs),
        in_specs=[pl.BlockSpec(memory_space=pl.ANY)] * count,
        out_specs=[pl.BlockSpec(memory_space=pltpu.VMEM)] * len(outputs),
        scratch_shapes=[
            *[pltpu.VMEM(shape_of(x), array.dtype) for x, array in zip(inputs, arrays)],
            *scratch,
            pltpu.SemaphoreType.DMA((count,)),
        ],
        compiler_params=pltpu.CompilerParams(vmem_limit_bytes=VMEM_LIMIT),
        cost_estimate=pl.CostEstimate(flops=cost, bytes_accessed=4_000_000, transcendentals=0),
        name=name,
    )(*arrays)


def like(shape, kind):
    return jax.ShapeDtypeStruct(shape, kind)


def chunks_of(source, slots):
    return (2 * source, 2 * slots - 1 - 2 * source)


def stack_heads(ref, dst, half, groups=range(KV_HEADS)):
    group = HEADS // KV_HEADS
    for g in groups:
        for part in range(2):
            for i in range(group):
                h = g * group + i
                dst[g, part, i * half : (i + 1) * half] = ref[
                    part * half : (part + 1) * half, h * HD : (h + 1) * HD
                ]


def thrice(row):
    return jnp.concatenate([row] * (HEADS // KV_HEADS), axis=1)


def attend_kernel(slots, *refs):
    q_ref, start_ref = refs[:2]
    kv_refs = refs[2 : 2 + slots]
    o_ref, lse_ref, qs, ks, vt, top_s, acc_s, ot = refs[2 + slots :]
    rank = lax.axis_index("ctx")
    half = q_ref.shape[0] // 2
    group = HEADS // KV_HEADS
    wide_cols = group * half
    stack_heads(q_ref, qs, half)
    ones = jnp.ones((16, half), jnp.bfloat16)
    for k in range(slots):
        values_t = low(jnp.transpose(wide(kv_refs[k][:, 128:])))
        for g in range(KV_HEADS):
            row = KV_HEADS * HD - 128 + g * HD
            for part in range(2):
                rows = slice(part * half, (part + 1) * half)
                ks[k, g, part] = kv_refs[k][rows, g * HD : (g + 1) * HD]
                vt[k, g, part, :HD] = values_t[row : row + HD, rows]
                vt[k, g, part, HD:] = ones
    lse_ref[...] = jnp.zeros_like(lse_ref)
    mine = chunks_of(rank, slots)

    def one_group(g, carry):
        for part in range(2):
            cols = slice(part * half, (part + 1) * half)
            start = thrice(start_ref[:, cols])
            q = qs[g, part]

            def scores(k, other, first):
                s = dot_nt(ks[k, g, other], q)
                key = lax.broadcasted_iota(jnp.int32, s.shape, 0)
                visible = key >= start - first
                return s, key, visible

            s, key, visible = scores(0, part, mine[part] * half)
            query = thrice(lax.broadcasted_iota(jnp.int32, (half, half), 1))
            s = jnp.where(visible & (key <= query), s, mask_filler)
            top = jnp.floor(jnp.max(s, axis=0, keepdims=True))
            top_s[...] = top
            acc_s[...] = dot_nn(vt[0, g, part], low(jnp.exp2(s - top)))

            def tile(k, other, chunk):
                @pl.when(chunk < mine[part])
                def _():
                    s, _, visible = scores(k, other, chunk * half)
                    s = jnp.where(visible, s, mask_filler)
                    old = top_s[...]
                    top = jnp.maximum(old, jnp.floor(jnp.max(s, axis=0, keepdims=True)))
                    top_s[...] = top
                    acc_s[...] = acc_s[...] * jnp.exp2(old - top) + dot_nn(
                        vt[k, g, other], low(jnp.exp2(s - top))
                    )

            tile(0, 1 - part, mine[1 - part])

            def slot(k, carry):
                theirs = chunks_of(rank ^ k, slots)
                for other in range(2):
                    tile(k, other, theirs[other])
                return carry

            lax.fori_loop(1, slots, slot, 0)
            total = acc_s[HD : HD + 1]
            out = acc_s[:HD] / total
            level = top_s[...] + jnp.log2(total)
            for i in range(group):
                inner = slice(i * half, (i + 1) * half)
                ot[g, i, :, cols] = out[:, inner]
                lse_ref[pl.ds(g * group + i, 1), cols] = level[:, inner]
        return carry

    lax.fori_loop(0, KV_HEADS, one_group, 0)
    o_ref[...] = low(jnp.transpose(ot[...].reshape(HEADS * HD, 2 * half)))


def attend(q, start, kvs):
    block = q.shape[0]
    half = block // 2
    slots = len(kvs)
    group = HEADS // KV_HEADS
    inputs = (q, start, *kvs)

    def body(get, outs, extra):
        attend_kernel(slots, *[get(i) for i in range(len(inputs))], *outs, *extra)

    return run_kernel(
        body,
        inputs,
        (like((block, HEADS * HD), jnp.bfloat16), like((16, block), jnp.float32)),
        scratch=(
            pltpu.VMEM((KV_HEADS, 2, group * half, HD), jnp.bfloat16),
            pltpu.VMEM((slots, KV_HEADS, 2, half, HD), jnp.bfloat16),
            pltpu.VMEM((slots, KV_HEADS, 2, HD + 16, half), jnp.bfloat16),
            pltpu.VMEM((1, group * half), jnp.float32),
            pltpu.VMEM((HD + 16, group * half), jnp.float32),
            pltpu.VMEM((KV_HEADS, group, HD, block), jnp.float32),
        ),
        cost=15_000_000_000,
        name="attend",
    )


def attend_back_kernel(slots, groups, *refs):
    q_ref, o_ref, do_ref, lse_ref, start_ref = refs[:5]
    kv_refs = refs[5 : 5 + slots]
    dq_ref = refs[5 + slots]
    dkv_refs = refs[6 + slots : 6 + 2 * slots]
    qs, dos, ks, kt, vs, dk_s, dv_s, dqt_s, delta_s, dqt_all = refs[6 + 2 * slots :]
    rank = lax.axis_index("ctx")
    half = q_ref.shape[0] // 2
    group = HEADS // KV_HEADS
    stack_heads(q_ref, qs, half, groups)
    stack_heads(do_ref, dos, half, groups)
    for k in range(slots):
        keys_t = low(jnp.transpose(wide(kv_refs[k][:, : 2 * 128])))
        for g in groups:
            for part in range(2):
                rows = slice(part * half, (part + 1) * half)
                ks[k, g, part] = kv_refs[k][rows, g * HD : (g + 1) * HD]
                kt[k, g, part] = keys_t[g * HD : (g + 1) * HD, rows]
                vs[k, g, part] = kv_refs[k][rows, (KV_HEADS + g) * HD : (KV_HEADS + g + 1) * HD]
    product = wide(do_ref[...]) * wide(o_ref[...])
    coarse = low(product)
    fine = low(product - wide(coarse))
    shape = (16, HEADS * HD)
    owner = lax.div(lax.broadcasted_iota(jnp.int32, shape, 1), HD)
    pick = jnp.where(owner == lax.broadcasted_iota(jnp.int32, shape, 0), 1.0, 0.0)
    pick = pick.astype(jnp.bfloat16)
    delta_s[...] = dot_nt(pick, coarse) + dot_nt(pick, fine)
    dk_s[...] = jnp.zeros_like(dk_s)
    dv_s[...] = jnp.zeros_like(dv_s)
    mine = chunks_of(rank, slots)

    def one_group(g, carry):
        for part in range(2):
            cols = slice(part * half, (part + 1) * half)
            start = thrice(start_ref[:, cols])
            heads = [pl.ds(g * group + i, 1) for i in range(group)]
            lse = jnp.concatenate([lse_ref[h, cols] for h in heads], axis=1)
            delta = jnp.concatenate([delta_s[h, cols] for h in heads], axis=1)

            def tile(k, other, first, diagonal):
                q = qs[g, part]
                do = dos[g, part]
                s = dot_nt(ks[k, g, other], q)
                key = lax.broadcasted_iota(jnp.int32, s.shape, 0)
                visible = key >= start - first
                if diagonal:
                    query = thrice(lax.broadcasted_iota(jnp.int32, (half, half), 1))
                    visible = visible & (key <= query)
                p = jnp.where(visible, jnp.exp2(s - lse), 0.0)
                dv = dot_nn(low(p), do)
                dp = dot_nt(vs[k, g, other], do)
                ds = low(p * (dp - delta))
                dk_s[k, g, other] += dot_nn(ds, q)
                dv_s[k, g, other] += dv
                dq = dot_nn(kt[k, g, other], ds)
                if diagonal:
                    dqt_s[...] = dq
                else:
                    dqt_s[...] += dq

            tile(0, part, mine[part] * half, True)

            @pl.when(mine[1 - part] < mine[part])
            def _():
                tile(0, 1 - part, mine[1 - part] * half, False)

            def slot(k, carry):
                theirs = chunks_of(rank ^ k, slots)
                for other in range(2):

                    @pl.when(theirs[other] < mine[part])
                    def _():
                        tile(k, other, theirs[other] * half, False)

                return carry

            lax.fori_loop(1, slots, slot, 0)
            for i in range(group):
                dqt_all[g, i, :, cols] = dqt_s[:, i * half : (i + 1) * half]
        return carry

    lax.fori_loop(groups.start, groups.stop, one_group, 0)
    dqt = dqt_all[groups.start : groups.stop]
    dq_ref[...] = jnp.transpose(dqt.reshape(len(groups) * group * HD, 2 * half)) * 0.125
    for k in range(slots):
        for part in range(2):
            dkv = jnp.concatenate(
                [
                    x
                    for g in groups
                    for x in (dk_s[k, g, part] * (1.0 / log_two_e), dv_s[k, g, part])
                ],
                axis=1,
            )
            dkv_refs[k][part * half : (part + 1) * half] = dkv.astype(dkv_refs[k].dtype)


def attend_back(q, o, do, lse, start_row, kvs, groups):
    block = q.shape[0]
    half = block // 2
    slots = len(kvs)
    group = HEADS // KV_HEADS
    inputs = (q, o, do, lse, start_row, *kvs)
    pair = lambda kind: like((block, 2 * len(groups) * HD), kind)

    def body(get, outs, extra):
        attend_back_kernel(slots, groups, *[get(i) for i in range(len(inputs))], *outs, *extra)

    return run_kernel(
        body,
        inputs,
        (
            like((block, len(groups) * group * HD), jnp.float32),
            pair(jnp.float32),
            *[pair(jnp.bfloat16)] * (slots - 1),
        ),
        scratch=(
            pltpu.VMEM((KV_HEADS, 2, group * half, HD), jnp.bfloat16),
            pltpu.VMEM((KV_HEADS, 2, group * half, HD), jnp.bfloat16),
            pltpu.VMEM((slots, KV_HEADS, 2, half, HD), jnp.bfloat16),
            pltpu.VMEM((slots, KV_HEADS, 2, HD, half), jnp.bfloat16),
            pltpu.VMEM((slots, KV_HEADS, 2, half, HD), jnp.bfloat16),
            pltpu.VMEM((slots, KV_HEADS, 2, half, HD), jnp.float32),
            pltpu.VMEM((slots, KV_HEADS, 2, half, HD), jnp.float32),
            pltpu.VMEM((HD, group * half), jnp.float32),
            pltpu.VMEM((16, block), jnp.float32),
            pltpu.VMEM((KV_HEADS, group, HD, block), jnp.float32),
        ),
        cost=7_000_000_000 * len(groups),
        name="attend_back",
    )


def scale_of(x):
    return lax.rsqrt(jnp.mean(x * x, axis=1, keepdims=True) + epsilon)


def tiled_lanes(table, columns):
    full = [table] * (columns // 128)
    if columns % 128:
        full.append(table[:, : columns % 128])
    return jnp.concatenate(full, axis=1)


def swapped(x):
    columns = x.shape[1]
    row = lax.broadcasted_iota(jnp.int32, (columns, columns), 0)
    col = lax.broadcasted_iota(jnp.int32, (columns, columns), 1)
    partner = jnp.where((col & (HD - 1)) < HD // 2, col + HD // 2, col - HD // 2)
    exchange = jnp.where(row == partner, 1.0, 0.0).astype(jnp.bfloat16)
    coarse = low(x)
    rest = x - wide(coarse)
    fine = low(rest)
    return dot_nn(coarse, exchange) + dot_nn(fine, exchange)


def turned(x, cosine, sine, sign):
    columns = x.shape[1]
    return x * tiled_lanes(cosine, columns) + swapped(x) * (sign * tiled_lanes(sine, columns))


QUERY = HEADS * HD
KVW = KV_HEADS * HD
QKV = QUERY + 2 * KVW


def project_in(hidden, gains, which, weights, cosine, sine):
    tokens, width = hidden.shape

    def body(get, outs, extra):
        normed_ref, q_ref, pair_ref = outs
        h = get(0)[...]
        normed = low(h * scale_of(h) * get(1)[which : which + 1])
        normed_ref[...] = normed
        out = dot_nn(normed, get(2)[:, :QKV])
        cos, sin = get(3)[...], get(4)[...]
        q_ref[...] = low(turned(out[:, :QUERY], cos, sin, 1.0) * (0.125 * log_two_e))
        keys = turned(out[:, QUERY : QUERY + KVW], cos, sin, 1.0)
        pair_ref[...] = low(jnp.concatenate([keys, out[:, QUERY + KVW :]], axis=1))

    return run_kernel(
        body,
        (hidden, gains, weights, cosine, sine),
        (
            like((tokens, width), jnp.bfloat16),
            like((tokens, QUERY), jnp.bfloat16),
            like((tokens, 2 * KVW), jnp.bfloat16),
        ),
        cost=4_000_000_000,
        name="project_in",
    )


def down_scratch(hidden):
    return (
        pltpu.VMEM((hidden, PIECE), jnp.bfloat16),
        pltpu.VMEM((hidden, PIECE // 2), jnp.bfloat16),
        pltpu.VMEM((hidden, PIECE // 2), jnp.float32),
    )


def open_down(down, left, right, wide_right):
    if len(down.shape) == 2:
        left[...] = down[:, :PIECE]
        right[...] = down[:, PIECE:]
        return
    shards, rows, columns = down.shape
    step = rows * 2 // 3
    for f in range(shards):
        for j in range(columns // PIECE):
            at = (f * (columns // PIECE) + j) * step
            lanes = slice(j * PIECE, (j + 1) * PIECE)
            left[at : at + step] = down[f, :step, lanes]
            rest = wide(down[f, step:, lanes])
            wide_right[at : at + step // 2] = rest[:, : PIECE // 2]
            wide_right[at + step // 2 : at + step] = rest[:, PIECE // 2 :]
    right[...] = low(wide_right[...])


def mlp(hidden, attention, gains, which, attn_weights, gate_w, up_w, down_w):
    tokens, width = hidden.shape
    ff = shape_of(gate_w)[1]
    chunk = 512

    def body(get, outs, extra):
        middle_ref, mixed_ref, gate_ref, up_ref, inner_ref, out_ref = outs
        left, right, wide_right = extra
        middle = get(0)[...] + dot_nn(get(1)[...], get(3)[:, QKV:])
        middle_ref[...] = middle
        mixed = low(middle * scale_of(middle) * get(2)[which : which + 1])
        mixed_ref[...] = mixed
        open_down(get(6), left, right, wide_right)
        gate_weight, up_weight = get(4), get(5)
        sums = [0.0, 0.0]
        for c in range(ff // chunk):
            cols = slice(c * chunk, (c + 1) * chunk)
            gate = dot_nn(mixed, gate_weight[:, cols])
            up = dot_nn(mixed, up_weight[:, cols])
            gate_ref[:, cols] = low(gate)
            up_ref[:, cols] = low(up)
            inner = low(gate * jax.nn.sigmoid(gate) * up)
            inner_ref[:, cols] = inner
            sums[0] = sums[0] + dot_nn(inner, left[cols])
            sums[1] = sums[1] + dot_nn(inner, right[cols])
        out_ref[...] = middle + jnp.concatenate(sums, axis=1)

    return run_kernel(
        body,
        (hidden, attention, gains, attn_weights, gate_w, up_w, down_w),
        (
            like((tokens, width), jnp.float32),
            like((tokens, width), jnp.bfloat16),
            like((tokens, ff), jnp.bfloat16),
            like((tokens, ff), jnp.bfloat16),
            like((tokens, ff), jnp.bfloat16),
            like((tokens, width), jnp.float32),
        ),
        scratch=down_scratch(ff),
        cost=8_000_000_000,
        name="mlp",
    )


def norm_back(x, gain, grad):
    scale = scale_of(x)
    unit = x * scale
    e = grad * gain
    dx = scale * (e - unit * jnp.mean(e * unit, axis=1, keepdims=True))
    return dx, jnp.sum(grad * unit, axis=0, keepdims=True)


def place_of(relative, ranks, shards):
    if not relative:
        return lambda f, j: f * ranks + j
    me, rank = lax.axis_index("fsdp"), lax.axis_index("ctx")

    def place(f, j):
        apart = f ^ me
        return (apart & 1) * (ranks * shards // 2) + (j ^ rank) * (shards // 2) + (apart >> 1)

    return place


def put_rows(ref, index, value, shards, place):
    if shards is None:
        ref[index] = low(value)
        return
    rows = value.shape[0] // shards
    ranks = value.shape[1] // PIECE
    for j in range(ranks):
        for f in range(shards):
            ref[place(f, j), index] = low(
                value[f * rows : (f + 1) * rows, j * PIECE : (j + 1) * PIECE]
            )


def mlp_back(grad, kept, gains, which, attn_weights, gate_w, up_w, down_w, shards, relative):
    middle, mixed, gate, up, inner, attention = kept
    tokens, width = grad.shape
    ff = shape_of(gate_w)[1]
    chunk = 512

    def body(get, outs, extra):
        datt_ref, mid_ref, gain_ref, out_grad_ref, weights_ref = outs[:5]
        left, right, wide_right, grad_s, total = extra
        place = None if shards is None else place_of(relative, ff // PIECE, shards)
        open_down(get(11), left, right, wide_right)
        grad = get(0)[...]
        grad_low = low(grad)
        mixed_t = low(jnp.transpose(wide(get(2)[...])))
        d_mixed = 0.0
        for c in range(ff // chunk):
            cols = slice(c * chunk, (c + 1) * chunk)
            d_inner = dot_nt(grad_low[:, :PIECE], left[cols]) + dot_nt(
                grad_low[:, PIECE:], right[cols]
            )
            g = wide(get(3)[:, cols])
            sig = jax.nn.sigmoid(g)
            d_gate = low(d_inner * wide(get(4)[:, cols]) * (sig * (1.0 + g * (1.0 - sig))))
            d_up = low(d_inner * (g * sig))
            grad_s[0, :, cols] = dot_nn(mixed_t, d_gate)
            grad_s[1, :, cols] = dot_nn(mixed_t, d_up)
            part = dot_nt(d_gate, get(9)[:, cols]) + dot_nt(d_up, get(10)[:, cols])
            d_mixed = part + d_mixed
            d_down = dot_tn(get(5)[:, cols], grad_low)
            if shards is None:
                outs[5][cols] = low(d_down)
            else:
                total[cols] = d_down
        for index in range(2):
            put_rows(weights_ref, index, grad_s[index], shards, place)
        if shards is not None:
            rows = width // shards
            step = rows * 2 // 3
            ranks = ff // PIECE
            for f in range(shards):
                for j in range(ranks):
                    at = (f * ranks + j) * step
                    rest = total[at : at + step, PIECE:]
                    value = jnp.concatenate(
                        [
                            total[at : at + step, :PIECE],
                            jnp.concatenate([rest[: step // 2], rest[step // 2 :]], axis=1),
                        ],
                        axis=0,
                    )
                    weights_ref[place(f, j), 2] = low(value)
        dx, gain_grad = norm_back(get(1)[...], get(7)[which : which + 1], d_mixed)
        gain_ref[...] = jnp.broadcast_to(gain_grad, gain_ref.shape)
        mid = grad + dx
        mid_ref[...] = mid
        mid_low = low(mid)
        out_grad_ref[...] = low(dot_tn(get(6)[...], mid_low))
        datt_ref[...] = low(dot_nt(mid_low, get(8)[:, QKV:]))

    if shards is None:
        weight_outs = (like((2, width, ff), jnp.bfloat16), like((ff, width), jnp.bfloat16))
    else:
        weight_outs = (like((ff // PIECE * shards, 3, width // shards, PIECE), jnp.bfloat16),)
    return run_kernel(
        body,
        (
            grad, middle, mixed, gate, up, inner, attention, gains,
            attn_weights, gate_w, up_w, down_w,
        ),
        (
            like((tokens, width), jnp.bfloat16),
            like((tokens, width), jnp.float32),
            like((8, width), jnp.float32),
            like((width, width), jnp.bfloat16),
            *weight_outs,
        ),
        scratch=(
            *down_scratch(ff),
            pltpu.VMEM((2, width, ff), jnp.float32),
            pltpu.VMEM((ff, width), jnp.float32),
        ),
        cost=15_000_000_000,
        name="mlp_back",
    )


def project_back(d_queries, pairs, cosine, sine, kept, gains, which, weights, out_grad, mid, shards, riders, relative):
    hidden, normed = kept
    tokens, width = hidden.shape
    parts = len(d_queries)
    slots = len(pairs[0])
    fixed = 8 + parts
    pair_at = lambda part, k: fixed + part * slots + k
    columns = shape_of(weights)[1]
    extra_rows = 0 if riders is None else 8

    def body(get, outs, extra):
        grad_ref, gain_ref, weights_ref = outs
        cos, sin = get(0)[...], get(1)[...]
        d_query = jnp.concatenate([get(8 + part)[...] for part in range(parts)], axis=1)
        dq = turned(d_query, cos, sin, -1.0)
        keys, values = [], []
        for part in range(parts):
            pair = get(pair_at(part, 0))[...]
            for k in range(1, slots):
                pair = pair + wide(get(pair_at(part, k))[...])
            for at in range(0, pair.shape[1], 2 * HD):
                keys.append(pair[:, at : at + HD])
                values.append(pair[:, at + HD : at + 2 * HD])
        dk = turned(jnp.concatenate(keys, axis=1), cos, sin, -1.0)
        d_all = low(jnp.concatenate([dq, dk, *values], axis=1))
        normed_grad = dot_nt(d_all, get(5)[:, :QKV])
        dx, gain_grad = norm_back(get(2)[...], get(4)[which : which + 1], normed_grad)
        gain_ref[...] = jnp.broadcast_to(gain_grad, gain_ref.shape)
        grad_ref[...] = get(7)[...] + dx
        d_weights = dot_tn(get(3)[...], d_all)
        value = jnp.concatenate([d_weights, wide(get(6)[...])], axis=1)
        if riders is None:
            place = None if shards is None else place_of(relative, columns // PIECE, shards)
            put_rows(weights_ref, 0, value, shards, place)
        else:
            rows = width // shards
            lines = [get(fixed + parts * slots)[...], gain_grad]
            lines.append(jnp.zeros((8 - 1 - lines[0].shape[0], width), jnp.float32))
            ride = jnp.concatenate(lines, axis=0)
            ride = jnp.concatenate(
                [ride, jnp.zeros((8, columns - width), jnp.float32)], axis=1
            )
            ranks = columns // PIECE
            place = place_of(relative, ranks, shards)
            for j in range(ranks):
                cols = slice(j * PIECE, (j + 1) * PIECE)
                for f in range(shards):
                    weights_ref[place(f, j), 0] = low(
                        jnp.concatenate(
                            [value[f * rows : (f + 1) * rows, cols], ride[:, cols]], axis=0
                        )
                    )

    if shards is None:
        shape = (1, width, columns)
    else:
        shape = (columns // PIECE * shards, 1, width // shards + extra_rows, PIECE)
    inputs = (cosine, sine, hidden, normed, gains, weights, out_grad, mid, *d_queries)
    inputs = (*inputs, *[x for pair in pairs for x in pair])
    if riders is not None:
        inputs = (*inputs, riders)
    return run_kernel(
        body,
        inputs,
        (
            like((tokens, width), jnp.float32),
            like((8, width), jnp.float32),
            like(shape, jnp.bfloat16),
        ),
        cost=6_000_000_000,
        name="project_back",
    )


def rope_tables(positions, head_size):
    half = head_size // 2
    freq = theta ** (-(jnp.arange(half, dtype=jnp.float32) * 2.0 / head_size))
    angle = positions.astype(jnp.float32)[..., None] * freq
    return (jnp.cos(angle), jnp.sin(angle))


def body(
    tokens,
    positions,
    query_weight,
    key_matrix,
    value_weight,
    out_weight,
    gate_weight,
    up_weight,
    down_weight,
    attn_gain,
    mlp_gain,
    cotangent,
):
    slots = lax.axis_size("ctx")
    rank = lax.axis_index("ctx")
    shard = lax.axis_index("fsdp")
    shards = lax.axis_size("fsdp")
    fast = slots == 4 and shards == 8
    tokens = swap_halves(tokens)
    positions = swap_halves(positions)
    half = tokens.shape[1] // 2
    rows = attn_gain.shape[1]
    gain_count = 2 * LAYERS
    own_gains = jnp.concatenate([attn_gain, mlp_gain])
    attn_own = [
        jnp.concatenate([query_weight[i], key_matrix[i], value_weight[i], out_weight[i]], axis=1)
        for i in range(LAYERS)
    ]
    mlp_own = [[gate_weight[i], up_weight[i]] for i in range(LAYERS)]
    if fast:
        for i in range(LAYERS):
            mlp_own[i].append(fold_down(down_weight[i]))
        ride = jnp.pad(own_gains, ((0, 8 - gain_count), (0, PIECE - rows)))
        own_first = jnp.concatenate([attn_own[0], jnp.tile(ride, (1, 4))], axis=0)[None]
        own_second = jnp.stack([*mlp_own[0], attn_own[1]])
        own_third = jnp.stack(mlp_own[1])
        first_line = gather_line(own_first)
        second_line = gather_line(tied(own_second, first_line))
        third = gather_plain(tied(own_third, second_line))
        first_sides = gather_sides(first_line)
        first_flip = flip(own_first, "fsdp", 1)
        (first, gains), first_mine = gather_rest(
            rows, own_first, first_flip, first_line, first_sides
        )
        gains = wide(gains[:, :gain_count, :rows]).transpose(1, 0, 2).reshape(gain_count, -1)
        second_flip = flip(tied(own_second, first_mine), "fsdp", 1)
        merge = lambda x: x.reshape(x.shape[0], -1, x.shape[-1])
        attn_full = [(merge(first), 0), None]
        by_row = third.reshape(3, shards, rows, -1)
        mlp_full = [None, ((third, 0), (third, 1), (by_row, 2))]
    else:
        gains = wide(lax.all_gather(own_gains, "fsdp", axis=1, tiled=True))
        gather = lambda x: lax.all_gather(x, "fsdp", axis=0, tiled=True)
        attn_full = [gather(x) for x in attn_own]
        mlp_full = [
            (gather(gate_weight[i]), gather(up_weight[i]), gather(down_weight[i]))
            for i in range(LAYERS)
        ]
    gains = jnp.pad(gains, ((0, 8 - gain_count), (0, 0)))
    cosine, sine = rope_tables(positions[0], HD)
    cosine = jnp.concatenate([cosine] * 4, axis=1)
    sine = jnp.concatenate([-sine, sine] * 2, axis=1)
    first_row, second_row = chunks_of(rank, slots)
    offsets = jnp.arange(half, dtype=jnp.int32)
    row_index = jnp.concatenate([first_row * half + offsets, second_row * half + offsets])
    doc_start = row_index[None, :] - positions

    hidden = wide(tokens[0])
    saved = []
    for i in range(LAYERS):
        normed, q, pair = project_in(hidden, gains, i, attn_full[i], cosine, sine)
        if fast and i == 0:
            second_line, pair = lax.optimization_barrier((second_line, pair))
        kvs = [pair] + [flip(pair, "ctx", k) for k in range(1, slots)]
        if fast and i == 0:
            second_sides = gather_sides(second_line)
        attention, lse = attend(q, doc_start, kvs)
        if fast and i == 0:
            second_sides, cotangent = tied((second_sides, cotangent), attention)
            (second,), _ = gather_rest(
                rows, own_second, second_flip, second_line, second_sides
            )
            merged = merge(second)
            mlp_full[0] = ((merged, 0), (merged, 1), (second, 2))
            attn_full[1] = (merged, 3)
        middle, mixed, gate, up, inner, out = mlp(
            hidden, attention, gains, LAYERS + i, attn_full[i], *mlp_full[i]
        )
        saved.append((hidden, normed, q, kvs, attention, lse, middle, mixed, gate, up, inner))
        hidden = out
    layer_out = swap_halves(low(hidden)[None])
    grad = wide(swap_halves(cotangent)[0])

    gain_grads = {}
    mlp_grads = [None] * LAYERS
    attn_grads = [None] * LAYERS
    by_shard = shards if fast else None
    for i in reversed(range(LAYERS)):
        hidden, normed, q, kvs, attention, lse, middle, mixed, gate, up, inner = saved[i]
        d_attention, mid, gain_grads[LAYERS + i], out_grad, *weight_grads = mlp_back(
            grad,
            (middle, mixed, gate, up, inner, attention),
            gains,
            LAYERS + i,
            attn_full[i],
            *mlp_full[i],
            by_shard,
            i == 0,
        )
        if fast and i == 0:
            moved = [
                lax.dynamic_index_in_dim(early, rank ^ k, axis=0, keepdims=False)
                for k in range(4)
            ]
            weight_grads[0], moved = lax.optimization_barrier((weight_grads[0], moved))
            begun = reduce_start(weight_grads[0])
            moved = [moved[0]] + [flip(moved[k], "ctx", k) for k in (1, 2, 3)]
            early = low(sum((wide(part) for part in moved[1:]), wide(moved[0])))
            sums, sends = reduce_begin(begun, attn_begun)
            d_attention, sends, early = lax.optimization_barrier((d_attention, sends, early))
            sides = reduce_sides(sends)
        elif fast:
            early = lax.psum_scatter(
                weight_grads[0], "fsdp", scatter_dimension=0, tiled=True
            )
        else:
            mlp_grads[i] = (
                reduce_plain(weight_grads[0], 1),
                reduce_plain(weight_grads[1], 0),
            )
        d_queries, pairs = [], []
        for groups in (range(KV_HEADS - 1), range(KV_HEADS - 1, KV_HEADS)):
            d_query, *pair = attend_back(
                q, attention, d_attention, lse, doc_start, kvs, groups
            )
            d_queries.append(d_query)
            if pairs:
                pair, pairs = lax.optimization_barrier((pair, pairs))
            d_attention, pair = lax.optimization_barrier((d_attention, pair))
            pairs.append([pair[0]] + [flip(pair[k], "ctx", k) for k in range(1, slots)])
            if fast and i == 0 and groups.start == 0:
                sides = tied(sides, d_query)
                sums, sends = reduce_middle(sums, sides)
                d_attention, sends = lax.optimization_barrier((d_attention, sends))
                across = reduce_across(sends)
            elif fast and i == 0:
                sums, sends = reduce_turn(sums, tied(across, d_query))
                d_queries, sends = lax.optimization_barrier((d_queries, sends))
                line = (sums, *reduce_line(sends))
        riders = None
        if fast and i == 0:
            riders = jnp.concatenate([gain_grads[v][:1] for v in (1, 2, 3)])
        grad, gain_grads[i], attn_grad = project_back(
            d_queries,
            pairs,
            cosine,
            sine,
            (hidden, normed),
            gains,
            i,
            attn_full[i],
            out_grad,
            mid,
            by_shard,
            riders,
            True,
        )
        if fast and i == 0:
            sums, sends = reduce_begin(reduce_start(attn_grad))
            sides = reduce_sides(sends)
            line = tied(line, sends)
            sums, sends = reduce_middle(sums, sides)
            across = reduce_across(sends)
            across, early = lax.optimization_barrier((across, early))
            far = flip(low(grad[half:]), "ctx", slots - 1)
            line, across, far = lax.optimization_barrier((line, across, far))
            rest = spread_fast(low(reduce_end(line)))
            sums, sends = reduce_turn(sums, across)
            last = reduce_end((sums, *reduce_line(sends)))
            last = spread_fast(last)
            early = spread_fast(early)
            all_gains = lax.dynamic_slice_in_dim(last[0, rows:], shard * rows, rows, axis=1)
            order = (3, 0, 1, 2)
            all_gains = jnp.stack([all_gains[v] for v in order])
            attn_rows = jnp.stack([last[0, :rows], rest[3]])
            gate_rows = jnp.stack([rest[0], early[0]])
            up_rows = jnp.stack([rest[1], early[1]])
            down_rows = unfold_down(jnp.stack([rest[2], early[2]]))
        elif fast:
            attn_begun = reduce_start(attn_grad)
            grad, layer_out = lax.optimization_barrier((grad, layer_out))
        else:
            attn_grads[i] = reduce_plain(attn_grad[0], 0)
    if not fast:
        attn_rows = jnp.stack(attn_grads)
        gate_rows = jnp.stack([part[0][0] for part in mlp_grads])
        up_rows = jnp.stack([part[0][1] for part in mlp_grads])
        down_rows = jnp.stack([part[1] for part in mlp_grads])
        all_gains = jnp.concatenate([gain_grads[v][:1] for v in range(gain_count)])
        all_gains = lax.psum(all_gains, ("ctx", "fsdp"))
        all_gains = lax.dynamic_slice_in_dim(all_gains, shard * rows, rows, axis=1)
    if not fast:
        far = flip(low(grad[half:]), "ctx", slots - 1)
    grad = jnp.concatenate([grad[:half], wide(far)])[None]
    return (
        layer_out,
        grad,
        attn_rows[..., :QUERY],
        attn_rows[..., QUERY : QUERY + KVW],
        attn_rows[..., QUERY + KVW : QKV],
        attn_rows[..., QKV:],
        gate_rows,
        up_rows,
        down_rows,
        all_gains[:LAYERS],
        all_gains[LAYERS:],
    )


def solution(mesh):
    return jax.shard_map(
        body,
        mesh=mesh,
        in_specs=(
            P("fsdp", "ctx", None),
            P("fsdp", "ctx"),
            P(None, "fsdp", None),
            P(None, "fsdp", None),
            P(None, "fsdp", None),
            P(None, "fsdp", None),
            P(None, "fsdp", None),
            P(None, "fsdp", None),
            P(None, "fsdp", None),
            P(None, "fsdp"),
            P(None, "fsdp"),
            P("fsdp", "ctx", None),
        ),
        out_specs=(
            P("fsdp", "ctx", None),
            P("fsdp", "ctx", None),
            P(None, "fsdp", None),
            P(None, "fsdp", None),
            P(None, "fsdp", None),
            P(None, "fsdp", None),
            P(None, "fsdp", None),
            P(None, "fsdp", None),
            P(None, "fsdp", None),
            P(None, "fsdp"),
            P(None, "fsdp"),
        ),
        check_vma=False,
    )
```

```python
import jax
import jax.numpy as jnp
from jax import lax
from jax.experimental import pallas as pl
from jax.experimental.pallas import tpu as pltpu
from jax.sharding import PartitionSpec as P

HEADS = 9
KV_HEADS = 3
HD = 64
LAYERS = 2


epsilon = 1e-05
theta = 100000.0
log_two_e = 1.4426950408889634
mask_filler = -1e30


def flip(block, axis, mask):
    route = [(i, i ^ mask) for i in range(lax.axis_size(axis))]
    return lax.ppermute(block, axis, route)


def swap_halves(x):
    half = x.shape[1] // 2
    return jnp.concatenate(
        [x[:, :half], flip(x[:, half:], "ctx", lax.axis_size("ctx") - 1)], axis=1
    )


def tied(first, *then):
    return lax.optimization_barrier((first, then))[0]


def low(x):
    return x.astype(jnp.bfloat16)


def wide(x):
    return x.astype(jnp.float32)


PIECE = 384
VMEM_LIMIT = 48 * 1024 * 1024


def fold_down(shard):
    step = shard.shape[0] // 4
    pieces = []
    for j in range(4):
        rows = shard[j * step : (j + 1) * step]
        rest = rows[:, PIECE:]
        rest = jnp.concatenate([rest[: step // 2], rest[step // 2 :]], axis=1)
        pieces.append(jnp.concatenate([rows[:, :PIECE], rest], axis=0))
    return jnp.concatenate(pieces, axis=1)


def unfold_down(folded):
    step = folded.shape[-2] * 2 // 3
    pieces = []
    for piece in jnp.split(folded, 4, axis=-1):
        rest = piece[..., step:, :]
        rest = jnp.concatenate(jnp.split(rest, 2, axis=-1), axis=-2)
        pieces.append(jnp.concatenate([piece[..., :step, :], rest], axis=-1))
    return jnp.concatenate(pieces, axis=-2)


def assemble_kernel(rows, own, own_flip, mine, theirs, out, *rest):
    sems = rest[-1]
    j = lax.axis_index("ctx")
    f = lax.axis_index("fsdp")
    copies = []

    def copy(src, dst):
        made = pltpu.make_async_copy(src, dst, sems.at[len(copies)])
        made.start()
        copies.append(made)

    for core, shard in ((0, own), (1, own_flip)):
        copy(shard.at[:, :rows], out.at[:, f ^ core])
        if len(rest) > 1:
            copy(shard.at[0, rows:, :PIECE], rest[0].at[f ^ core])
    for core, pieces in ((0, mine), (1, theirs)):
        for jrel in range(4):
            for zrel in range(1, 4):
                row = f ^ (core + 2 * zrel)
                column = pl.multiple_of((j ^ jrel) * PIECE, 128)
                piece = pieces.at[jrel * 3 + zrel - 1]
                copy(piece.at[:, :rows], out.at[:, row, :, pl.ds(column, PIECE)])
                if jrel == 0 and len(rest) > 1:
                    copy(piece.at[0, rows:], rest[0].at[row])
    for made in copies:
        made.wait()


def assemble(rows, own, own_flip, mine, theirs):
    count, all_rows, columns = own.shape
    fsdp = lax.axis_size("fsdp")
    shapes = [jax.ShapeDtypeStruct((count, fsdp, rows, columns), own.dtype)]
    if all_rows > rows:
        shapes.append(jax.ShapeDtypeStruct((fsdp, all_rows - rows, PIECE), own.dtype))
    return pl.pallas_call(
        lambda *refs: assemble_kernel(rows, *refs),
        out_shape=tuple(shapes),
        in_specs=[pl.BlockSpec(memory_space=pl.ANY)] * 4,
        out_specs=[pl.BlockSpec(memory_space=pltpu.VMEM)] * len(shapes),
        scratch_shapes=[pltpu.SemaphoreType.DMA((34,))],
        compiler_params=pltpu.CompilerParams(vmem_limit_bytes=VMEM_LIMIT),
        name="assemble",
    )(own, own_flip, mine, theirs)


def gather_line(own):
    j = lax.axis_index("ctx")
    piece = lax.dynamic_slice_in_dim(own, j * PIECE, PIECE, axis=2)
    return jnp.stack([flip(piece, "fsdp", 2 * k) for k in (1, 2, 3)])


def gather_sides(line):
    return flip(line, "ctx", 1), flip(line, "ctx", 2)


def gather_rest(rows, own, own_flip, line, sides):
    by_x, by_y = sides
    diag = jnp.concatenate([flip(by_x[:2], "ctx", 2), flip(by_y[2:], "ctx", 1)])
    mine = jnp.concatenate([line, by_x, by_y, diag])
    theirs = flip(mine, "fsdp", 1)
    return assemble(rows, own, own_flip, mine, theirs), mine


def gather_plain(own):
    return lax.all_gather(own, "fsdp", axis=1, tiled=True)


def reduce_start(whole):
    by_core = whole.reshape(2, 4, 4, *whole.shape[1:])
    return by_core[0], flip(by_core[1], "fsdp", 1)


def reduce_begin(*halves):
    total = jnp.concatenate([wide(keep) + wide(other) for keep, other in halves], axis=2)
    a = low(total[:, :2])
    b = low(total[:, 2:])
    return (a[0], a[2], b[0], b[1]), (jnp.stack([a[1], a[3]]), jnp.stack([b[2], b[3]]))


def reduce_sides(sends):
    return flip(sends[0], "ctx", 1), flip(sends[1], "ctx", 2)


def reduce_middle(sums, sides):
    a0, a2, b0, b1 = (wide(part) for part in sums)
    x1, y1 = wide(sides[0]), wide(sides[1])
    return (a0 + x1[0], b0 + y1[0]), (low(a2 + x1[1]), low(b1 + y1[1]))


def reduce_across(sends):
    return flip(sends[0], "ctx", 2), flip(sends[1], "ctx", 1)


def reduce_turn(sums, across):
    a0 = sums[0] + wide(across[0])
    b0 = sums[1] + wide(across[1])
    return a0[0], (low(a0[1]), low(b0[0]), low(b0[1]))


def reduce_line(sends):
    return [flip(part, "fsdp", 2 * k + 2) for k, part in enumerate(sends)]


def reduce_end(line):
    return line[0] + sum(wide(part) for part in line[1:])


def spread_fast(piece):
    j = lax.axis_index("ctx")
    own = low(piece)
    parts = [own] + [flip(own, "ctx", k) for k in (1, 2, 3)]
    for bit in (1, 2):
        odd = (j & bit) != 0
        parts = [jnp.where(odd, parts[i ^ bit], parts[i]) for i in range(4)]
    return wide(jnp.concatenate(parts, axis=2))


def reduce_plain(whole, dim):
    part = lax.psum_scatter(whole, "fsdp", scatter_dimension=dim, tiled=True)
    return wide(lax.psum(part, "ctx"))


def dot_nn(a, b):
    return jnp.dot(a, b, preferred_element_type=jnp.float32)


def dot_nt(a, b):
    return lax.dot_general(a, b, (((1,), (1,)), ((), ())), preferred_element_type=jnp.float32)


def dot_tn(a, b):
    return lax.dot_general(a, b, (((0,), (0,)), ((), ())), preferred_element_type=jnp.float32)


def shape_of(x):
    return x[0].shape[1:] if isinstance(x, tuple) else x.shape


def run_kernel(body, inputs, outputs, scratch=(), cost=0, name=None):
    count = len(inputs)
    arrays = [x[0] if isinstance(x, tuple) else x for x in inputs]

    def kernel(*refs):
        sources = refs[:count]
        outs = refs[count : count + len(outputs)]
        rest = refs[count + len(outputs) :]
        buffers, extra, sems = rest[:count], rest[count:-1], rest[-1]
        copies = [
            pltpu.make_async_copy(
                source.at[x[1]] if isinstance(x, tuple) else source, buffer, sems.at[i]
            )
            for i, (x, source, buffer) in enumerate(zip(inputs, sources, buffers))
        ]
        for copy in copies:
            copy.start()
        waited = set()

        def get(i):
            if i not in waited:
                waited.add(i)
                copies[i].wait()
            return buffers[i]

        body(get, outs, extra)
        for i in range(count):
            get(i)

    return pl.pallas_call(
        kernel,
        out_shape=tuple(outputs),
        in_specs=[pl.BlockSpec(memory_space=pl.ANY)] * count,
        out_specs=[pl.BlockSpec(memory_space=pltpu.VMEM)] * len(outputs),
        scratch_shapes=[
            *[pltpu.VMEM(shape_of(x), array.dtype) for x, array in zip(inputs, arrays)],
            *scratch,
            pltpu.SemaphoreType.DMA((count,)),
        ],
        compiler_params=pltpu.CompilerParams(vmem_limit_bytes=VMEM_LIMIT),
        cost_estimate=pl.CostEstimate(flops=cost, bytes_accessed=4_000_000, transcendentals=0),
        name=name,
    )(*arrays)


def like(shape, kind):
    return jax.ShapeDtypeStruct(shape, kind)


def chunks_of(source, slots):
    return (2 * source, 2 * slots - 1 - 2 * source)


def stack_heads(ref, dst, half, groups=range(KV_HEADS)):
    group = HEADS // KV_HEADS
    for g in groups:
        for part in range(2):
            for i in range(group):
                h = g * group + i
                dst[g, part, i * half : (i + 1) * half] = ref[
                    part * half : (part + 1) * half, h * HD : (h + 1) * HD
                ]


def thrice(row):
    return jnp.concatenate([row] * (HEADS // KV_HEADS), axis=1)


def attend_kernel(slots, *refs):
    q_ref, start_ref = refs[:2]
    kv_refs = refs[2 : 2 + slots]
    o_ref, lse_ref, qs, ks, vt, top_s, acc_s, ot = refs[2 + slots :]
    rank = lax.axis_index("ctx")
    half = q_ref.shape[0] // 2
    group = HEADS // KV_HEADS
    wide_cols = group * half
    stack_heads(q_ref, qs, half)
    ones = jnp.ones((16, half), jnp.bfloat16)
    for k in range(slots):
        values_t = low(jnp.transpose(wide(kv_refs[k][:, 128:])))
        for g in range(KV_HEADS):
            row = KV_HEADS * HD - 128 + g * HD
            for part in range(2):
                rows = slice(part * half, (part + 1) * half)
                ks[k, g, part] = kv_refs[k][rows, g * HD : (g + 1) * HD]
                vt[k, g, part, :HD] = values_t[row : row + HD, rows]
                vt[k, g, part, HD:] = ones
    lse_ref[...] = jnp.zeros_like(lse_ref)
    mine = chunks_of(rank, slots)

    def one_group(g, carry):
        for part in range(2):
            cols = slice(part * half, (part + 1) * half)
            start = thrice(start_ref[:, cols])
            q = qs[g, part]

            def scores(k, other, first):
                s = dot_nt(ks[k, g, other], q)
                key = lax.broadcasted_iota(jnp.int32, s.shape, 0)
                visible = key >= start - first
                return s, key, visible

            s, key, visible = scores(0, part, mine[part] * half)
            query = thrice(lax.broadcasted_iota(jnp.int32, (half, half), 1))
            s = jnp.where(visible & (key <= query), s, mask_filler)
            top = jnp.floor(jnp.max(s, axis=0, keepdims=True))
            top_s[...] = top
            acc_s[...] = dot_nn(vt[0, g, part], low(jnp.exp2(s - top)))

            def tile(k, other, chunk):
                @pl.when(chunk < mine[part])
                def _():
                    s, _, visible = scores(k, other, chunk * half)
                    s = jnp.where(visible, s, mask_filler)
                    old = top_s[...]
                    top = jnp.maximum(old, jnp.floor(jnp.max(s, axis=0, keepdims=True)))
                    top_s[...] = top
                    acc_s[...] = acc_s[...] * jnp.exp2(old - top) + dot_nn(
                        vt[k, g, other], low(jnp.exp2(s - top))
                    )

            tile(0, 1 - part, mine[1 - part])

            def slot(k, carry):
                theirs = chunks_of(rank ^ k, slots)
                for other in range(2):
                    tile(k, other, theirs[other])
                return carry

            lax.fori_loop(1, slots, slot, 0)
            total = acc_s[HD : HD + 1]
            out = acc_s[:HD] / total
            level = top_s[...] + jnp.log2(total)
            for i in range(group):
                inner = slice(i * half, (i + 1) * half)
                ot[g, i, :, cols] = out[:, inner]
                lse_ref[pl.ds(g * group + i, 1), cols] = level[:, inner]
        return carry

    lax.fori_loop(0, KV_HEADS, one_group, 0)
    o_ref[...] = low(jnp.transpose(ot[...].reshape(HEADS * HD, 2 * half)))


def attend(q, start, kvs):
    block = q.shape[0]
    half = block // 2
    slots = len(kvs)
    group = HEADS // KV_HEADS
    inputs = (q, start, *kvs)

    def body(get, outs, extra):
        attend_kernel(slots, *[get(i) for i in range(len(inputs))], *outs, *extra)

    return run_kernel(
        body,
        inputs,
        (like((block, HEADS * HD), jnp.bfloat16), like((16, block), jnp.float32)),
        scratch=(
            pltpu.VMEM((KV_HEADS, 2, group * half, HD), jnp.bfloat16),
            pltpu.VMEM((slots, KV_HEADS, 2, half, HD), jnp.bfloat16),
            pltpu.VMEM((slots, KV_HEADS, 2, HD + 16, half), jnp.bfloat16),
            pltpu.VMEM((1, group * half), jnp.float32),
            pltpu.VMEM((HD + 16, group * half), jnp.float32),
            pltpu.VMEM((KV_HEADS, group, HD, block), jnp.float32),
        ),
        cost=15_000_000_000,
        name="attend",
    )


def attend_back_kernel(slots, groups, *refs):
    q_ref, o_ref, do_ref, lse_ref, start_ref = refs[:5]
    kv_refs = refs[5 : 5 + slots]
    dq_ref = refs[5 + slots]
    dkv_refs = refs[6 + slots : 6 + 2 * slots]
    qs, dos, ks, kt, vs, dk_s, dv_s, dqt_s, delta_s, dqt_all = refs[6 + 2 * slots :]
    rank = lax.axis_index("ctx")
    half = q_ref.shape[0] // 2
    group = HEADS // KV_HEADS
    stack_heads(q_ref, qs, half, groups)
    stack_heads(do_ref, dos, half, groups)
    for k in range(slots):
        keys_t = low(jnp.transpose(wide(kv_refs[k][:, : 2 * 128])))
        for g in groups:
            for part in range(2):
                rows = slice(part * half, (part + 1) * half)
                ks[k, g, part] = kv_refs[k][rows, g * HD : (g + 1) * HD]
                kt[k, g, part] = keys_t[g * HD : (g + 1) * HD, rows]
                vs[k, g, part] = kv_refs[k][rows, (KV_HEADS + g) * HD : (KV_HEADS + g + 1) * HD]
    product = wide(do_ref[...]) * wide(o_ref[...])
    coarse = low(product)
    fine = low(product - wide(coarse))
    shape = (16, HEADS * HD)
    owner = lax.div(lax.broadcasted_iota(jnp.int32, shape, 1), HD)
    pick = jnp.where(owner == lax.broadcasted_iota(jnp.int32, shape, 0), 1.0, 0.0)
    pick = pick.astype(jnp.bfloat16)
    delta_s[...] = dot_nt(pick, coarse) + dot_nt(pick, fine)
    dk_s[...] = jnp.zeros_like(dk_s)
    dv_s[...] = jnp.zeros_like(dv_s)
    mine = chunks_of(rank, slots)

    def one_group(g, carry):
        for part in range(2):
            cols = slice(part * half, (part + 1) * half)
            start = thrice(start_ref[:, cols])
            heads = [pl.ds(g * group + i, 1) for i in range(group)]
            lse = jnp.concatenate([lse_ref[h, cols] for h in heads], axis=1)
            delta = jnp.concatenate([delta_s[h, cols] for h in heads], axis=1)

            def tile(k, other, first, diagonal):
                q = qs[g, part]
                do = dos[g, part]
                s = dot_nt(ks[k, g, other], q)
                key = lax.broadcasted_iota(jnp.int32, s.shape, 0)
                visible = key >= start - first
                if diagonal:
                    query = thrice(lax.broadcasted_iota(jnp.int32, (half, half), 1))
                    visible = visible & (key <= query)
                p = jnp.where(visible, jnp.exp2(s - lse), 0.0)
                dv = dot_nn(low(p), do)
                dp = dot_nt(vs[k, g, other], do)
                ds = low(p * (dp - delta))
                dk_s[k, g, other] += dot_nn(ds, q)
                dv_s[k, g, other] += dv
                dq = dot_nn(kt[k, g, other], ds)
                if diagonal:
                    dqt_s[...] = dq
                else:
                    dqt_s[...] += dq

            tile(0, part, mine[part] * half, True)

            @pl.when(mine[1 - part] < mine[part])
            def _():
                tile(0, 1 - part, mine[1 - part] * half, False)

            def slot(k, carry):
                theirs = chunks_of(rank ^ k, slots)
                for other in range(2):

                    @pl.when(theirs[other] < mine[part])
                    def _():
                        tile(k, other, theirs[other] * half, False)

                return carry

            lax.fori_loop(1, slots, slot, 0)
            for i in range(group):
                dqt_all[g, i, :, cols] = dqt_s[:, i * half : (i + 1) * half]
        return carry

    lax.fori_loop(groups.start, groups.stop, one_group, 0)
    dqt = dqt_all[groups.start : groups.stop]
    dq_ref[...] = jnp.transpose(dqt.reshape(len(groups) * group * HD, 2 * half)) * 0.125
    for k in range(slots):
        for part in range(2):
            dkv = jnp.concatenate(
                [
                    x
                    for g in groups
                    for x in (dk_s[k, g, part] * (1.0 / log_two_e), dv_s[k, g, part])
                ],
                axis=1,
            )
            dkv_refs[k][part * half : (part + 1) * half] = dkv.astype(dkv_refs[k].dtype)


def attend_back(q, o, do, lse, start_row, kvs, groups):
    block = q.shape[0]
    half = block // 2
    slots = len(kvs)
    group = HEADS // KV_HEADS
    inputs = (q, o, do, lse, start_row, *kvs)
    pair = lambda kind: like((block, 2 * len(groups) * HD), kind)

    def body(get, outs, extra):
        attend_back_kernel(slots, groups, *[get(i) for i in range(len(inputs))], *outs, *extra)

    return run_kernel(
        body,
        inputs,
        (
            like((block, len(groups) * group * HD), jnp.float32),
            pair(jnp.float32),
            *[pair(jnp.bfloat16)] * (slots - 1),
        ),
        scratch=(
            pltpu.VMEM((KV_HEADS, 2, group * half, HD), jnp.bfloat16),
            pltpu.VMEM((KV_HEADS, 2, group * half, HD), jnp.bfloat16),
            pltpu.VMEM((slots, KV_HEADS, 2, half, HD), jnp.bfloat16),
            pltpu.VMEM((slots, KV_HEADS, 2, HD, half), jnp.bfloat16),
            pltpu.VMEM((slots, KV_HEADS, 2, half, HD), jnp.bfloat16),
            pltpu.VMEM((slots, KV_HEADS, 2, half, HD), jnp.float32),
            pltpu.VMEM((slots, KV_HEADS, 2, half, HD), jnp.float32),
            pltpu.VMEM((HD, group * half), jnp.float32),
            pltpu.VMEM((16, block), jnp.float32),
            pltpu.VMEM((KV_HEADS, group, HD, block), jnp.float32),
        ),
        cost=7_000_000_000 * len(groups),
        name="attend_back",
    )


def scale_of(x):
    return lax.rsqrt(jnp.mean(x * x, axis=1, keepdims=True) + epsilon)


def tiled_lanes(table, columns):
    full = [table] * (columns // 128)
    if columns % 128:
        full.append(table[:, : columns % 128])
    return jnp.concatenate(full, axis=1)


def swapped(x):
    columns = x.shape[1]
    row = lax.broadcasted_iota(jnp.int32, (columns, columns), 0)
    col = lax.broadcasted_iota(jnp.int32, (columns, columns), 1)
    partner = jnp.where((col & (HD - 1)) < HD // 2, col + HD // 2, col - HD // 2)
    exchange = jnp.where(row == partner, 1.0, 0.0).astype(jnp.bfloat16)
    coarse = low(x)
    rest = x - wide(coarse)
    fine = low(rest)
    return dot_nn(coarse, exchange) + dot_nn(fine, exchange)


def turned(x, cosine, sine, sign):
    columns = x.shape[1]
    return x * tiled_lanes(cosine, columns) + swapped(x) * (sign * tiled_lanes(sine, columns))


QUERY = HEADS * HD
KVW = KV_HEADS * HD
QKV = QUERY + 2 * KVW


def project_in(hidden, gains, which, weights, cosine, sine):
    tokens, width = hidden.shape

    def body(get, outs, extra):
        normed_ref, q_ref, pair_ref = outs
        h = get(0)[...]
        normed = low(h * scale_of(h) * get(1)[which : which + 1])
        normed_ref[...] = normed
        out = dot_nn(normed, get(2)[:, :QKV])
        cos, sin = get(3)[...], get(4)[...]
        q_ref[...] = low(turned(out[:, :QUERY], cos, sin, 1.0) * (0.125 * log_two_e))
        keys = turned(out[:, QUERY : QUERY + KVW], cos, sin, 1.0)
        pair_ref[...] = low(jnp.concatenate([keys, out[:, QUERY + KVW :]], axis=1))

    return run_kernel(
        body,
        (hidden, gains, weights, cosine, sine),
        (
            like((tokens, width), jnp.bfloat16),
            like((tokens, QUERY), jnp.bfloat16),
            like((tokens, 2 * KVW), jnp.bfloat16),
        ),
        cost=4_000_000_000,
        name="project_in",
    )


def down_scratch(hidden):
    return (
        pltpu.VMEM((hidden, PIECE), jnp.bfloat16),
        pltpu.VMEM((hidden, PIECE // 2), jnp.bfloat16),
        pltpu.VMEM((hidden, PIECE // 2), jnp.float32),
    )


def open_down(down, left, right, wide_right):
    if len(down.shape) == 2:
        left[...] = down[:, :PIECE]
        right[...] = down[:, PIECE:]
        return
    shards, rows, columns = down.shape
    step = rows * 2 // 3
    for f in range(shards):
        for j in range(columns // PIECE):
            at = (f * (columns // PIECE) + j) * step
            lanes = slice(j * PIECE, (j + 1) * PIECE)
            left[at : at + step] = down[f, :step, lanes]
            rest = wide(down[f, step:, lanes])
            wide_right[at : at + step // 2] = rest[:, : PIECE // 2]
            wide_right[at + step // 2 : at + step] = rest[:, PIECE // 2 :]
    right[...] = low(wide_right[...])


def mlp(hidden, attention, gains, which, attn_weights, gate_w, up_w, down_w):
    tokens, width = hidden.shape
    ff = shape_of(gate_w)[1]
    chunk = 512

    def body(get, outs, extra):
        middle_ref, mixed_ref, gate_ref, up_ref, inner_ref, out_ref = outs
        left, right, wide_right = extra
        middle = get(0)[...] + dot_nn(get(1)[...], get(3)[:, QKV:])
        middle_ref[...] = middle
        mixed = low(middle * scale_of(middle) * get(2)[which : which + 1])
        mixed_ref[...] = mixed
        open_down(get(6), left, right, wide_right)
        gate_weight, up_weight = get(4), get(5)
        sums = [0.0, 0.0]
        for c in range(ff // chunk):
            cols = slice(c * chunk, (c + 1) * chunk)
            gate = dot_nn(mixed, gate_weight[:, cols])
            up = dot_nn(mixed, up_weight[:, cols])
            gate_ref[:, cols] = low(gate)
            up_ref[:, cols] = low(up)
            inner = low(gate * jax.nn.sigmoid(gate) * up)
            inner_ref[:, cols] = inner
            sums[0] = sums[0] + dot_nn(inner, left[cols])
            sums[1] = sums[1] + dot_nn(inner, right[cols])
        out_ref[...] = middle + jnp.concatenate(sums, axis=1)

    return run_kernel(
        body,
        (hidden, attention, gains, attn_weights, gate_w, up_w, down_w),
        (
            like((tokens, width), jnp.float32),
            like((tokens, width), jnp.bfloat16),
            like((tokens, ff), jnp.bfloat16),
            like((tokens, ff), jnp.bfloat16),
            like((tokens, ff), jnp.bfloat16),
            like((tokens, width), jnp.float32),
        ),
        scratch=down_scratch(ff),
        cost=8_000_000_000,
        name="mlp",
    )


def norm_back(x, gain, grad):
    scale = scale_of(x)
    unit = x * scale
    e = grad * gain
    dx = scale * (e - unit * jnp.mean(e * unit, axis=1, keepdims=True))
    return dx, jnp.sum(grad * unit, axis=0, keepdims=True)


def place_of(relative, ranks, shards):
    if not relative:
        return lambda f, j: f * ranks + j
    me, rank = lax.axis_index("fsdp"), lax.axis_index("ctx")

    def place(f, j):
        apart = f ^ me
        return (apart & 1) * (ranks * shards // 2) + (j ^ rank) * (shards // 2) + (apart >> 1)

    return place


def put_rows(ref, index, value, shards, place):
    if shards is None:
        ref[index] = low(value)
        return
    rows = value.shape[0] // shards
    ranks = value.shape[1] // PIECE
    for j in range(ranks):
        for f in range(shards):
            ref[place(f, j), index] = low(
                value[f * rows : (f + 1) * rows, j * PIECE : (j + 1) * PIECE]
            )


def mlp_back(grad, kept, gains, which, attn_weights, gate_w, up_w, down_w, shards, relative):
    middle, mixed, gate, up, inner, attention = kept
    tokens, width = grad.shape
    ff = shape_of(gate_w)[1]
    chunk = 512

    def body(get, outs, extra):
        datt_ref, mid_ref, gain_ref, out_grad_ref, weights_ref = outs[:5]
        left, right, wide_right, grad_s, total = extra
        place = None if shards is None else place_of(relative, ff // PIECE, shards)
        open_down(get(11), left, right, wide_right)
        grad = get(0)[...]
        grad_low = low(grad)
        mixed_t = low(jnp.transpose(wide(get(2)[...])))
        d_mixed = 0.0
        for c in range(ff // chunk):
            cols = slice(c * chunk, (c + 1) * chunk)
            d_inner = dot_nt(grad_low[:, :PIECE], left[cols]) + dot_nt(
                grad_low[:, PIECE:], right[cols]
            )
            g = wide(get(3)[:, cols])
            sig = jax.nn.sigmoid(g)
            d_gate = low(d_inner * wide(get(4)[:, cols]) * (sig * (1.0 + g * (1.0 - sig))))
            d_up = low(d_inner * (g * sig))
            grad_s[0, :, cols] = dot_nn(mixed_t, d_gate)
            grad_s[1, :, cols] = dot_nn(mixed_t, d_up)
            part = dot_nt(d_gate, get(9)[:, cols]) + dot_nt(d_up, get(10)[:, cols])
            d_mixed = part + d_mixed
            d_down = dot_tn(get(5)[:, cols], grad_low)
            if shards is None:
                outs[5][cols] = low(d_down)
            else:
                total[cols] = d_down
        for index in range(2):
            put_rows(weights_ref, index, grad_s[index], shards, place)
        if shards is not None:
            rows = width // shards
            step = rows * 2 // 3
            ranks = ff // PIECE
            for f in range(shards):
                for j in range(ranks):
                    at = (f * ranks + j) * step
                    rest = total[at : at + step, PIECE:]
                    value = jnp.concatenate(
                        [
                            total[at : at + step, :PIECE],
                            jnp.concatenate([rest[: step // 2], rest[step // 2 :]], axis=1),
                        ],
                        axis=0,
                    )
                    weights_ref[place(f, j), 2] = low(value)
        dx, gain_grad = norm_back(get(1)[...], get(7)[which : which + 1], d_mixed)
        gain_ref[...] = jnp.broadcast_to(gain_grad, gain_ref.shape)
        mid = grad + dx
        mid_ref[...] = mid
        mid_low = low(mid)
        out_grad_ref[...] = low(dot_tn(get(6)[...], mid_low))
        datt_ref[...] = low(dot_nt(mid_low, get(8)[:, QKV:]))

    if shards is None:
        weight_outs = (like((2, width, ff), jnp.bfloat16), like((ff, width), jnp.bfloat16))
    else:
        weight_outs = (like((ff // PIECE * shards, 3, width // shards, PIECE), jnp.bfloat16),)
    return run_kernel(
        body,
        (
            grad, middle, mixed, gate, up, inner, attention, gains,
            attn_weights, gate_w, up_w, down_w,
        ),
        (
            like((tokens, width), jnp.bfloat16),
            like((tokens, width), jnp.float32),
            like((8, width), jnp.float32),
            like((width, width), jnp.bfloat16),
            *weight_outs,
        ),
        scratch=(
            *down_scratch(ff),
            pltpu.VMEM((2, width, ff), jnp.float32),
            pltpu.VMEM((ff, width), jnp.float32),
        ),
        cost=15_000_000_000,
        name="mlp_back",
    )


def project_back(d_queries, pairs, cosine, sine, kept, gains, which, weights, out_grad, mid, shards, riders, relative):
    hidden, normed = kept
    tokens, width = hidden.shape
    parts = len(d_queries)
    slots = len(pairs[0])
    fixed = 8 + parts
    pair_at = lambda part, k: fixed + part * slots + k
    columns = shape_of(weights)[1]
    extra_rows = 0 if riders is None else 8

    def body(get, outs, extra):
        grad_ref, gain_ref, weights_ref = outs
        cos, sin = get(0)[...], get(1)[...]
        d_query = jnp.concatenate([get(8 + part)[...] for part in range(parts)], axis=1)
        dq = turned(d_query, cos, sin, -1.0)
        keys, values = [], []
        for part in range(parts):
            pair = get(pair_at(part, 0))[...]
            for k in range(1, slots):
                pair = pair + wide(get(pair_at(part, k))[...])
            for at in range(0, pair.shape[1], 2 * HD):
                keys.append(pair[:, at : at + HD])
                values.append(pair[:, at + HD : at + 2 * HD])
        dk = turned(jnp.concatenate(keys, axis=1), cos, sin, -1.0)
        d_all = low(jnp.concatenate([dq, dk, *values], axis=1))
        normed_grad = dot_nt(d_all, get(5)[:, :QKV])
        dx, gain_grad = norm_back(get(2)[...], get(4)[which : which + 1], normed_grad)
        gain_ref[...] = jnp.broadcast_to(gain_grad, gain_ref.shape)
        grad_ref[...] = get(7)[...] + dx
        d_weights = dot_tn(get(3)[...], d_all)
        value = jnp.concatenate([d_weights, wide(get(6)[...])], axis=1)
        if riders is None:
            place = None if shards is None else place_of(relative, columns // PIECE, shards)
            put_rows(weights_ref, 0, value, shards, place)
        else:
            rows = width // shards
            lines = [get(fixed + parts * slots)[...], gain_grad]
            lines.append(jnp.zeros((8 - 1 - lines[0].shape[0], width), jnp.float32))
            ride = jnp.concatenate(lines, axis=0)
            ride = jnp.concatenate(
                [ride, jnp.zeros((8, columns - width), jnp.float32)], axis=1
            )
            ranks = columns // PIECE
            place = place_of(relative, ranks, shards)
            for j in range(ranks):
                cols = slice(j * PIECE, (j + 1) * PIECE)
                for f in range(shards):
                    weights_ref[place(f, j), 0] = low(
                        jnp.concatenate(
                            [value[f * rows : (f + 1) * rows, cols], ride[:, cols]], axis=0
                        )
                    )

    if shards is None:
        shape = (1, width, columns)
    else:
        shape = (columns // PIECE * shards, 1, width // shards + extra_rows, PIECE)
    inputs = (cosine, sine, hidden, normed, gains, weights, out_grad, mid, *d_queries)
    inputs = (*inputs, *[x for pair in pairs for x in pair])
    if riders is not None:
        inputs = (*inputs, riders)
    return run_kernel(
        body,
        inputs,
        (
            like((tokens, width), jnp.float32),
            like((8, width), jnp.float32),
            like(shape, jnp.bfloat16),
        ),
        cost=6_000_000_000,
        name="project_back",
    )


def rope_tables(positions, head_size):
    half = head_size // 2
    freq = theta ** (-(jnp.arange(half, dtype=jnp.float32) * 2.0 / head_size))
    angle = positions.astype(jnp.float32)[..., None] * freq
    return (jnp.cos(angle), jnp.sin(angle))


def body(
    tokens,
    positions,
    query_weight,
    key_matrix,
    value_weight,
    out_weight,
    gate_weight,
    up_weight,
    down_weight,
    attn_gain,
    mlp_gain,
    cotangent,
):
    slots = lax.axis_size("ctx")
    rank = lax.axis_index("ctx")
    shard = lax.axis_index("fsdp")
    shards = lax.axis_size("fsdp")
    fast = slots == 4 and shards == 8
    tokens = swap_halves(tokens)
    positions = swap_halves(positions)
    half = tokens.shape[1] // 2
    rows = attn_gain.shape[1]
    gain_count = 2 * LAYERS
    own_gains = jnp.concatenate([attn_gain, mlp_gain])
    attn_own = [
        jnp.concatenate([query_weight[i], key_matrix[i], value_weight[i], out_weight[i]], axis=1)
        for i in range(LAYERS)
    ]
    mlp_own = [[gate_weight[i], up_weight[i]] for i in range(LAYERS)]
    if fast:
        for i in range(LAYERS):
            mlp_own[i].append(fold_down(down_weight[i]))
        ride = jnp.pad(own_gains, ((0, 8 - gain_count), (0, PIECE - rows)))
        own_first = jnp.concatenate([attn_own[0], jnp.tile(ride, (1, 4))], axis=0)[None]
        own_second = jnp.stack([*mlp_own[0], attn_own[1]])
        own_third = jnp.stack(mlp_own[1])
        first_line = gather_line(own_first)
        first_sides = gather_sides(first_line)
        first_sides, tokens, positions = lax.optimization_barrier(
            (first_sides, tokens, positions)
        )
        second_line = gather_line(tied(own_second, first_sides))
        third = gather_plain(tied(own_third, second_line))
        first_flip = flip(own_first, "fsdp", 1)
        (first, gains), first_mine = gather_rest(
            rows, own_first, first_flip, first_line, first_sides
        )
        gains = wide(gains[:, :gain_count, :rows]).transpose(1, 0, 2).reshape(gain_count, -1)
        second_flip = flip(tied(own_second, first_mine), "fsdp", 1)
        merge = lambda x: x.reshape(x.shape[0], -1, x.shape[-1])
        attn_full = [(merge(first), 0), None]
        by_row = third.reshape(3, shards, rows, -1)
        mlp_full = [None, ((third, 0), (third, 1), (by_row, 2))]
    else:
        gains = wide(lax.all_gather(own_gains, "fsdp", axis=1, tiled=True))
        gather = lambda x: lax.all_gather(x, "fsdp", axis=0, tiled=True)
        attn_full = [gather(x) for x in attn_own]
        mlp_full = [
            (gather(gate_weight[i]), gather(up_weight[i]), gather(down_weight[i]))
            for i in range(LAYERS)
        ]
    gains = jnp.pad(gains, ((0, 8 - gain_count), (0, 0)))
    cosine, sine = rope_tables(positions[0], HD)
    cosine = jnp.concatenate([cosine] * 4, axis=1)
    sine = jnp.concatenate([-sine, sine] * 2, axis=1)
    first_row, second_row = chunks_of(rank, slots)
    offsets = jnp.arange(half, dtype=jnp.int32)
    row_index = jnp.concatenate([first_row * half + offsets, second_row * half + offsets])
    doc_start = row_index[None, :] - positions

    hidden = wide(tokens[0])
    saved = []
    for i in range(LAYERS):
        normed, q, pair = project_in(hidden, gains, i, attn_full[i], cosine, sine)
        if fast and i == 0:
            second_line, pair = lax.optimization_barrier((second_line, pair))
        kvs = [pair] + [flip(pair, "ctx", k) for k in range(1, slots)]
        if fast and i == 0:
            second_sides = gather_sides(second_line)
        attention, lse = attend(q, doc_start, kvs)
        if fast and i == 0:
            second_sides, cotangent = tied((second_sides, cotangent), attention)
            (second,), _ = gather_rest(
                rows, own_second, second_flip, second_line, second_sides
            )
            merged = merge(second)
            mlp_full[0] = ((merged, 0), (merged, 1), (second, 2))
            attn_full[1] = (merged, 3)
        middle, mixed, gate, up, inner, out = mlp(
            hidden, attention, gains, LAYERS + i, attn_full[i], *mlp_full[i]
        )
        saved.append((hidden, normed, q, kvs, attention, lse, middle, mixed, gate, up, inner))
        hidden = out
    layer_out = swap_halves(low(hidden)[None])
    grad = wide(swap_halves(cotangent)[0])

    gain_grads = {}
    mlp_grads = [None] * LAYERS
    attn_grads = [None] * LAYERS
    by_shard = shards if fast else None
    for i in reversed(range(LAYERS)):
        hidden, normed, q, kvs, attention, lse, middle, mixed, gate, up, inner = saved[i]
        d_attention, mid, gain_grads[LAYERS + i], out_grad, *weight_grads = mlp_back(
            grad,
            (middle, mixed, gate, up, inner, attention),
            gains,
            LAYERS + i,
            attn_full[i],
            *mlp_full[i],
            by_shard,
            i == 0,
        )
        if fast and i == 0:
            moved = [
                lax.dynamic_index_in_dim(early, rank ^ k, axis=0, keepdims=False)
                for k in range(4)
            ]
            weight_grads[0], moved = lax.optimization_barrier((weight_grads[0], moved))
            begun = reduce_start(weight_grads[0])
            moved = [moved[0]] + [flip(moved[k], "ctx", k) for k in (1, 2, 3)]
            early = low(sum((wide(part) for part in moved[1:]), wide(moved[0])))
            sums, sends = reduce_begin(begun, attn_begun)
            d_attention, sends, early = lax.optimization_barrier((d_attention, sends, early))
            sides = reduce_sides(sends)
        elif fast:
            early = lax.psum_scatter(
                weight_grads[0], "fsdp", scatter_dimension=0, tiled=True
            )
        else:
            mlp_grads[i] = (
                reduce_plain(weight_grads[0], 1),
                reduce_plain(weight_grads[1], 0),
            )
        d_queries, pairs = [], []
        for groups in (range(KV_HEADS - 1), range(KV_HEADS - 1, KV_HEADS)):
            d_query, *pair = attend_back(
                q, attention, d_attention, lse, doc_start, kvs, groups
            )
            d_queries.append(d_query)
            if pairs:
                pair, pairs = lax.optimization_barrier((pair, pairs))
            d_attention, pair = lax.optimization_barrier((d_attention, pair))
            pairs.append([pair[0]] + [flip(pair[k], "ctx", k) for k in range(1, slots)])
            if fast and i == 0 and groups.start == 0:
                sides = tied(sides, d_query)
                sums, sends = reduce_middle(sums, sides)
                d_attention, sends = lax.optimization_barrier((d_attention, sends))
                across = reduce_across(sends)
            elif fast and i == 0:
                sums, sends = reduce_turn(sums, tied(across, d_query))
                d_queries, sends = lax.optimization_barrier((d_queries, sends))
                line = (sums, *reduce_line(sends))
        riders = None
        if fast and i == 0:
            riders = jnp.concatenate([gain_grads[v][:1] for v in (1, 2, 3)])
        grad, gain_grads[i], attn_grad = project_back(
            d_queries,
            pairs,
            cosine,
            sine,
            (hidden, normed),
            gains,
            i,
            attn_full[i],
            out_grad,
            mid,
            by_shard,
            riders,
            True,
        )
        if fast and i == 0:
            sums, sends = reduce_begin(reduce_start(attn_grad))
            sides = reduce_sides(sends)
            line = tied(line, sends)
            sums, sends = reduce_middle(sums, sides)
            across = reduce_across(sends)
            across, early = lax.optimization_barrier((across, early))
            far = flip(low(grad[half:]), "ctx", slots - 1)
            line, across, far = lax.optimization_barrier((line, across, far))
            rest = spread_fast(low(reduce_end(line)))
            sums, sends = reduce_turn(sums, across)
            last = reduce_end((sums, *reduce_line(sends)))
            last = spread_fast(last)
            early = spread_fast(early)
            all_gains = lax.dynamic_slice_in_dim(last[0, rows:], shard * rows, rows, axis=1)
            order = (3, 0, 1, 2)
            all_gains = jnp.stack([all_gains[v] for v in order])
            attn_rows = jnp.stack([last[0, :rows], rest[3]])
            gate_rows = jnp.stack([rest[0], early[0]])
            up_rows = jnp.stack([rest[1], early[1]])
            down_rows = unfold_down(jnp.stack([rest[2], early[2]]))
        elif fast:
            attn_begun = reduce_start(attn_grad)
            grad, layer_out = lax.optimization_barrier((grad, layer_out))
        else:
            attn_grads[i] = reduce_plain(attn_grad[0], 0)
    if not fast:
        attn_rows = jnp.stack(attn_grads)
        gate_rows = jnp.stack([part[0][0] for part in mlp_grads])
        up_rows = jnp.stack([part[0][1] for part in mlp_grads])
        down_rows = jnp.stack([part[1] for part in mlp_grads])
        all_gains = jnp.concatenate([gain_grads[v][:1] for v in range(gain_count)])
        all_gains = lax.psum(all_gains, ("ctx", "fsdp"))
        all_gains = lax.dynamic_slice_in_dim(all_gains, shard * rows, rows, axis=1)
    if not fast:
        far = flip(low(grad[half:]), "ctx", slots - 1)
    grad = jnp.concatenate([grad[:half], wide(far)])[None]
    return (
        layer_out,
        grad,
        attn_rows[..., :QUERY],
        attn_rows[..., QUERY : QUERY + KVW],
        attn_rows[..., QUERY + KVW : QKV],
        attn_rows[..., QKV:],
        gate_rows,
        up_rows,
        down_rows,
        all_gains[:LAYERS],
        all_gains[LAYERS:],
    )


def solution(mesh):
    return jax.shard_map(
        body,
        mesh=mesh,
        in_specs=(
            P("fsdp", "ctx", None),
            P("fsdp", "ctx"),
            P(None, "fsdp", None),
            P(None, "fsdp", None),
            P(None, "fsdp", None),
            P(None, "fsdp", None),
            P(None, "fsdp", None),
            P(None, "fsdp", None),
            P(None, "fsdp", None),
            P(None, "fsdp"),
            P(None, "fsdp"),
            P("fsdp", "ctx", None),
        ),
        out_specs=(
            P("fsdp", "ctx", None),
            P("fsdp", "ctx", None),
            P(None, "fsdp", None),
            P(None, "fsdp", None),
            P(None, "fsdp", None),
            P(None, "fsdp", None),
            P(None, "fsdp", None),
            P(None, "fsdp", None),
            P(None, "fsdp", None),
            P(None, "fsdp"),
            P(None, "fsdp"),
        ),
        check_vma=False,
    )
```
